256 devices in a mesh: dp: 8 (over x, core), mp: 32 (over y, z).
Axes of the slice: x: 4, y: 4, z: 8, core: 2. Of those that a mesh axis runs over, the one named last changes fastest.
Arguments:
- hidden: bfloat16 [4096, 4096], P('dp'), may hold values from -170 to 170
- encoded: bfloat16 [64, 114688], P('dp'), may hold values from -4 to 4
- neighbours: int32 [64, 2], P('dp'), may hold values from 0 to 63, as said below
- w_query: bfloat16 [4096, 4096], P(None, 'mp'), as said below
- w_key: bfloat16 [896, 4096], P(None, 'mp'), as said below
- w_value: bfloat16 [896, 4096], P(None, 'mp'), may hold values from -0.1875 to 0.1875
- w_out: bfloat16 [4096, 4096], P('mp'), may hold values from -0.1875 to 0.1875
- cotangent: bfloat16 [4096, 4096], P('dp'), may hold values from -16 to 16
Outputs:
- attended: bfloat16 [4096, 4096], P('dp', 'mp')
- grad_hidden: bfloat16 [4096, 4096], P('dp', 'mp')
- grad_encoded: bfloat16 [64, 114688], P('dp', 'mp')
The draws below stay inside these ranges and needn't reach their ends.
Inputs may be any that keep to these rules, and one draw needn't show every extreme that they name: `neighbours`: an id is owner * 8 + slot: the neighbour is row slot of the rows of encoded held by dp index owner. Of the 16 ids of one index of dp, at most 4 name one owner; one owner, the same for every index, is named exactly 4 times by every index of dp. `w_query`: entries scaled by the inverse square root of 4096. `w_key`: entries scaled by the inverse square root of 896, or smaller.
All inputs are finite; a program needn't handle non-finite values.
Results may differ from the reference program's by a relative error of at most 0.0065.
The reference program's roundings to bfloat16 on the way (of `queries`, `prob_half`, `attn_out`, `grad_attn`, `grad_values` and `grad_scores`) count: a program that leaves them out, or rounds other values in their place, can miss the bound.
Values may be sent and summed in bfloat16 or wider, within the bound.
No kernel may reach another device: no remote copies, remote signals or barrier semaphores. Data moves between devices by JAX's collectives and lax.ppermute only.
A program may use at most 128 MiB of HBM per device.

```python
import math
import jax
import jax.numpy as jnp
from jax import lax

D = 4096
HEADS = 32
DH = 128
DE = 896
CL = 64
LN = 128
NEIGH = 2
NB_DEV = 8
CH_DEV = 8
CAP = 4
TOKENS = 4096
SPANS = 64
NB = 64


def encoded_base(key):
    key_a = jax.random.fold_in(jax.random.fold_in(key, 101), 0)
    values = jnp.clip(jax.random.normal(key_a, (NB, LN, DE), jnp.float32), -4.0, 4.0)
    return values


def neighbour_base(key):
    key_a, key_b, key_c, key_d, key_e, key_f = jax.random.split(jax.random.fold_in(key, 202), 6)
    owners = NB // NB_DEV
    requests = NEIGH * CH_DEV
    hot_owner = jax.random.randint(key_a, (), 0, owners)
    position = jnp.arange(requests)
    pattern = jnp.where(position < CAP, 0, 1 + (position - CAP) % (owners - 1))
    sub_keys = jax.random.split(key_b, owners)
    order = jax.vmap(lambda sub_key: jax.random.permutation(sub_key, requests))(sub_keys)
    owner_idx = (hot_owner + pattern[order]) % owners
    favourite = jax.random.randint(key_c, (4,), 0, NB_DEV)
    use_favourite = jax.random.randint(key_d, (owners, requests), 0, 2)
    favoured = favourite[jax.random.randint(key_e, (owners, requests), 0, 4)]
    slots = jnp.where(use_favourite == 0, favoured, jax.random.randint(key_f, (owners, requests), 0, NB_DEV))
    return (owner_idx * NB_DEV + slots).reshape(SPANS, NEIGH).astype(jnp.int32)


def query_base(key):
    key_a = jax.random.fold_in(key, 404)
    values = jnp.clip(jax.random.normal(key_a, (D, D), jnp.float32), -4.0, 4.0)
    return values / math.sqrt(D)


def draw_hidden(key, part):
    key_a = jax.random.fold_in(jax.random.fold_in(key, 303), 0)
    values = jnp.clip(2.0 * jax.random.normal(key_a, (TOKENS, D), jnp.float32), -8.0, 8.0)
    return values.astype(jnp.bfloat16)


def draw_encoded(key, part):
    return encoded_base(key).reshape(NB, LN * DE).astype(jnp.bfloat16)


def draw_neighbours(key, part):
    return neighbour_base(key)


def draw_w_query(key, part):
    return query_base(key).astype(jnp.bfloat16)


def draw_w_key(key, part):
    values = jnp.clip(jax.random.normal(jax.random.fold_in(key, 505), (DE, D), jnp.float32), -4.0, 4.0) / math.sqrt(DE)
    return values.astype(jnp.bfloat16)


def with_spikes(values, stream_key, source, target, blocks, factor):
    def block_of(axis_at):
        return (jnp.arange(values.shape[axis_at]) // (values.shape[axis_at] // blocks)).reshape((-1,) + (1,) * (values.ndim - 1 - axis_at))

    first = jax.random.permutation(stream_key, blocks)[block_of(target)]
    other_side = (block_of(target) + blocks // 2) % blocks
    return jnp.where((block_of(source) == first) | (block_of(source) == other_side), factor * values, values)


def shard_levels(rng, dims, shards, smallest, high):
    def one(dim, shards_of):
        heights = jax.random.uniform(jax.random.fold_in(jax.random.fold_in(rng, 6), dim), (shards_of,), jnp.float32, smallest / len(shards), high / len(shards))
        return jnp.repeat(jnp.exp(heights), dims[dim] // shards_of).reshape((-1,) + (1,) * (len(dims) - dim - 1))

    loudness = one(*shards[0])
    for cut in shards[1:]:
        loudness = loudness * one(*cut)
    return loudness


def bell_draw(key, extent, width, reach, cuts=(), dtype=jnp.bfloat16):
    gain = shard_levels(key, extent, cuts, -0.22, 0.18) if cuts else 1.0
    drawn = jax.random.normal(key, extent, jnp.float32) * width * gain
    return jnp.minimum(jnp.maximum(drawn, -reach), reach).astype(dtype)


def gaussian_with(rng, dims, deviation, reach, pieces, heavy, held_as=jnp.bfloat16):
    values = deviation * jax.random.normal(rng, dims, jnp.float32)
    if pieces:
        values = values * shard_levels(rng, dims, pieces, -0.22, 0.18)
    return jnp.clip(with_spikes(values, jax.random.fold_in(rng, 3), *heavy), -reach, reach).astype(held_as)


def setup_inputs(seed: int = 0) -> dict:
    key_of = jax.random.split(jax.random.key(seed), 9)
    hidden = draw_hidden(jax.random.fold_in(key_of[8], 71), 0)
    encoded = draw_encoded(jax.random.fold_in(key_of[8], 71), 0)
    neighbours = draw_neighbours(jax.random.fold_in(key_of[8], 71), 0)
    w_query = draw_w_query(jax.random.fold_in(key_of[8], 71), 0)
    w_key = draw_w_key(jax.random.fold_in(key_of[8], 71), 0)
    w_value = bell_draw(key_of[5], (DE, D), DE ** -0.5, 0.1875, ((1, 32),))
    w_out = gaussian_with(key_of[6], (D, D), D ** -0.5, 0.1875, ((0, 32),), (0, 1, 32, 2.75))
    cotangent = bell_draw(key_of[7], (TOKENS, D), 4.0, 16.0, ((0, 8),))
    return dict(hidden=hidden, encoded=encoded, neighbours=neighbours, w_query=w_query, w_key=w_key, w_value=w_value, w_out=w_out, cotangent=cotangent)


def to_half(value):
    return lax.optimization_barrier(value.astype(jnp.bfloat16))

def reference(hidden, encoded, neighbours, w_query, w_key, w_value, w_out, cotangent):
    inv_root = 1.0 / math.sqrt(DH)
    enc_rows = encoded.reshape(NB * LN, DE)
    flat_ids = neighbours.reshape(SPANS * NEIGH).astype(jnp.int32)
    query_heads = w_query.reshape(D, HEADS, DH).transpose(1, 0, 2)
    key_heads = w_key.reshape(DE, HEADS, DH).transpose(1, 0, 2)
    value_heads = w_value.reshape(DE, HEADS, DH).transpose(1, 0, 2)
    out_heads = w_out.reshape(HEADS, DH, D)

    def head_step(carry, parts):
        att_acc, hid_acc, enc_acc = carry
        query_w, key_w, value_w, out_w = parts
        queries = to_half(jnp.dot(hidden, query_w, preferred_element_type=jnp.float32))
        keys_all = to_half(jnp.dot(enc_rows, key_w, preferred_element_type=jnp.float32)).reshape(NB, LN, DH)
        values_all = to_half(jnp.dot(enc_rows, value_w, preferred_element_type=jnp.float32)).reshape(NB, LN, DH)
        ctx_keys = jnp.take(keys_all, flat_ids, axis=0).reshape(SPANS, NEIGH * LN, DH).astype(jnp.float32)
        ctx_values = jnp.take(values_all, flat_ids, axis=0).reshape(SPANS, NEIGH * LN, DH).astype(jnp.float32)
        q_blocks = queries.reshape(SPANS, CL, DH).astype(jnp.float32)
        scores = jnp.einsum('cqd,ckd->cqk', q_blocks, ctx_keys) * inv_root
        row_max = lax.optimization_barrier(jnp.max(scores, axis=-1, keepdims=True))
        exp_terms = jnp.exp(scores - row_max)
        prob_full = exp_terms / lax.optimization_barrier(jnp.sum(exp_terms, axis=-1, keepdims=True))
        prob_half = to_half(prob_full).astype(jnp.float32)
        attn_out = to_half(jnp.einsum('cqk,ckd->cqd', prob_half, ctx_values)).reshape(TOKENS, DH)
        att_acc = att_acc + jnp.dot(attn_out, out_w, preferred_element_type=jnp.float32)
        grad_attn = to_half(jnp.dot(cotangent, out_w.T, preferred_element_type=jnp.float32))
        grad_blocks = grad_attn.reshape(SPANS, CL, DH).astype(jnp.float32)
        grad_prob = jnp.einsum('cqd,ckd->cqk', grad_blocks, ctx_values)
        grad_values = to_half(jnp.einsum('cqk,cqd->ckd', prob_half, grad_blocks)).astype(jnp.float32)
        grad_scores = to_half(prob_full * (grad_prob - lax.optimization_barrier(jnp.sum(prob_full * grad_prob, axis=-1, keepdims=True)))).astype(jnp.float32)
        grad_query = to_half(jnp.einsum('cqk,ckd->cqd', grad_scores, ctx_keys) * inv_root).reshape(TOKENS, DH)
        grad_keys = to_half(jnp.einsum('cqk,cqd->ckd', grad_scores, q_blocks) * inv_root).astype(jnp.float32)
        hid_acc = hid_acc + jnp.dot(grad_query, query_w.T, preferred_element_type=jnp.float32)
        key_sum = jnp.zeros((NB, LN, DH), jnp.float32).at[flat_ids].add(grad_keys.reshape(SPANS * NEIGH, LN, DH))
        value_sum = jnp.zeros((NB, LN, DH), jnp.float32).at[flat_ids].add(grad_values.reshape(SPANS * NEIGH, LN, DH))
        key_half = key_sum.astype(jnp.bfloat16).reshape(NB * LN, DH)
        value_half = value_sum.astype(jnp.bfloat16).reshape(NB * LN, DH)
        enc_acc = enc_acc + jnp.dot(key_half, key_w.T, preferred_element_type=jnp.float32)
        enc_acc = enc_acc + jnp.dot(value_half, value_w.T, preferred_element_type=jnp.float32)
        return ((att_acc, hid_acc, enc_acc), None)
    start = (jnp.zeros((TOKENS, D), jnp.float32), jnp.zeros((TOKENS, D), jnp.float32), jnp.zeros((NB * LN, DE), jnp.float32))
    (att_acc, hid_acc, enc_acc), unused = lax.scan(head_step, start, (query_heads, key_heads, value_heads, out_heads))
    attended = att_acc.astype(jnp.bfloat16)
    grad_hidden = hid_acc.astype(jnp.bfloat16)
    grad_encoded = enc_acc.reshape(NB, LN * DE).astype(jnp.bfloat16)
    return (attended, grad_hidden, grad_encoded)
```

```python
import functools
import math

import jax
import jax.numpy as jnp
from jax import lax
from jax.experimental import pallas as pl
from jax.experimental.pallas import tpu as pltpu
from jax.sharding import Mesh, PartitionSpec as P

DH = 128
BF = jnp.bfloat16
F32 = jnp.float32
NT = (((1,), (1,)), ((), ()))
TN = (((0,), (0,)), ((), ()))
VMEM_LIMIT = 48 * 1024 * 1024


def params():
    return pltpu.CompilerParams(vmem_limit_bytes=VMEM_LIMIT)


def call(body, out_shape, n_scalar, n_in, flops, moved, scratch=()):
    single = not isinstance(out_shape, (tuple, list))
    n_out = 1 if single else len(out_shape)
    vmem = pl.BlockSpec(memory_space=pltpu.VMEM)
    smem = pl.BlockSpec(memory_space=pltpu.SMEM)
    return pl.pallas_call(
        body,
        out_shape=out_shape,
        in_specs=[smem] * n_scalar + [vmem] * n_in,
        out_specs=vmem if single else (vmem,) * n_out,
        scratch_shapes=list(scratch),
        compiler_params=params(),
        cost_estimate=pl.CostEstimate(flops=flops, bytes_accessed=moved, transcendentals=0),
    )


def attention_body(geom, pos_ref, ids_ref, q_ref, g_ref, *refs):
    blocks, block_len, n_x, n_y, cap, stored = geom
    kv_refs, (attn_ref, gq_ref, out_ref, kv_ref) = refs[:-4], refs[-4:]
    near, far = kv_refs[:6], kv_refs[6:]
    inv_root = 1.0 / math.sqrt(DH)
    seg = kv_ref.shape[1]
    piece = seg // n_y
    half = stored // 2
    my_x, my_c = pos_ref[0], pos_ref[1]
    requests = 2 * blocks
    out_ref[...] = jnp.zeros_like(out_ref)
    ids = [ids_ref[r // 2, r % 2] for r in range(requests)]
    owners = [i // stored for i in ids]
    for r in range(requests):
        slot = ids[r] % stored
        dx = lax.rem(owners[r] // 2 - my_x + n_x, n_x)
        dc = lax.rem(owners[r] % 2 + my_c, 2)
        which = dc * n_x + dx
        for c in range(2):
            for j, d in enumerate((0, 1, 3)):

                @pl.when(which == c * n_x + d)
                def _(r=r, ref=near[c * 3 + j], slot=slot):
                    kv_ref[r] = ref[slot]

            for h in range(2):

                @pl.when((which == c * n_x + 2) & (slot // half == h))
                def _(r=r, ref=far[c * 2 + h], slot=slot):
                    kv_ref[r] = ref[lax.rem(slot, half)]

    for c in range(blocks):
        k = kv_ref[2 * c : 2 * c + 2, :, :DH].reshape(2 * seg, DH)
        v = kv_ref[2 * c : 2 * c + 2, :, DH:].reshape(2 * seg, DH)
        rows = slice(c * block_len, (c + 1) * block_len)
        q = q_ref[rows, :]
        g = g_ref[rows, :]
        s = lax.dot_general(q, k, NT, preferred_element_type=F32) * inv_root
        e = jnp.exp(s - jnp.max(s, axis=-1, keepdims=True))
        p = e / jnp.sum(e, axis=-1, keepdims=True)
        ph = p.astype(BF)
        gp = lax.dot_general(g, v, NT, preferred_element_type=F32)
        attn_ref[rows, :] = jnp.dot(ph, v, preferred_element_type=F32).astype(BF)
        gs = (p * (gp - jnp.sum(p * gp, axis=-1, keepdims=True))).astype(BF)
        gq_ref[rows, :] = (jnp.dot(gs, k, preferred_element_type=F32) * inv_root).astype(BF)
        gv = lax.dot_general(ph, g, TN, preferred_element_type=F32).astype(BF)
        gk = (lax.dot_general(gs, q, TN, preferred_element_type=F32) * inv_root).astype(BF)
        for j in range(2):
            r = 2 * c + j
            pos = sum([(owners[i] == owners[r]).astype(jnp.int32) for i in range(r)], jnp.int32(0))
            for y in range(n_y):
                part = slice(j * seg + y * piece, j * seg + (y + 1) * piece)
                out_ref[owners[r], y, pos, :, :DH] = gk[part, :]
                out_ref[owners[r], y, pos, :, DH:] = gv[part, :]


def encoded_body(stored, pos_ref, ids_ref, ret_ref, w_ref, out_ref, acc_ref, prod_ref):
    owners, n_y, cap, piece, _ = ret_ref.shape
    me = pos_ref[0] * 2 + pos_ref[1]
    blocks = ids_ref.shape[0] // owners
    acc_ref[...] = jnp.zeros_like(acc_ref)

    def from_device(d, carry):
        count = jnp.int32(0)
        for r in range(2 * blocks):
            at = ids_ref[d * blocks + r // 2, r % 2]
            named = at // stored == me

            @pl.when(named)
            def _(at=at, count=count):
                slot = lax.rem(at, stored)
                for y in range(n_y):
                    acc_ref[y, slot] += ret_ref[d, y, count].astype(F32)

            count = count + named.astype(jnp.int32)
        return carry

    lax.fori_loop(0, owners, from_device, 0)
    lanes = prod_ref.shape[0]
    for y in range(n_y):
        both = acc_ref[y].astype(BF).reshape(stored * piece, 2 * DH)
        for n in range(lanes):
            w = w_ref[y, n * DH : (n + 1) * DH, :]
            term = lax.dot_general(both, w, NT, preferred_element_type=F32)
            prod_ref[n] = term if y == 0 else prod_ref[n] + term
    for t in range(0, piece, 2):
        for n in range(lanes):
            two = [prod_ref[n, pl.ds(t + k, stored, stride=piece), :] for k in range(2)]
            out_ref[pl.ds(t * stored, 2 * stored), n * DH : (n + 1) * DH] = jnp.concatenate(two, axis=0).astype(BF)


def head_sum_body(n_z, n_y, second, pos_ref, *refs):
    pieces, (mine_ref, other_ref), outs = refs[:n_z], refs[n_z : n_z + 2], refs[n_z + 2 :]
    my_c, my_y, my_z = pos_ref[1], pos_ref[2], pos_ref[3]

    def with_weights(w_ref):
        for k in range(0, n_y, 2):
            total = None
            for j in range(n_z):
                src = lax.rem(my_z + j, n_z)
                w = [w_ref[src, lax.rem(my_y + k + i, n_y)] for i in range(2)]
                if second:
                    w = jnp.concatenate(w, axis=0)
                    term = lax.dot_general(pieces[j][...], w, NT, preferred_element_type=F32)
                else:
                    w = jnp.concatenate(w, axis=1)
                    term = jnp.dot(pieces[j][...], w, preferred_element_type=F32)
                total = term if total is None else total + term
            for i in range(2):
                outs[k + i][...] = total[:, i * DH : (i + 1) * DH].astype(outs[k + i].dtype)

    @pl.when(my_c == second)
    def _():
        with_weights(mine_ref)

    @pl.when(my_c != second)
    def _():
        with_weights(other_ref)


def shards(hidden, encoded, neighbours, w_query, w_key, w_value, w_out, cotangent):
    n_x, n_c, n_y, n_z = (lax.axis_size(a) for a in ("x", "c", "y", "z"))
    dp = ("x", "c")
    owners = n_x * n_c
    rows, width = hidden.shape
    blocks, per_block = neighbours.shape
    cap = blocks * per_block // 4
    stored = encoded.shape[0]
    enc_width = w_key.shape[0]
    seg = encoded.shape[1] // enc_width
    block_len = rows // blocks
    piece = seg // n_y
    core = lax.axis_index("c")
    place = jnp.stack([lax.axis_index(a) for a in ("x", "c", "y", "z")]).astype(jnp.int32)

    def shift(axis, n, k):
        return lambda a: lax.ppermute(a, axis, [(i, (i + k) % n) for i in range(n)])

    swap = shift("c", n_c, 1)
    x_up, x_down = shift("x", n_x, -1), shift("x", n_x, 1)
    z_up, z_down = shift("z", n_z, -1), shift("z", n_z, 1)

    w_pair = jnp.concatenate([w_key, w_value], axis=1)
    enc_rows = encoded.reshape(stored, seg, enc_width).transpose(1, 0, 2).reshape(seg * stored, enc_width)
    kv = jnp.dot(enc_rows, w_pair, preferred_element_type=F32).astype(BF)
    kv = kv.reshape(seg, stored, 2 * DH).transpose(1, 0, 2)
    after, before = x_up(kv), x_down(kv)
    half = stored // 2
    far = [x_up(after[:half]), x_down(before[half:])]
    near = [kv, after, before]
    kv_all = near + [swap(a) for a in near] + far + [swap(a) for a in far]

    w_query_, w_out_, w_pair_, hidden_, cotangent_, neighbours_, kv_ = lax.optimization_barrier(
        (w_query, w_out, w_pair, hidden, cotangent, neighbours, kv)
    )
    wo_blocks = w_out_.reshape(DH, n_y, n_z, DH).transpose(2, 1, 0, 3)
    wq_blocks = w_query_.reshape(n_y, n_z, DH, DH).transpose(1, 0, 2, 3)
    mine = jnp.where(core == 0, wo_blocks, wq_blocks)
    mine = lax.all_to_all(mine, "z", 0, 0, tiled=True)
    other = swap(mine)
    pair_all = lax.all_gather(w_pair, "y")
    ids_all = lax.all_gather(neighbours_, dp, tiled=True)

    queries = jnp.dot(hidden_, w_query_, preferred_element_type=F32).astype(BF)
    grad_attn = lax.dot_general(cotangent_, w_out_, NT, preferred_element_type=F32).astype(BF)

    slab = jax.ShapeDtypeStruct((rows, DH), BF)
    attn, gq, outgoing = call(
        functools.partial(attention_body, (blocks, block_len, n_x, n_y, cap, stored)),
        (slab, slab, jax.ShapeDtypeStruct((owners, n_y, cap, piece, 2 * DH), BF)),
        2, 2 + len(kv_all), 500_000_000, 5 << 20,
        scratch=(pltpu.VMEM((blocks * per_block, seg, 2 * DH), BF),),
    )(place, neighbours, queries, grad_attn, *kv_all)

    returned = lax.all_to_all(
        outgoing.reshape(owners * n_y, cap, piece, 2 * DH), dp + ("y",), 0, 0, tiled=True
    ).reshape(owners, n_y, cap, piece, 2 * DH)
    enc_part = call(
        functools.partial(encoded_body, stored),
        jax.ShapeDtypeStruct((piece * stored, enc_width), BF), 2, 2, 500_000_000, 5 << 20,
        scratch=(
            pltpu.VMEM((n_y, stored, piece, 2 * DH), F32),
            pltpu.VMEM((enc_width // DH, stored * piece, DH), F32),
        ),
    )(place, ids_all, returned, pair_all)
    enc_parts = lax.all_to_all(enc_part.reshape(n_z, -1, enc_width), "z", 0, 0, tiled=True)
    enc_rows_sum = jnp.sum(enc_parts.astype(F32), axis=0).astype(BF)
    grad_encoded = enc_rows_sum.reshape(seg // (n_y * n_z), stored, enc_width).transpose(1, 0, 2).reshape(stored, -1)

    def ring(own):
        pieces = {0: own}
        for k in range(1, n_z // 2 + 1):
            pieces[k] = z_up(pieces[k - 1])
        last = own
        for k in range(1, n_z - n_z // 2):
            last = z_down(last)
            pieces[n_z - k] = last
        return [pieces[k] for k in range(n_z)]

    def summed(own, second):
        parts = call(
            functools.partial(head_sum_body, n_z, n_y, second),
            (jax.ShapeDtypeStruct((rows, DH), F32),) + (slab,) * (n_y - 1),
            1, n_z + 2, 540_000_000, 3 << 20,
        )(place, *ring(own), mine, other)
        total = parts[0]
        for k in range(1, n_y):
            total = total + shift("y", n_y, k)(parts[k]).astype(F32)
        return total.astype(BF)

    return summed(attn, 0), summed(gq, 1), grad_encoded


def solution(mesh):
    n_y = 4
    dp, mp = mesh.shape["dp"], mesh.shape["mp"]
    split = Mesh(mesh.devices.reshape(dp // 2, 2, n_y, mp // n_y), ("x", "c", "y", "z"))
    d, m = ("x", "c"), ("y", "z")
    return jax.shard_map(
        shards,
        mesh=split,
        in_specs=(P(d, None), P(d, None), P(d, None), P(None, m), P(None, m), P(None, m), P(m, None), P(d, None)),
        out_specs=(P(d, m), P(d, m), P(d, m)),
        check_vma=False,
    )
```

```python
import functools
import math

import jax
import jax.numpy as jnp
from jax import lax
from jax.experimental import pallas as pl
from jax.experimental.pallas import tpu as pltpu
from jax.sharding import Mesh, PartitionSpec as P

DH = 128
BF = jnp.bfloat16
F32 = jnp.float32
NT = (((1,), (1,)), ((), ()))
TN = (((0,), (0,)), ((), ()))
VMEM_LIMIT = 60 * 1024 * 1024


def params():
    return pltpu.CompilerParams(vmem_limit_bytes=VMEM_LIMIT)


def call(body, out_shape, in_spaces, flops, moved, scratch=()):
    spaces = {"s": pltpu.SMEM, "v": pltpu.VMEM, "a": pl.ANY}
    single = not isinstance(out_shape, (tuple, list))
    vmem = pl.BlockSpec(memory_space=pltpu.VMEM)
    return pl.pallas_call(
        body,
        out_shape=out_shape,
        in_specs=[pl.BlockSpec(memory_space=spaces[k]) for k in in_spaces],
        out_specs=vmem if single else (vmem,) * len(out_shape),
        scratch_shapes=list(scratch),
        compiler_params=params(),
        cost_estimate=pl.CostEstimate(flops=flops, bytes_accessed=moved, transcendentals=0),
    )


def keys_values_body(stored, ids_ref, x_ref, wk_ref, wv_ref, lo_ref, hi_ref, pair_ref, kv_ref):
    pair = jnp.concatenate([wk_ref[...], wv_ref[...]], axis=1)
    pair_ref[...] = pair
    seg = x_ref.shape[0] // stored
    half = stored // 2
    for n in range(kv_ref.shape[0]):
        kv_ref[n] = jnp.dot(x_ref[...], pair[:, n * DH : (n + 1) * DH], preferred_element_type=F32)
        for s in range(stored):
            rows = slice((s % half) * seg, (s % half + 1) * seg)
            ref = lo_ref if s < half else hi_ref
            ref[rows, n * DH : (n + 1) * DH] = kv_ref[n, pl.ds(s, seg, stride=stored), :].astype(BF)
    extra = lo_ref.shape[0] - half * seg
    lane = lax.broadcasted_iota(jnp.int32, (extra, 2 * DH), 1)
    row = jnp.zeros((extra, 2 * DH), F32)
    for r in range(2 * ids_ref.shape[0]):
        row = jnp.where(lane == r, ids_ref[r // 2, r % 2].astype(F32), row)
    lo_ref[half * seg :, :] = row.astype(BF)


def weights_body(n_z, n_y, pos_ref, wo_ref, wq_ref, *out_refs):
    my_y, my_z = pos_ref[2], pos_ref[3]

    def fill(block):
        for k in range(n_z):
            for y in range(n_y):
                to = lax.rem(my_z - k + n_z, n_z)
                at = (lax.rem(my_y + y, n_y) * n_z + to) * DH
                out_refs[k][y] = block(pl.multiple_of(at, DH))

    @pl.when(pos_ref[1] == 0)
    def _():
        fill(lambda at: wo_ref[:, pl.ds(at, DH)])

    @pl.when(pos_ref[1] != 0)
    def _():
        fill(lambda at: wq_ref[pl.ds(at, DH), :])


def merge_body(*refs):
    for k, ref in enumerate(refs[:-1]):
        refs[-1][k] = ref[...]


def attention_body(geom, pos_ref, ids_ref, q_ref, g_ref, *refs):
    blocks, block_len, n_x, n_y, cap, stored, seg = geom
    kv_refs, (attn_ref, gq_ref, out_ref, all_ids_ref, kv_ref, sem) = refs[:-6], refs[-6:]
    inv_root = 1.0 / math.sqrt(DH)
    half = stored // 2
    piece = seg // n_y
    my_x, my_c = pos_ref[0], pos_ref[1]
    copies = []
    for i, ref in enumerate(kv_refs):
        copies.append(pltpu.make_async_copy(ref, kv_ref.at[i, : ref.shape[0]], sem.at[i]))
        copies[-1].start()
    out_ref[...] = jnp.zeros_like(out_ref)
    for copy in copies:
        copy.wait()
    for c in range(2):
        for d in range(n_x):
            owner = lax.rem(my_x + d, n_x) * 2 + lax.rem(my_c + c, 2)
            row = kv_ref[(c * n_x + d) * 2, half * seg :, :DH].astype(F32).astype(jnp.int32)
            all_ids_ref[pl.ds(owner, 1), :] = row[:1, :]

    def place(r):
        i = ids_ref[r // 2, r % 2]
        owner, slot = i // stored, lax.rem(i, stored)
        dx = lax.rem(owner // 2 - my_x + n_x, n_x)
        dc = lax.rem(lax.rem(owner, 2) + my_c, 2)
        at = (dc * n_x + dx) * 2 + slot // half
        return owner, at, pl.multiple_of(lax.rem(slot, half) * seg, seg)

    spots = [place(r) for r in range(2 * blocks)]
    for c in range(blocks):
        both = [kv_ref[spots[r][1], pl.ds(spots[r][2], seg), :] for r in (2 * c, 2 * c + 1)]
        k = jnp.concatenate([b[:, :DH] for b in both], axis=0)
        v = jnp.concatenate([b[:, DH:] for b in both], axis=0)
        rows = slice(c * block_len, (c + 1) * block_len)
        q = q_ref[rows, :]
        g = g_ref[rows, :]
        s = lax.dot_general(q, k, NT, preferred_element_type=F32) * inv_root
        e = jnp.exp(s - jnp.max(s, axis=-1, keepdims=True))
        p = e / jnp.sum(e, axis=-1, keepdims=True)
        ph = p.astype(BF)
        gp = lax.dot_general(g, v, NT, preferred_element_type=F32)
        attn_ref[rows, :] = jnp.dot(ph, v, preferred_element_type=F32).astype(BF)
        gs = (p * (gp - jnp.sum(p * gp, axis=-1, keepdims=True))).astype(BF)
        gq_ref[rows, :] = (jnp.dot(gs, k, preferred_element_type=F32) * inv_root).astype(BF)
        gv = lax.dot_general(ph, g, TN, preferred_element_type=F32).astype(BF)
        gk = (lax.dot_general(gs, q, TN, preferred_element_type=F32) * inv_root).astype(BF)
        for j in range(2):
            r = 2 * c + j
            owner = spots[r][0]
            pos = sum([(spots[i][0] == owner).astype(jnp.int32) for i in range(r)], jnp.int32(0))
            for y in range(n_y):
                part = slice(j * seg + y * piece, j * seg + (y + 1) * piece)
                out_ref[owner, y, pos, :, :DH] = gk[part, :]
                out_ref[owner, y, pos, :, DH:] = gv[part, :]


def encoded_body(stored, blocks, pos_ref, ids_ref, ret_ref, *refs):
    owners, n_y, cap, piece, _ = ret_ref.shape
    w_refs, (out_ref, acc_ref, prod_ref) = refs[:n_y], refs[n_y:]
    me = pos_ref[0] * 2 + pos_ref[1]
    my_y = pos_ref[2]
    acc_ref[...] = jnp.zeros_like(acc_ref)

    def from_device(d, carry):
        count = jnp.int32(0)
        for r in range(2 * blocks):
            at = ids_ref[d, r]
            named = at // stored == me

            @pl.when(named)
            def _(at=at, count=count):
                slot = lax.rem(at, stored)
                for y in range(n_y):
                    acc_ref[y, slot] += ret_ref[d, y, count].astype(F32)

            count = count + named.astype(jnp.int32)
        return carry

    lax.fori_loop(0, owners, from_device, 0)
    lanes = prod_ref.shape[0]
    for y in range(n_y):
        both = acc_ref[lax.rem(my_y + y, n_y)].astype(BF).reshape(stored * piece, 2 * DH)
        for n in range(lanes):
            w = w_refs[y][n * DH : (n + 1) * DH, :]
            term = lax.dot_general(both, w, NT, preferred_element_type=F32)
            prod_ref[n] = term if y == 0 else prod_ref[n] + term
    for t in range(0, piece, 2):
        for n in range(lanes):
            two = [prod_ref[n, pl.ds(t + k, stored, stride=piece), :] for k in range(2)]
            out_ref[pl.ds(t * stored, 2 * stored), n * DH : (n + 1) * DH] = jnp.concatenate(two, axis=0).astype(BF)


def head_sum_body(n_z, n_y, second, pos_ref, *refs):
    pieces, (mine_ref, other_ref), outs = refs[:n_z], refs[n_z : n_z + 2], refs[n_z + 2 :]
    my_c = pos_ref[1]

    def with_weights(w_ref):
        for k in range(0, n_y, 2):
            total = None
            for j in range(n_z):
                w = [w_ref[j, k + i] for i in range(2)]
                if second:
                    w = jnp.concatenate(w, axis=0)
                    term = lax.dot_general(pieces[j][...], w, NT, preferred_element_type=F32)
                else:
                    w = jnp.concatenate(w, axis=1)
                    term = jnp.dot(pieces[j][...], w, preferred_element_type=F32)
                total = term if total is None else total + term
            for i in range(2):
                outs[k + i][...] = total[:, i * DH : (i + 1) * DH].astype(outs[k + i].dtype)

    @pl.when(my_c == second)
    def _():
        with_weights(mine_ref)

    @pl.when(my_c != second)
    def _():
        with_weights(other_ref)


def shards(hidden, encoded, neighbours, w_query, w_key, w_value, w_out, cotangent):
    n_x, n_c, n_y, n_z = (lax.axis_size(a) for a in ("x", "c", "y", "z"))
    dp = ("x", "c")
    owners = n_x * n_c
    rows, width = hidden.shape
    blocks, per_block = neighbours.shape
    cap = blocks * per_block // 4
    stored = encoded.shape[0]
    enc_width = w_key.shape[0]
    seg = encoded.shape[1] // enc_width
    block_len = rows // blocks
    piece = seg // n_y
    core = lax.axis_index("c")
    place = jnp.stack([lax.axis_index(a) for a in ("x", "c", "y", "z")]).astype(jnp.int32)

    def shift(axis, n, k):
        return lambda a: lax.ppermute(a, axis, [(i, (i + k) % n) for i in range(n)])

    swap = shift("c", n_c, 1)
    x_up, x_down = shift("x", n_x, -1), shift("x", n_x, 1)
    z_up, z_down = shift("z", n_z, -1), shift("z", n_z, 1)
    tie = lax.optimization_barrier

    enc_rows = encoded.reshape(stored, seg, enc_width).transpose(1, 0, 2).reshape(seg * stored, enc_width)
    half = stored // 2 * seg
    lo, hi, pair = call(
        functools.partial(keys_values_body, stored),
        (
            jax.ShapeDtypeStruct((half + 16, 2 * DH), BF),
            jax.ShapeDtypeStruct((half, 2 * DH), BF),
            jax.ShapeDtypeStruct((enc_width, 2 * DH), BF),
        ),
        "svvv", 470_000_000, 3 << 20,
        scratch=(pltpu.VMEM((2, seg * stored, DH), F32),),
    )(neighbours, enc_rows, w_key, w_value)
    after_lo, before_hi = x_up(lo), x_down(hi)
    after_hi, before_lo = x_up(hi), x_down(lo)
    w_query_, w_out_, pair_, hidden_, cotangent_, _ = tie((w_query, w_out, pair, hidden, cotangent, lo))
    mine = call(
        functools.partial(weights_body, n_z, n_y),
        (jax.ShapeDtypeStruct((n_y, DH, DH), BF),) * n_z, "svv", 0, 3 << 20,
    )(place, w_out_, w_query_)
    other_hi = swap(hi)
    mine, pair_, other_hi = tie((mine, pair_, other_hi))
    mine = [mine[0]] + [shift("z", n_z, -k)(mine[k]) for k in range(1, n_z)]
    pairs = [pair] + [shift("y", n_y, -k)(pair_) for k in range(1, n_y)]

    far_lo, far_hi = x_up(after_lo), x_down(before_hi)
    here = [lo, hi, after_lo, after_hi, far_lo, far_hi, before_lo, before_hi]
    kv_all = here + [swap(lo), other_hi] + [swap(a) for a in here[2:]]

    queries = jnp.dot(hidden_, w_query_, preferred_element_type=F32).astype(BF)
    grad_attn = lax.dot_general(cotangent_, w_out_, NT, preferred_element_type=F32).astype(BF)

    queries, grad_attn, pairs, mine = tie((queries, grad_attn, pairs, mine))
    mine = call(merge_body, jax.ShapeDtypeStruct((n_z, n_y, DH, DH), BF), "v" * n_z, 0, 2 << 20)(*mine)
    other = swap(mine)

    slab = jax.ShapeDtypeStruct((rows, DH), BF)
    attn, gq, outgoing, ids_all = call(
        functools.partial(attention_body, (blocks, block_len, n_x, n_y, cap, stored, seg)),
        (
            slab,
            slab,
            jax.ShapeDtypeStruct((owners, n_y, cap, piece, 2 * DH), BF),
            jax.ShapeDtypeStruct((owners, DH), jnp.int32),
        ),
        "ssvv" + "a" * len(kv_all), 500_000_000, 7 << 20,
        scratch=(
            pltpu.VMEM((len(kv_all), half + 16, 2 * DH), BF),
            pltpu.SemaphoreType.DMA((len(kv_all),)),
        ),
    )(place, neighbours, queries, grad_attn, *kv_all)

    def ring(own):
        pieces = {0: own}
        for k in range(1, n_z // 2 + 1):
            pieces[k] = z_up(pieces[k - 1])
        last = own
        for k in range(1, n_z - n_z // 2):
            last = z_down(last)
            pieces[n_z - k] = last
        return [pieces[k] for k in range(n_z)]

    returned = lax.all_to_all(
        outgoing.reshape(owners * n_y, cap, piece, 2 * DH), dp + ("y",), 0, 0, tiled=True
    ).reshape(owners, n_y, cap, piece, 2 * DH)
    attn_all, gq_all = ring(attn), ring(gq)
    attn_all, gq_all, returned = tie((attn_all, gq_all, returned))
    enc_part = call(
        functools.partial(encoded_body, stored, blocks),
        jax.ShapeDtypeStruct((piece * stored, enc_width), BF), "ssv" + "v" * n_y, 500_000_000, 5 << 20,
        scratch=(
            pltpu.VMEM((n_y, stored, piece, 2 * DH), F32),
            pltpu.VMEM((enc_width // DH, stored * piece, DH), F32),
        ),
    )(place, ids_all, returned, *pairs)
    attn_all, gq_all, enc_part = tie((attn_all, gq_all, enc_part))
    enc_parts = lax.all_to_all(enc_part.reshape(n_z, -1, enc_width), "z", 0, 0, tiled=True)
    enc_rows_sum = jnp.sum(enc_parts.astype(F32), axis=0).astype(BF)
    grad_encoded = enc_rows_sum.reshape(seg // (n_y * n_z), stored, enc_width).transpose(1, 0, 2).reshape(stored, -1)

    def summed(pieces, second):
        parts = call(
            functools.partial(head_sum_body, n_z, n_y, second),
            (jax.ShapeDtypeStruct((rows, DH), F32),) + (slab,) * (n_y - 1),
            "s" + "v" * (n_z + 2), 540_000_000, 3 << 20,
        )(place, *pieces, mine, other)
        total = parts[0]
        for k in range(1, n_y):
            total = total + shift("y", n_y, k)(parts[k]).astype(F32)
        return total.astype(BF)

    return summed(attn_all, 0), summed(gq_all, 1), grad_encoded


def solution(mesh):
    n_y = 4
    dp, mp = mesh.shape["dp"], mesh.shape["mp"]
    split = Mesh(mesh.devices.reshape(dp // 2, 2, n_y, mp // n_y), ("x", "c", "y", "z"))
    d, m = ("x", "c"), ("y", "z")
    return jax.shard_map(
        shards,
        mesh=split,
        in_specs=(P(d, None), P(d, None), P(d, None), P(None, m), P(None, m), P(None, m), P(m, None), P(d, None)),
        out_specs=(P(d, m), P(d, m), P(d, m)),
        check_vma=False,
    )
```

```python
import functools
import math

import jax
import jax.numpy as jnp
from jax import lax
from jax.experimental import pallas as pl
from jax.experimental.pallas import tpu as pltpu
from jax.sharding import Mesh, PartitionSpec as P

DH = 128
BF = jnp.bfloat16
F32 = jnp.float32
NT = (((1,), (1,)), ((), ()))
TN = (((0,), (0,)), ((), ()))
HEAD = 16
VMEM_LIMIT = 60 * 1024 * 1024


def params():
    return pltpu.CompilerParams(vmem_limit_bytes=VMEM_LIMIT)


def call(body, out_shape, in_spaces, flops, moved, scratch=(), out_space="v"):
    spaces = {"s": pltpu.SMEM, "v": pltpu.VMEM, "a": pl.ANY}
    single = not isinstance(out_shape, (tuple, list))
    out = pl.BlockSpec(memory_space=spaces[out_space])
    return pl.pallas_call(
        body,
        out_shape=out_shape,
        in_specs=[pl.BlockSpec(memory_space=spaces[k]) for k in in_spaces],
        out_specs=out if single else (out,) * len(out_shape),
        scratch_shapes=list(scratch),
        compiler_params=params(),
        cost_estimate=pl.CostEstimate(flops=flops, bytes_accessed=moved, transcendentals=0),
    )


def keys_values_body(stored, ids_ref, x_ref, wk_ref, wv_ref, out_ref, pair_ref, kv_ref):
    pair = jnp.concatenate([wk_ref[...], wv_ref[...]], axis=1)
    pair_ref[...] = pair
    seg = x_ref.shape[0] // stored
    both = jnp.dot(x_ref[...], pair, preferred_element_type=F32)
    for n in range(kv_ref.shape[0]):
        kv_ref[n] = both[:, n * DH : (n + 1) * DH]
        for s in range(stored):
            rows = slice(HEAD + s * seg, HEAD + (s + 1) * seg)
            out_ref[rows, n * DH : (n + 1) * DH] = kv_ref[n, pl.ds(s, seg, stride=stored), :].astype(BF)
    lane = lax.broadcasted_iota(jnp.int32, (HEAD, 2 * DH), 1)
    row = jnp.zeros((HEAD, 2 * DH), F32)
    for r in range(2 * ids_ref.shape[0]):
        row = jnp.where(lane == r, ids_ref[r // 2, r % 2].astype(F32), row)
    out_ref[:HEAD, :] = row.astype(BF)


def halves_body(cut, after_ref, before_ref, lo_ref, hi_ref, sem):
    copies = [
        pltpu.make_async_copy(after_ref.at[:cut], lo_ref, sem.at[0]),
        pltpu.make_async_copy(before_ref.at[cut:], hi_ref, sem.at[1]),
    ]
    for copy in copies:
        copy.start()
    for copy in copies:
        copy.wait()


def weights_body(n_z, pos_ref, wo_ref, wq_ref, out_ref, sem):
    first = 2 * lax.rem(pos_ref[0], 2) * n_z

    def move(block):
        copies = [
            pltpu.make_async_copy(block(i * n_z + z), out_ref.at[z, i], sem.at[i * n_z + z])
            for i in range(2)
            for z in range(n_z)
        ]
        for copy in copies:
            copy.start()
        for copy in copies:
            copy.wait()

    @pl.when(pos_ref[1] == 0)
    def _():
        move(lambda k: wo_ref.at[:, pl.ds(pl.multiple_of((first + k) * DH, DH), DH)])

    @pl.when(pos_ref[1] != 0)
    def _():
        move(lambda k: wq_ref.at[pl.ds(pl.multiple_of((first + k) * DH, DH), DH), :])


def attention_body(geom, pos_ref, ids_ref, q_ref, g_ref, *refs):
    blocks, block_len, n_x, n_y, cap, stored, seg = geom
    kv_refs, (attn_ref, gq_ref, out_ref, all_ids_ref, kv_ref, sem) = refs[:-6], refs[-6:]
    inv_root = 1.0 / math.sqrt(DH)
    piece = seg // n_y
    my_x, my_c = pos_ref[0], pos_ref[1]
    copies = []
    for i, ref in enumerate(kv_refs):
        c, k = i // 5, i % 5
        cut = HEAD + stored // 2 * seg
        if k < 2:
            to = kv_ref.at[c * n_x + k]
        elif k == 4:
            to = kv_ref.at[c * n_x + 3]
        else:
            to = kv_ref.at[c * n_x + 2, :cut] if k == 2 else kv_ref.at[c * n_x + 2, cut:]
        copies.append(pltpu.make_async_copy(ref, to, sem.at[i]))
        copies[-1].start()
    out_ref[...] = jnp.zeros_like(out_ref)
    for copy in copies:
        copy.wait()
    for c in range(2):
        for d in range(n_x):
            owner = lax.rem(my_x + d, n_x) * 2 + lax.rem(my_c + c, 2)
            row = kv_ref[c * n_x + d, :HEAD, :DH].astype(F32).astype(jnp.int32)
            all_ids_ref[pl.ds(owner, 1), :] = row[:1, :]

    def place(r):
        i = ids_ref[r // 2, r % 2]
        owner, slot = i // stored, lax.rem(i, stored)
        dx = lax.rem(owner // 2 - my_x + n_x, n_x)
        dc = lax.rem(lax.rem(owner, 2) + my_c, 2)
        return owner, dc * n_x + dx, pl.multiple_of(HEAD + slot * seg, HEAD)

    spots = [place(r) for r in range(2 * blocks)]
    for c in range(blocks):
        both = [kv_ref[spots[r][1], pl.ds(spots[r][2], seg), :] for r in (2 * c, 2 * c + 1)]
        k = jnp.concatenate([b[:, :DH] for b in both], axis=0)
        v = jnp.concatenate([b[:, DH:] for b in both], axis=0)
        rows = slice(c * block_len, (c + 1) * block_len)
        q = q_ref[rows, :]
        g = g_ref[rows, :]
        s = lax.dot_general(q, k, NT, preferred_element_type=F32) * inv_root
        e = jnp.exp(s - jnp.max(s, axis=-1, keepdims=True))
        p = e / jnp.sum(e, axis=-1, keepdims=True)
        ph = p.astype(BF)
        gp = lax.dot_general(g, v, NT, preferred_element_type=F32)
        attn_ref[rows, :] = jnp.dot(ph, v, preferred_element_type=F32).astype(BF)
        gs = (p * (gp - jnp.sum(p * gp, axis=-1, keepdims=True))).astype(BF)
        gq_ref[rows, :] = (jnp.dot(gs, k, preferred_element_type=F32) * inv_root).astype(BF)
        gv = lax.dot_general(ph, g, TN, preferred_element_type=F32).astype(BF)
        gk = (lax.dot_general(gs, q, TN, preferred_element_type=F32) * inv_root).astype(BF)
        for j in range(2):
            r = 2 * c + j
            owner = spots[r][0]
            pos = sum([(spots[i][0] == owner).astype(jnp.int32) for i in range(r)], jnp.int32(0))
            for y in range(n_y):
                part = slice(j * seg + y * piece, j * seg + (y + 1) * piece)
                out_ref[owner, y, pos, :, :DH] = gk[part, :]
                out_ref[owner, y, pos, :, DH:] = gv[part, :]


def encoded_body(stored, pos_ref, ids_ref, ret_ref, *refs):
    owners, n_y, cap, piece, _ = ret_ref.shape
    w_refs, (out_ref, got_ref, w_ref, acc_ref, prod_ref, sem) = refs[:n_y], refs[n_y:]
    me = pos_ref[0] * 2 + pos_ref[1]
    my_y = pos_ref[2]
    for d in range(owners):
        pltpu.make_async_copy(ret_ref.at[d], got_ref.at[d], sem.at[d]).start()
    weights = [pltpu.make_async_copy(w_refs[y], w_ref.at[y], sem.at[owners + y]) for y in range(n_y)]
    for copy in weights:
        copy.start()
    acc_ref[...] = jnp.zeros_like(acc_ref)

    def from_device(d, carry):
        pltpu.make_async_copy(ret_ref.at[d], got_ref.at[d], sem.at[d]).wait()
        count = jnp.int32(0)
        for r in range(owners * 2):
            at = ids_ref[d, r]
            named = at // stored == me

            @pl.when(named)
            def _(at=at, count=count):
                slot = lax.rem(at, stored)
                for y in range(n_y):
                    acc_ref[y, slot] += got_ref[d, y, count].astype(F32)

            count = count + named.astype(jnp.int32)
        return carry

    lax.fori_loop(0, owners, from_device, 0)
    lanes = prod_ref.shape[0]
    for copy in weights:
        copy.wait()
    both = [acc_ref[lax.rem(my_y + y, n_y)].astype(BF).reshape(stored * piece, 2 * DH) for y in range(n_y)]
    both = jnp.concatenate(both, axis=1)
    for n in range(0, lanes, 2):
        wide = min(2, lanes - n)
        w = jnp.concatenate([w_ref[y, n * DH : (n + wide) * DH, :] for y in range(n_y)], axis=1)
        term = lax.dot_general(both, w, NT, preferred_element_type=F32)
        for i in range(wide):
            prod_ref[n + i] = term[:, i * DH : (i + 1) * DH]
    for t in range(0, piece, 2):
        for n in range(lanes):
            two = [prod_ref[n, pl.ds(t + k, stored, stride=piece), :] for k in range(2)]
            out_ref[pl.ds(t * stored, 2 * stored), n * DH : (n + 1) * DH] = jnp.concatenate(two, axis=0).astype(BF)


def head_sum_body(n_z, n_y, second, pos_ref, *refs):
    pieces, mine, other = refs[:n_z], refs[n_z : n_z + 2], refs[n_z + 2 : n_z + 4]
    *outs, a_ref, w_ref, sem = refs[n_z + 4 :]
    my_x, my_c, my_y, my_z = (pos_ref[i] for i in range(4))

    def weight_copies(refs):
        own = lax.rem(my_x, 2)
        return [pltpu.make_async_copy(refs[i], w_ref.at[own if i == 0 else 1 - own], sem.at[n_z + i]) for i in range(2)]

    @pl.when(my_c == second)
    def _():
        for copy in weight_copies(mine):
            copy.start()

    @pl.when(my_c != second)
    def _():
        for copy in weight_copies(other):
            copy.start()

    copies = [
        pltpu.make_async_copy(pieces[j], a_ref.at[:, j * DH : (j + 1) * DH], sem.at[j]) for j in range(n_z)
    ]
    for copy in copies:
        copy.start()
    for copy in weight_copies(mine) + copies:
        copy.wait()
    heads = [lax.rem(my_z + j, n_z) for j in range(n_z)]
    for k in range(0, n_y, 2):
        at = [lax.rem(my_y + k + i, n_y) for i in range(2)]
        if second:
            w = [jnp.concatenate([w_ref[at[i] // 2, h, lax.rem(at[i], 2)] for h in heads], axis=1) for i in range(2)]
            total = lax.dot_general(a_ref[...], jnp.concatenate(w, axis=0), NT, preferred_element_type=F32)
        else:
            w = [jnp.concatenate([w_ref[at[i] // 2, h, lax.rem(at[i], 2)] for h in heads], axis=0) for i in range(2)]
            total = jnp.dot(a_ref[...], jnp.concatenate(w, axis=1), preferred_element_type=F32)
        for i in range(2):
            outs[k + i][...] = total[:, i * DH : (i + 1) * DH].astype(outs[k + i].dtype)


def shards(hidden, encoded, neighbours, w_query, w_key, w_value, w_out, cotangent):
    n_x, n_c, n_y, n_z = (lax.axis_size(a) for a in ("x", "c", "y", "z"))
    dp = ("x", "c")
    owners = n_x * n_c
    rows, width = hidden.shape
    blocks, per_block = neighbours.shape
    cap = blocks * per_block // 4
    stored = encoded.shape[0]
    enc_width = w_key.shape[0]
    seg = encoded.shape[1] // enc_width
    block_len = rows // blocks
    piece = seg // n_y
    core = lax.axis_index("c")
    place = jnp.stack([lax.axis_index(a) for a in ("x", "c", "y", "z")]).astype(jnp.int32)

    def shift(axis, n, k):
        return lambda a: lax.ppermute(a, axis, [(i, (i + k) % n) for i in range(n)])

    swap = shift("c", n_c, 1)
    x_up, x_down = shift("x", n_x, -1), shift("x", n_x, 1)
    z_up, z_down = shift("z", n_z, -1), shift("z", n_z, 1)
    tie = lax.optimization_barrier

    enc_rows = encoded.reshape(stored, seg, enc_width).transpose(1, 0, 2).reshape(seg * stored, enc_width)
    kv, pair = call(
        functools.partial(keys_values_body, stored),
        (jax.ShapeDtypeStruct((HEAD + stored * seg, 2 * DH), BF), jax.ShapeDtypeStruct((enc_width, 2 * DH), BF)),
        "svvv", 470_000_000, 3 << 20,
        scratch=(pltpu.VMEM((2, seg * stored, DH), F32),),
    )(neighbours, enc_rows, w_key, w_value)
    after, before, kv_other = x_up(kv), x_down(kv), swap(kv)
    cut = HEAD + stored // 2 * seg
    next_lo, next_hi = call(
        functools.partial(halves_body, cut),
        (jax.ShapeDtypeStruct((cut, 2 * DH), BF), jax.ShapeDtypeStruct((kv.shape[0] - cut, 2 * DH), BF)),
        "aa", 0, 1 << 20, scratch=(pltpu.SemaphoreType.DMA((2,)),), out_space="a",
    )(after, before)
    far_lo, far_hi = x_up(next_lo), x_down(next_hi)
    w_query_, w_out_, _ = tie((w_query, w_out, next_lo))
    mine = call(
        functools.partial(weights_body, n_z),
        jax.ShapeDtypeStruct((n_z, 2, DH, DH), BF), "saa", 0, 1 << 20,
        scratch=(pltpu.SemaphoreType.DMA((2 * n_z,)),), out_space="a",
    )(place, w_out_, w_query_)
    kv_all = [kv, after, far_lo, far_hi, before, kv_other] + [swap(a) for a in (after, far_lo, far_hi, before)]

    mine = lax.all_to_all(mine, "z", 0, 0, tiled=True)
    y_up, y_down = shift("y", n_y, -1), shift("y", n_y, 1)
    pair_up, pair_down = y_up(pair), y_down(pair)
    pairs = [pair, pair_up, y_up(pair_up), pair_down]

    queries = jnp.dot(hidden, w_query, preferred_element_type=F32).astype(BF)
    grad_attn = lax.dot_general(cotangent, w_out, NT, preferred_element_type=F32).astype(BF)

    queries, grad_attn, pairs = tie((queries, grad_attn, pairs))
    mine = [mine, lax.ppermute(mine, "x", [(i, i ^ 1) for i in range(n_x)])]
    other = [swap(a) for a in mine]

    slab = jax.ShapeDtypeStruct((rows, DH), BF)
    attn, gq, outgoing, ids_all = call(
        functools.partial(attention_body, (blocks, block_len, n_x, n_y, cap, stored, seg)),
        (
            slab,
            slab,
            jax.ShapeDtypeStruct((owners, n_y, cap, piece, 2 * DH), BF),
            jax.ShapeDtypeStruct((owners, DH), jnp.int32),
        ),
        "ssvv" + "a" * len(kv_all), 500_000_000, 7 << 20,
        scratch=(
            pltpu.VMEM((owners, kv.shape[0], 2 * DH), BF),
            pltpu.SemaphoreType.DMA((len(kv_all),)),
        ),
    )(place, neighbours, queries, grad_attn, *kv_all)

    def ring(own):
        pieces = {0: own}
        for k in range(1, n_z // 2 + 1):
            pieces[k] = z_up(pieces[k - 1])
        last = own
        for k in range(1, n_z - n_z // 2):
            last = z_down(last)
            pieces[n_z - k] = last
        return [pieces[k] for k in range(n_z)]

    returned = lax.all_to_all(
        outgoing.reshape(owners * n_y, cap, piece, 2 * DH), dp + ("y",), 0, 0, tiled=True
    ).reshape(owners, n_y, cap, piece, 2 * DH)
    attn_all, gq_all = ring(attn), ring(gq)
    attn_all, gq_all, returned = tie((attn_all, gq_all, returned))
    enc_part = call(
        functools.partial(encoded_body, stored),
        jax.ShapeDtypeStruct((piece * stored, enc_width), BF), "ssa" + "a" * n_y, 500_000_000, 5 << 20,
        scratch=(
            pltpu.VMEM((owners, n_y, cap, piece, 2 * DH), BF),
            pltpu.VMEM((n_y, enc_width, 2 * DH), BF),
            pltpu.VMEM((n_y, stored, piece, 2 * DH), F32),
            pltpu.VMEM((enc_width // DH, stored * piece, DH), F32),
            pltpu.SemaphoreType.DMA((owners + n_y,)),
        ),
    )(place, ids_all, returned, *pairs)
    attn_all, gq_all, enc_part = tie((attn_all, gq_all, enc_part))
    enc_parts = lax.all_to_all(enc_part.reshape(n_z, -1, enc_width), "z", 0, 0, tiled=True)
    enc_rows_sum = jnp.sum(enc_parts.astype(F32), axis=0).astype(BF)
    grad_encoded = enc_rows_sum.reshape(seg // (n_y * n_z), stored, enc_width).transpose(1, 0, 2).reshape(stored, -1)

    def summed(pieces, second):
        parts = call(
            functools.partial(head_sum_body, n_z, n_y, second),
            (jax.ShapeDtypeStruct((rows, DH), F32),) + (slab,) * (n_y - 1),
            "s" + "a" * (n_z + 4), 540_000_000, 3 << 20,
            scratch=(
                pltpu.VMEM((rows, n_z * DH), BF),
                pltpu.VMEM((2, n_z, 2, DH, DH), BF),
                pltpu.SemaphoreType.DMA((n_z + 2,)),
            ),
        )(place, *pieces, *mine, *other)
        total = parts[0]
        for k in range(1, n_y):
            total = total + shift("y", n_y, k)(parts[k]).astype(F32)
        return total.astype(BF)

    return summed(attn_all, 0), summed(gq_all, 1), grad_encoded


def solution(mesh):
    n_y = 4
    dp, mp = mesh.shape["dp"], mesh.shape["mp"]
    split = Mesh(mesh.devices.reshape(dp // 2, 2, n_y, mp // n_y), ("x", "c", "y", "z"))
    d, m = ("x", "c"), ("y", "z")
    return jax.shard_map(
        shards,
        mesh=split,
        in_specs=(P(d, None), P(d, None), P(d, None), P(None, m), P(None, m), P(None, m), P(m, None), P(d, None)),
        out_specs=(P(d, m), P(d, m), P(d, m)),
        check_vma=False,
    )
```

```python
import functools
import math

import jax
import jax.numpy as jnp
from jax import lax
from jax.experimental import pallas as pl
from jax.experimental.pallas import tpu as pltpu
from jax.sharding import Mesh, PartitionSpec as P

DH = 128
BF = jnp.bfloat16
F32 = jnp.float32
NT = (((1,), (1,)), ((), ()))
TN = (((0,), (0,)), ((), ()))
HEAD = 16
VMEM_LIMIT = 60 * 1024 * 1024


def params():
    return pltpu.CompilerParams(vmem_limit_bytes=VMEM_LIMIT)


def call(body, out_shape, in_spaces, flops, moved, scratch=(), out_space="v"):
    spaces = {"s": pltpu.SMEM, "v": pltpu.VMEM, "a": pltpu.HBM}
    single = not isinstance(out_shape, (tuple, list))
    out = pl.BlockSpec(memory_space=spaces[out_space])
    return pl.pallas_call(
        body,
        out_shape=out_shape,
        in_specs=[pl.BlockSpec(memory_space=spaces[k]) for k in in_spaces],
        out_specs=out if single else (out,) * len(out_shape),
        scratch_shapes=list(scratch),
        compiler_params=params(),
        cost_estimate=pl.CostEstimate(flops=flops, bytes_accessed=moved, transcendentals=0),
    )


def keys_values_body(stored, ids_ref, x_ref, wk_ref, wv_ref, out_ref, pair_ref, kv_ref):
    pair = jnp.concatenate([wk_ref[...], wv_ref[...]], axis=1)
    pair_ref[...] = pair
    seg = x_ref.shape[0] // stored
    both = jnp.dot(x_ref[...], pair, preferred_element_type=F32)
    for n in range(kv_ref.shape[0]):
        kv_ref[n] = both[:, n * DH : (n + 1) * DH]
        for s in range(stored):
            rows = slice(HEAD + s * seg, HEAD + (s + 1) * seg)
            out_ref[rows, n * DH : (n + 1) * DH] = kv_ref[n, pl.ds(s, seg, stride=stored), :].astype(BF)
    lane = lax.broadcasted_iota(jnp.int32, (HEAD, 2 * DH), 1)
    row = jnp.zeros((HEAD, 2 * DH), F32)
    for r in range(2 * ids_ref.shape[0]):
        row = jnp.where(lane == r, ids_ref[r // 2, r % 2].astype(F32), row)
    out_ref[:HEAD, :] = row.astype(BF)


def halves_body(cut, after_ref, before_ref, lo_ref, hi_ref, sem):
    copies = [
        pltpu.make_async_copy(after_ref.at[:cut], lo_ref, sem.at[0]),
        pltpu.make_async_copy(before_ref.at[cut:], hi_ref, sem.at[1]),
    ]
    for copy in copies:
        copy.start()
    for copy in copies:
        copy.wait()


def weights_body(n_z, n_y, pos_ref, wo_ref, wq_ref, out_ref, sem):
    def move(block):
        copies = [
            pltpu.make_async_copy(block((y * n_z + z) * DH), out_ref.at[z, y], sem.at[y * n_z + z])
            for y in range(n_y)
            for z in range(n_z)
        ]
        for copy in copies:
            copy.start()
        for copy in copies:
            copy.wait()

    @pl.when(pos_ref[1] == 0)
    def _():
        move(lambda at: wo_ref.at[:, at : at + DH])

    @pl.when(pos_ref[1] != 0)
    def _():
        move(lambda at: wq_ref.at[at : at + DH, :])


def attention_body(geom, pos_ref, ids_ref, q_ref, g_ref, *refs):
    blocks, block_len, n_x, n_y, cap, stored, seg = geom
    kv_refs, (attn_ref, gq_ref, out_ref, all_ids_ref, kv_ref, sem) = refs[:-6], refs[-6:]
    inv_root = 1.0 / math.sqrt(DH)
    piece = seg // n_y
    my_x, my_c = pos_ref[0], pos_ref[1]
    copies = []
    for i, ref in enumerate(kv_refs):
        c, k = i // 5, i % 5
        cut = HEAD + stored // 2 * seg
        if k < 2:
            to = kv_ref.at[c * n_x + k]
        elif k == 4:
            to = kv_ref.at[c * n_x + 3]
        else:
            to = kv_ref.at[c * n_x + 2, :cut] if k == 2 else kv_ref.at[c * n_x + 2, cut:]
        copies.append(pltpu.make_async_copy(ref, to, sem.at[i]))
        copies[-1].start()
    out_ref[...] = jnp.zeros_like(out_ref)
    for copy in copies:
        copy.wait()
    for c in range(2):
        for d in range(n_x):
            owner = lax.rem(my_x + d, n_x) * 2 + lax.rem(my_c + c, 2)
            row = kv_ref[c * n_x + d, :HEAD, :DH].astype(F32).astype(jnp.int32)
            all_ids_ref[pl.ds(owner, 1), :] = row[:1, :]

    def place(r):
        i = ids_ref[r // 2, r % 2]
        owner, slot = i // stored, lax.rem(i, stored)
        dx = lax.rem(owner // 2 - my_x + n_x, n_x)
        dc = lax.rem(lax.rem(owner, 2) + my_c, 2)
        return owner, dc * n_x + dx, pl.multiple_of(HEAD + slot * seg, HEAD)

    spots = [place(r) for r in range(2 * blocks)]
    for c in range(blocks):
        both = [kv_ref[spots[r][1], pl.ds(spots[r][2], seg), :] for r in (2 * c, 2 * c + 1)]
        k = jnp.concatenate([b[:, :DH] for b in both], axis=0)
        v = jnp.concatenate([b[:, DH:] for b in both], axis=0)
        rows = slice(c * block_len, (c + 1) * block_len)
        q = q_ref[rows, :]
        g = g_ref[rows, :]
        s = lax.dot_general(q, k, NT, preferred_element_type=F32) * inv_root
        e = jnp.exp(s - jnp.max(s, axis=-1, keepdims=True))
        p = e / jnp.sum(e, axis=-1, keepdims=True)
        ph = p.astype(BF)
        gp = lax.dot_general(g, v, NT, preferred_element_type=F32)
        attn_ref[rows, :] = jnp.dot(ph, v, preferred_element_type=F32).astype(BF)
        gs = (p * (gp - jnp.sum(p * gp, axis=-1, keepdims=True))).astype(BF)
        gq_ref[rows, :] = (jnp.dot(gs, k, preferred_element_type=F32) * inv_root).astype(BF)
        gv = lax.dot_general(ph, g, TN, preferred_element_type=F32).astype(BF)
        gk = (lax.dot_general(gs, q, TN, preferred_element_type=F32) * inv_root).astype(BF)
        for j in range(2):
            r = 2 * c + j
            owner = spots[r][0]
            pos = sum([(spots[i][0] == owner).astype(jnp.int32) for i in range(r)], jnp.int32(0))
            for y in range(n_y):
                part = slice(j * seg + y * piece, j * seg + (y + 1) * piece)
                out_ref[owner, y, pos, :, :DH] = gk[part, :]
                out_ref[owner, y, pos, :, DH:] = gv[part, :]


def encoded_body(stored, pos_ref, ids_ref, ret_ref, *refs):
    owners, n_y, cap, piece, _ = ret_ref.shape
    w_refs, (out_ref, got_ref, w_ref, acc_ref, prod_ref, sem) = refs[:n_y], refs[n_y:]
    me = pos_ref[0] * 2 + pos_ref[1]
    my_y = pos_ref[2]
    for d in range(owners):
        pltpu.make_async_copy(ret_ref.at[d], got_ref.at[d], sem.at[d]).start()
    weights = [pltpu.make_async_copy(w_refs[y], w_ref.at[y], sem.at[owners + y]) for y in range(n_y)]
    for copy in weights:
        copy.start()
    acc_ref[...] = jnp.zeros_like(acc_ref)

    def from_device(d, carry):
        pltpu.make_async_copy(ret_ref.at[d], got_ref.at[d], sem.at[d]).wait()
        count = jnp.int32(0)
        for r in range(owners * 2):
            at = ids_ref[d, r]
            named = at // stored == me

            @pl.when(named)
            def _(at=at, count=count):
                slot = lax.rem(at, stored)
                for y in range(n_y):
                    acc_ref[y, slot] += got_ref[d, y, count].astype(F32)

            count = count + named.astype(jnp.int32)
        return carry

    lax.fori_loop(0, owners, from_device, 0)
    lanes = prod_ref.shape[0]
    for copy in weights:
        copy.wait()
    both = [acc_ref[lax.rem(my_y + y, n_y)].astype(BF).reshape(stored * piece, 2 * DH) for y in range(n_y)]
    both = jnp.concatenate(both, axis=1)
    for n in range(0, lanes, 2):
        wide = min(2, lanes - n)
        w = jnp.concatenate([w_ref[y, n * DH : (n + wide) * DH, :] for y in range(n_y)], axis=1)
        term = lax.dot_general(both, w, NT, preferred_element_type=F32)
        for i in range(wide):
            prod_ref[n + i] = term[:, i * DH : (i + 1) * DH]
    for t in range(0, piece, 2):
        for n in range(lanes):
            two = [prod_ref[n, pl.ds(t + k, stored, stride=piece), :] for k in range(2)]
            out_ref[pl.ds(t * stored, 2 * stored), n * DH : (n + 1) * DH] = jnp.concatenate(two, axis=0).astype(BF)


def head_sum_body(n_z, n_y, second, pos_ref, *refs):
    pieces, mine, other = refs[:n_z], refs[n_z], refs[n_z + 1]
    *outs, a_ref, w_ref, sem = refs[n_z + 2 :]
    my_c, my_y, my_z = (pos_ref[i] for i in range(1, 4))

    @pl.when(my_c == second)
    def _():
        pltpu.make_async_copy(mine, w_ref, sem.at[n_z]).start()

    @pl.when(my_c != second)
    def _():
        pltpu.make_async_copy(other, w_ref, sem.at[n_z]).start()

    copies = [
        pltpu.make_async_copy(pieces[j], a_ref.at[:, j * DH : (j + 1) * DH], sem.at[j]) for j in range(n_z)
    ]
    for copy in copies:
        copy.start()
    pltpu.make_async_copy(mine, w_ref, sem.at[n_z]).wait()
    for copy in copies:
        copy.wait()
    heads = [lax.rem(my_z + j, n_z) for j in range(n_z)]
    for k in range(0, n_y, 2):
        at = [lax.rem(my_y + k + i, n_y) for i in range(2)]
        if second:
            w = [jnp.concatenate([w_ref[h, at[i]] for h in heads], axis=1) for i in range(2)]
            total = lax.dot_general(a_ref[...], jnp.concatenate(w, axis=0), NT, preferred_element_type=F32)
        else:
            w = [jnp.concatenate([w_ref[h, at[i]] for h in heads], axis=0) for i in range(2)]
            total = jnp.dot(a_ref[...], jnp.concatenate(w, axis=1), preferred_element_type=F32)
        for i in range(2):
            outs[k + i][...] = total[:, i * DH : (i + 1) * DH].astype(outs[k + i].dtype)


def shards(hidden, encoded, neighbours, w_query, w_key, w_value, w_out, cotangent):
    n_x, n_c, n_y, n_z = (lax.axis_size(a) for a in ("x", "c", "y", "z"))
    dp = ("x", "c")
    owners = n_x * n_c
    rows, width = hidden.shape
    blocks, per_block = neighbours.shape
    cap = blocks * per_block // 4
    stored = encoded.shape[0]
    enc_width = w_key.shape[0]
    seg = encoded.shape[1] // enc_width
    block_len = rows // blocks
    piece = seg // n_y
    core = lax.axis_index("c")
    place = jnp.stack([lax.axis_index(a) for a in ("x", "c", "y", "z")]).astype(jnp.int32)

    def shift(axis, n, k):
        return lambda a: lax.ppermute(a, axis, [(i, (i + k) % n) for i in range(n)])

    swap = shift("c", n_c, 1)
    x_up, x_down = shift("x", n_x, -1), shift("x", n_x, 1)
    z_up, z_down = shift("z", n_z, -1), shift("z", n_z, 1)
    tie = lax.optimization_barrier

    enc_rows = encoded.reshape(stored, seg, enc_width).transpose(1, 0, 2).reshape(seg * stored, enc_width)
    kv, pair = call(
        functools.partial(keys_values_body, stored),
        (jax.ShapeDtypeStruct((HEAD + stored * seg, 2 * DH), BF), jax.ShapeDtypeStruct((enc_width, 2 * DH), BF)),
        "svvv", 470_000_000, 3 << 20,
        scratch=(pltpu.VMEM((2, seg * stored, DH), F32),),
    )(neighbours, enc_rows, w_key, w_value)
    after, before, kv_other = x_up(kv), x_down(kv), swap(kv)

    w_query_, w_out_, kv_other = tie((w_query, w_out, kv_other))
    mine = call(
        functools.partial(weights_body, n_z, n_y),
        jax.ShapeDtypeStruct((n_z, n_y, DH, DH), BF), "saa", 0, 2 << 20,
        scratch=(pltpu.SemaphoreType.DMA((n_z * n_y,)),),
    )(place, w_out_, w_query_)
    after, before, mine = tie((after, before, mine))
    mine = lax.all_to_all(mine, "z", 0, 0, tiled=True)

    cut = HEAD + stored // 2 * seg
    next_lo, next_hi = call(
        functools.partial(halves_body, cut),
        (jax.ShapeDtypeStruct((cut, 2 * DH), BF), jax.ShapeDtypeStruct((kv.shape[0] - cut, 2 * DH), BF)),
        "aa", 0, 1 << 20, scratch=(pltpu.SemaphoreType.DMA((2,)),),
    )(after, before)
    far_lo, far_hi = x_up(next_lo), x_down(next_hi)
    pair_, far_lo, far_hi = tie((pair, far_lo, far_hi))
    kv_all = [kv, after, far_lo, far_hi, before, kv_other] + [swap(a) for a in (after, far_lo, far_hi, before)]

    y_up, y_down = shift("y", n_y, -1), shift("y", n_y, 1)
    pair_up, pair_down = y_up(pair_), y_down(pair_)
    pairs = [pair, pair_up, y_up(pair_up), pair_down]

    queries = jnp.dot(hidden, w_query, preferred_element_type=F32).astype(BF)
    grad_attn = lax.dot_general(cotangent, w_out, NT, preferred_element_type=F32).astype(BF)

    other = swap(mine)

    slab = jax.ShapeDtypeStruct((rows, DH), BF)
    attn, gq, outgoing, ids_all = call(
        functools.partial(attention_body, (blocks, block_len, n_x, n_y, cap, stored, seg)),
        (
            slab,
            slab,
            jax.ShapeDtypeStruct((owners, n_y, cap, piece, 2 * DH), BF),
            jax.ShapeDtypeStruct((owners, DH), jnp.int32),
        ),
        "ssvv" + "a" * len(kv_all), 500_000_000, 7 << 20,
        scratch=(
            pltpu.VMEM((owners, kv.shape[0], 2 * DH), BF),
            pltpu.SemaphoreType.DMA((len(kv_all),)),
        ),
    )(place, neighbours, queries, grad_attn, *kv_all)

    def ring(own):
        pieces = {0: own}
        for k in range(1, n_z // 2 + 1):
            pieces[k] = z_up(pieces[k - 1])
        last = own
        for k in range(1, n_z - n_z // 2):
            last = z_down(last)
            pieces[n_z - k] = last
        return [pieces[k] for k in range(n_z)]

    returned = lax.all_to_all(
        outgoing.reshape(owners * n_y, cap, piece, 2 * DH), dp + ("y",), 0, 0, tiled=True
    ).reshape(owners, n_y, cap, piece, 2 * DH)
    attn_all, gq_all = ring(attn), ring(gq)
    attn_all, gq_all, returned = tie((attn_all, gq_all, returned))
    enc_part = call(
        functools.partial(encoded_body, stored),
        jax.ShapeDtypeStruct((piece * stored, enc_width), BF), "ssa" + "a" * n_y, 500_000_000, 5 << 20,
        scratch=(
            pltpu.VMEM((owners, n_y, cap, piece, 2 * DH), BF),
            pltpu.VMEM((n_y, enc_width, 2 * DH), BF),
            pltpu.VMEM((n_y, stored, piece, 2 * DH), F32),
            pltpu.VMEM((enc_width // DH, stored * piece, DH), F32),
            pltpu.SemaphoreType.DMA((owners + n_y,)),
        ),
    )(place, ids_all, returned, *pairs)
    attn_all, gq_all, enc_part = tie((attn_all, gq_all, enc_part))
    enc_parts = lax.all_to_all(enc_part.reshape(n_z, -1, enc_width), "z", 0, 0, tiled=True)
    enc_rows_sum = jnp.sum(enc_parts.astype(F32), axis=0).astype(BF)
    grad_encoded = enc_rows_sum.reshape(seg // (n_y * n_z), stored, enc_width).transpose(1, 0, 2).reshape(stored, -1)

    def summed(pieces, second):
        parts = call(
            functools.partial(head_sum_body, n_z, n_y, second),
            (jax.ShapeDtypeStruct((rows, DH), F32),) + (slab,) * (n_y - 1),
            "s" + "a" * (n_z + 2), 540_000_000, 3 << 20,
            scratch=(
                pltpu.VMEM((rows, n_z * DH), BF),
                pltpu.VMEM((n_z, n_y, DH, DH), BF),
                pltpu.SemaphoreType.DMA((n_z + 1,)),
            ),
        )(place, *pieces, mine, other)
        total = parts[0]
        for k in range(1, n_y):
            total = total + shift("y", n_y, k)(parts[k]).astype(F32)
        return total.astype(BF)

    return summed(attn_all, 0), summed(gq_all, 1), grad_encoded


def solution(mesh):
    n_y = 4
    dp, mp = mesh.shape["dp"], mesh.shape["mp"]
    split = Mesh(mesh.devices.reshape(dp // 2, 2, n_y, mp // n_y), ("x", "c", "y", "z"))
    d, m = ("x", "c"), ("y", "z")
    return jax.shard_map(
        shards,
        mesh=split,
        in_specs=(P(d, None), P(d, None), P(d, None), P(None, m), P(None, m), P(None, m), P(m, None), P(d, None)),
        out_specs=(P(d, m), P(d, m), P(d, m)),
        check_vma=False,
    )
```

```python
import functools
import math

import jax
import jax.numpy as jnp
from jax import lax
from jax.experimental import pallas as pl
from jax.experimental.pallas import tpu as pltpu
from jax.sharding import Mesh, PartitionSpec as P

DH = 128
BF = jnp.bfloat16
F32 = jnp.float32
NT = (((1,), (1,)), ((), ()))
TN = (((0,), (0,)), ((), ()))
HEAD = 16
VMEM_LIMIT = 63 * 1024 * 1024


def params():
    return pltpu.CompilerParams(vmem_limit_bytes=VMEM_LIMIT)


def call(body, out_shape, in_spaces, flops, moved, scratch=(), out_space="v"):
    spaces = {"s": pltpu.SMEM, "v": pltpu.VMEM, "a": pltpu.HBM}
    single = not isinstance(out_shape, (tuple, list))
    out = pl.BlockSpec(memory_space=spaces[out_space])
    return pl.pallas_call(
        body,
        out_shape=out_shape,
        in_specs=[pl.BlockSpec(memory_space=spaces[k]) for k in in_spaces],
        out_specs=out if single else (out,) * len(out_shape),
        scratch_shapes=list(scratch),
        compiler_params=params(),
        cost_estimate=pl.CostEstimate(flops=flops, bytes_accessed=moved, transcendentals=0),
    )


def keys_values_body(stored, ids_ref, x_ref, wk_ref, wv_ref, out_ref, pair_ref, kv_ref):
    pair = jnp.concatenate([wk_ref[...], wv_ref[...]], axis=1)
    pair_ref[...] = pair
    seg = x_ref.shape[0] // stored
    both = jnp.dot(x_ref[...], pair, preferred_element_type=F32)
    for n in range(kv_ref.shape[0]):
        kv_ref[n] = both[:, n * DH : (n + 1) * DH]
        for s in range(stored):
            rows = slice(HEAD + s * seg, HEAD + (s + 1) * seg)
            out_ref[rows, n * DH : (n + 1) * DH] = kv_ref[n, pl.ds(s, seg, stride=stored), :].astype(BF)
    lane = lax.broadcasted_iota(jnp.int32, (HEAD, 2 * DH), 1)
    row = jnp.zeros((HEAD, 2 * DH), F32)
    for r in range(2 * ids_ref.shape[1]):
        row = jnp.where(lane == r, ids_ref[r % 2, r // 2].astype(F32), row)
    out_ref[:HEAD, :] = row.astype(BF)


def halves_body(cut, after_ref, before_ref, lo_ref, hi_ref, sem):
    copies = [
        pltpu.make_async_copy(after_ref.at[:cut], lo_ref, sem.at[0]),
        pltpu.make_async_copy(before_ref.at[cut:], hi_ref, sem.at[1]),
    ]
    for copy in copies:
        copy.start()
    for copy in copies:
        copy.wait()


def weights_body(n_z, n_y, pos_ref, wo_ref, wq_ref, out_ref, sem):
    def move(block):
        copies = [
            pltpu.make_async_copy(block((y * n_z + z) * DH), out_ref.at[z, y], sem.at[y * n_z + z])
            for y in range(n_y)
            for z in range(n_z)
        ]
        for copy in copies:
            copy.start()
        for copy in copies:
            copy.wait()

    @pl.when(pos_ref[1] == 0)
    def _():
        move(lambda at: wo_ref.at[:, at : at + DH])

    @pl.when(pos_ref[1] != 0)
    def _():
        move(lambda at: wq_ref.at[at : at + DH, :])


def attention_body(geom, pos_ref, ids_ref, q_ref, g_ref, *refs):
    blocks, block_len, n_x, n_y, cap, stored, seg = geom
    kv_refs, (attn_ref, gq_ref, out_ref, all_ids_ref, kv_ref, sem) = refs[:-6], refs[-6:]
    inv_root = 1.0 / math.sqrt(DH)
    piece = seg // n_y
    my_x, my_c = pos_ref[0], pos_ref[1]
    copies = []
    for i, ref in enumerate(kv_refs):
        c, k = i // 5, i % 5
        cut = HEAD + stored // 2 * seg
        if k < 2:
            to = kv_ref.at[c * n_x + k]
        elif k == 4:
            to = kv_ref.at[c * n_x + 3]
        else:
            to = kv_ref.at[c * n_x + 2, :cut] if k == 2 else kv_ref.at[c * n_x + 2, cut:]
        copies.append(pltpu.make_async_copy(ref, to, sem.at[i]))
        copies[-1].start()
    out_ref[...] = jnp.zeros_like(out_ref)
    for copy in copies:
        copy.wait()
    for c in range(2):
        for d in range(n_x):
            owner = lax.rem(my_x + d, n_x) * 2 + lax.rem(my_c + c, 2)
            row = kv_ref[c * n_x + d, :HEAD, :DH].astype(F32).astype(jnp.int32)
            all_ids_ref[pl.ds(owner, 1), :] = row[:1, :]

    def place(r):
        i = ids_ref[r % 2, r // 2]
        owner, slot = i // stored, lax.rem(i, stored)
        dx = lax.rem(owner // 2 - my_x + n_x, n_x)
        dc = lax.rem(lax.rem(owner, 2) + my_c, 2)
        return owner, dc * n_x + dx, pl.multiple_of(HEAD + slot * seg, HEAD)

    spots = [place(r) for r in range(2 * blocks)]
    for c in range(blocks):
        both = [kv_ref[spots[r][1], pl.ds(spots[r][2], seg), :] for r in (2 * c, 2 * c + 1)]
        k = jnp.concatenate([b[:, :DH] for b in both], axis=0)
        v = jnp.concatenate([b[:, DH:] for b in both], axis=0)
        rows = slice(c * block_len, (c + 1) * block_len)
        q = q_ref[rows, :]
        g = g_ref[rows, :]
        s = lax.dot_general(q, k, NT, preferred_element_type=F32) * inv_root
        e = jnp.exp(s - jnp.max(s, axis=-1, keepdims=True))
        p = e / jnp.sum(e, axis=-1, keepdims=True)
        ph = p.astype(BF)
        gp = lax.dot_general(g, v, NT, preferred_element_type=F32)
        attn_ref[rows, :] = jnp.dot(ph, v, preferred_element_type=F32).astype(BF)
        gs = (p * (gp - jnp.sum(p * gp, axis=-1, keepdims=True))).astype(BF)
        gq_ref[rows, :] = (jnp.dot(gs, k, preferred_element_type=F32) * inv_root).astype(BF)
        gv = lax.dot_general(ph, g, TN, preferred_element_type=F32).astype(BF)
        gk = (lax.dot_general(gs, q, TN, preferred_element_type=F32) * inv_root).astype(BF)
        for j in range(2):
            r = 2 * c + j
            owner = spots[r][0]
            pos = sum([(spots[i][0] == owner).astype(jnp.int32) for i in range(r)], jnp.int32(0))
            for y in range(n_y):
                part = slice(j * seg + y * piece, j * seg + (y + 1) * piece)
                out_ref[owner, y, pos, :, :DH] = gk[part, :]
                out_ref[owner, y, pos, :, DH:] = gv[part, :]


def encoded_body(stored, pos_ref, ids_ref, ret_ref, *refs):
    owners, n_y, cap, piece, _ = ret_ref.shape
    w_refs, (out_ref, got_ref, w_ref, acc_ref, prod_ref, sem) = refs[:n_y], refs[n_y:]
    me = pos_ref[0] * 2 + pos_ref[1]
    my_y = pos_ref[2]
    for d in range(owners):
        pltpu.make_async_copy(ret_ref.at[d], got_ref.at[d], sem.at[d]).start()
    weights = [pltpu.make_async_copy(w_refs[y], w_ref.at[y], sem.at[owners + y]) for y in range(n_y)]
    for copy in weights:
        copy.start()
    acc_ref[...] = jnp.zeros_like(acc_ref)

    def from_device(d, carry):
        pltpu.make_async_copy(ret_ref.at[d], got_ref.at[d], sem.at[d]).wait()
        count = jnp.int32(0)
        for r in range(owners * 2):
            at = ids_ref[d, r]
            named = at // stored == me

            @pl.when(named)
            def _(at=at, count=count):
                slot = lax.rem(at, stored)
                for y in range(n_y):
                    acc_ref[y, slot] += got_ref[d, y, count].astype(F32)

            count = count + named.astype(jnp.int32)
        return carry

    lax.fori_loop(0, owners, from_device, 0)
    lanes = prod_ref.shape[0]
    for copy in weights:
        copy.wait()
    both = [acc_ref[lax.rem(my_y + y, n_y)].astype(BF).reshape(stored * piece, 2 * DH) for y in range(n_y)]
    both = jnp.concatenate(both, axis=1)
    for n in range(0, lanes, 2):
        wide = min(2, lanes - n)
        w = jnp.concatenate([w_ref[y, n * DH : (n + wide) * DH, :] for y in range(n_y)], axis=1)
        term = lax.dot_general(both, w, NT, preferred_element_type=F32)
        for i in range(wide):
            prod_ref[n + i] = term[:, i * DH : (i + 1) * DH]
    for t in range(0, piece, 2):
        for n in range(lanes):
            two = [prod_ref[n, pl.ds(t + k, stored, stride=piece), :] for k in range(2)]
            out_ref[pl.ds(t * stored, 2 * stored), n * DH : (n + 1) * DH] = jnp.concatenate(two, axis=0).astype(BF)


def head_sum_body(n_z, n_y, second, pos_ref, *refs):
    pieces, mine, other = refs[:n_z], refs[n_z], refs[n_z + 1]
    *outs, a_ref, w_ref, sem = refs[n_z + 2 :]
    my_c, my_y, my_z = (pos_ref[i] for i in range(1, 4))

    @pl.when(my_c == second)
    def _():
        pltpu.make_async_copy(mine, w_ref, sem.at[n_z]).start()

    @pl.when(my_c != second)
    def _():
        pltpu.make_async_copy(other, w_ref, sem.at[n_z]).start()

    copies = [
        pltpu.make_async_copy(pieces[j], a_ref.at[:, j * DH : (j + 1) * DH], sem.at[j]) for j in range(n_z)
    ]
    for copy in copies:
        copy.start()
    pltpu.make_async_copy(mine, w_ref, sem.at[n_z]).wait()
    for copy in copies:
        copy.wait()
    heads = [lax.rem(my_z + j, n_z) for j in range(n_z)]
    for k in range(0, n_y, 2):
        at = [lax.rem(my_y + k + i, n_y) for i in range(2)]
        if second:
            w = [jnp.concatenate([w_ref[h, at[i]] for h in heads], axis=1) for i in range(2)]
            total = lax.dot_general(a_ref[...], jnp.concatenate(w, axis=0), NT, preferred_element_type=F32)
        else:
            w = [jnp.concatenate([w_ref[h, at[i]] for h in heads], axis=0) for i in range(2)]
            total = jnp.dot(a_ref[...], jnp.concatenate(w, axis=1), preferred_element_type=F32)
        for i in range(2):
            outs[k + i][...] = total[:, i * DH : (i + 1) * DH].astype(outs[k + i].dtype)


def shards(hidden, encoded, neighbours, w_query, w_key, w_value, w_out, cotangent):
    n_x, n_c, n_y, n_z = (lax.axis_size(a) for a in ("x", "c", "y", "z"))
    dp = ("x", "c")
    owners = n_x * n_c
    rows, width = hidden.shape
    blocks, per_block = neighbours.shape
    cap = blocks * per_block // 4
    stored = encoded.shape[0]
    enc_width = w_key.shape[0]
    seg = encoded.shape[1] // enc_width
    block_len = rows // blocks
    piece = seg // n_y
    ids = neighbours.T
    place = jnp.stack([lax.axis_index(a) for a in ("x", "c", "y", "z")]).astype(jnp.int32)

    def shift(axis, n, k):
        return lambda a: lax.ppermute(a, axis, [(i, (i + k) % n) for i in range(n)])

    swap = shift("c", n_c, 1)
    x_up, x_down = shift("x", n_x, -1), shift("x", n_x, 1)
    z_up, z_down = shift("z", n_z, -1), shift("z", n_z, 1)
    tie = lax.optimization_barrier

    enc_rows = encoded.reshape(stored, seg, enc_width).transpose(1, 0, 2).reshape(seg * stored, enc_width)
    kv, pair = call(
        functools.partial(keys_values_body, stored),
        (jax.ShapeDtypeStruct((HEAD + stored * seg, 2 * DH), BF), jax.ShapeDtypeStruct((enc_width, 2 * DH), BF)),
        "svvv", 470_000_000, 3 << 20,
        scratch=(pltpu.VMEM((2, seg * stored, DH), F32),),
    )(ids, enc_rows, w_key, w_value)
    after, before, kv_other = x_up(kv), x_down(kv), swap(kv)

    w_query_, w_out_, kv_other = tie((w_query, w_out, kv_other))
    mine = call(
        functools.partial(weights_body, n_z, n_y),
        jax.ShapeDtypeStruct((n_z, n_y, DH, DH), BF), "saa", 0, 2 << 20,
        scratch=(pltpu.SemaphoreType.DMA((n_z * n_y,)),),
    )(place, w_out_, w_query_)
    y_up, y_down = shift("y", n_y, -1), shift("y", n_y, 1)
    pair_up, pair_down = y_up(pair), y_down(pair)
    after, before, mine, pair_up, pair_down = tie((after, before, mine, pair_up, pair_down))
    mine = lax.all_to_all(mine, "z", 0, 0, tiled=True)

    cut = HEAD + stored // 2 * seg
    next_lo, next_hi = call(
        functools.partial(halves_body, cut),
        (jax.ShapeDtypeStruct((cut, 2 * DH), BF), jax.ShapeDtypeStruct((kv.shape[0] - cut, 2 * DH), BF)),
        "aa", 0, 1 << 20, scratch=(pltpu.SemaphoreType.DMA((2,)),),
    )(after, before)
    far_lo, far_hi = x_up(next_lo), x_down(next_hi)
    kv_all = [kv, after, far_lo, far_hi, before, kv_other] + [swap(a) for a in (after, far_lo, far_hi, before)]
    pairs = [pair, pair_up, y_up(pair_up), pair_down]

    queries = jnp.dot(hidden, w_query, preferred_element_type=F32).astype(BF)
    grad_attn = lax.dot_general(cotangent, w_out, NT, preferred_element_type=F32).astype(BF)

    queries, grad_attn, pairs = tie((queries, grad_attn, pairs))
    other = swap(mine)

    slab = jax.ShapeDtypeStruct((rows, DH), BF)
    attn, gq, outgoing, ids_all = call(
        functools.partial(attention_body, (blocks, block_len, n_x, n_y, cap, stored, seg)),
        (
            slab,
            slab,
            jax.ShapeDtypeStruct((owners, n_y, cap, piece, 2 * DH), BF),
            jax.ShapeDtypeStruct((owners, DH), jnp.int32),
        ),
        "ssvv" + "a" * len(kv_all), 500_000_000, 7 << 20,
        scratch=(
            pltpu.VMEM((owners, kv.shape[0], 2 * DH), BF),
            pltpu.SemaphoreType.DMA((len(kv_all),)),
        ),
    )(place, ids, queries, grad_attn, *kv_all)

    def ring(own):
        pieces = {0: own}
        for k in range(1, n_z // 2 + 1):
            pieces[k] = z_up(pieces[k - 1])
        last = own
        for k in range(1, n_z - n_z // 2):
            last = z_down(last)
            pieces[n_z - k] = last
        return [pieces[k] for k in range(n_z)]

    returned = lax.all_to_all(
        outgoing.reshape(owners * n_y, cap, piece, 2 * DH), dp + ("y",), 0, 0, tiled=True
    ).reshape(owners, n_y, cap, piece, 2 * DH)
    attn_all, gq_all = ring(attn), ring(gq)
    attn_all, gq_all, returned = tie((attn_all, gq_all, returned))
    enc_part = call(
        functools.partial(encoded_body, stored),
        jax.ShapeDtypeStruct((piece * stored, enc_width), BF), "ssa" + "a" * n_y, 500_000_000, 5 << 20,
        scratch=(
            pltpu.VMEM((owners, n_y, cap, piece, 2 * DH), BF),
            pltpu.VMEM((n_y, enc_width, 2 * DH), BF),
            pltpu.VMEM((n_y, stored, piece, 2 * DH), F32),
            pltpu.VMEM((enc_width // DH, stored * piece, DH), F32),
            pltpu.SemaphoreType.DMA((owners + n_y,)),
        ),
    )(place, ids_all, returned, *pairs)
    attn_all, gq_all, enc_part = tie((attn_all, gq_all, enc_part))
    enc_parts = lax.all_to_all(enc_part.reshape(n_z, -1, enc_width), "z", 0, 0, tiled=True)
    enc_rows_sum = jnp.sum(enc_parts.astype(F32), axis=0).astype(BF)
    grad_encoded = enc_rows_sum.reshape(seg // (n_y * n_z), stored, enc_width).transpose(1, 0, 2).reshape(stored, -1)

    def summed(pieces, second):
        parts = call(
            functools.partial(head_sum_body, n_z, n_y, second),
            (jax.ShapeDtypeStruct((rows, DH), F32),) + (slab,) * (n_y - 1),
            "s" + "a" * (n_z + 2), 540_000_000, 3 << 20,
            scratch=(
                pltpu.VMEM((rows, n_z * DH), BF),
                pltpu.VMEM((n_z, n_y, DH, DH), BF),
                pltpu.SemaphoreType.DMA((n_z + 1,)),
            ),
        )(place, *pieces, mine, other)
        total = parts[0]
        for k in range(1, n_y):
            total = total + shift("y", n_y, k)(parts[k]).astype(F32)
        return total.astype(BF)

    return summed(attn_all, 0), summed(gq_all, 1), grad_encoded


def solution(mesh):
    n_y = 4
    dp, mp = mesh.shape["dp"], mesh.shape["mp"]
    split = Mesh(mesh.devices.reshape(dp // 2, 2, n_y, mp // n_y), ("x", "c", "y", "z"))
    d, m = ("x", "c"), ("y", "z")
    return jax.shard_map(
        shards,
        mesh=split,
        in_specs=(P(d, None), P(d, None), P(d, None), P(None, m), P(None, m), P(None, m), P(m, None), P(d, None)),
        out_specs=(P(d, m), P(d, m), P(d, m)),
        check_vma=False,
    )
```

```python
import functools
import math

import jax
import jax.numpy as jnp
from jax import lax
from jax.experimental import pallas as pl
from jax.experimental.pallas import tpu as pltpu
from jax.sharding import Mesh, PartitionSpec as P

DH = 128
BF = jnp.bfloat16
F32 = jnp.float32
NT = (((1,), (1,)), ((), ()))
TN = (((0,), (0,)), ((), ()))
HEAD = 16
VMEM_LIMIT = 63 * 1024 * 1024


def params():
    return pltpu.CompilerParams(vmem_limit_bytes=VMEM_LIMIT)


def call(body, out_shape, in_spaces, flops, moved, scratch=(), out_space="v"):
    spaces = {"s": pltpu.SMEM, "v": pltpu.VMEM, "a": pltpu.HBM}
    single = not isinstance(out_shape, (tuple, list))
    outs = [out_shape] if single else out_shape
    out = tuple(pl.BlockSpec(memory_space=spaces[k]) for k in out_space * (len(outs) if len(out_space) == 1 else 1))
    return pl.pallas_call(
        body,
        out_shape=out_shape,
        in_specs=[pl.BlockSpec(memory_space=spaces[k]) for k in in_spaces],
        out_specs=out[0] if single else out,
        scratch_shapes=list(scratch),
        compiler_params=params(),
        cost_estimate=pl.CostEstimate(flops=flops, bytes_accessed=moved, transcendentals=0),
    )


def keys_values_body(stored, n_z, n_y, pos_ref, ids_ref, x_ref, wk_ref, wv_ref, wo_ref, wq_ref, out_ref, pair_ref, w_ref, kv_ref, sem):
    def moved(block):
        return [
            pltpu.make_async_copy(block((y * n_z + z) * DH), w_ref.at[z, y], sem.at[y * n_z + z])
            for y in range(n_y)
            for z in range(n_z)
        ]

    copies = moved(lambda at: wq_ref.at[at : at + DH, :])

    @pl.when(pos_ref[1] == 0)
    def _():
        for copy in moved(lambda at: wo_ref.at[:, at : at + DH]):
            copy.start()

    @pl.when(pos_ref[1] != 0)
    def _():
        for copy in copies:
            copy.start()

    pair = jnp.concatenate([wk_ref[...], wv_ref[...]], axis=1)
    pair_ref[...] = pair
    seg = x_ref.shape[0] // stored
    both = jnp.dot(x_ref[...], pair, preferred_element_type=F32)
    for n in range(kv_ref.shape[0]):
        kv_ref[n] = both[:, n * DH : (n + 1) * DH]
        for s in range(stored):
            rows = slice(HEAD + s * seg, HEAD + (s + 1) * seg)
            out_ref[rows, n * DH : (n + 1) * DH] = kv_ref[n, pl.ds(s, seg, stride=stored), :].astype(BF)
    for copy in copies:
        copy.wait()
    lane = lax.broadcasted_iota(jnp.int32, (HEAD, 2 * DH), 1)
    row = jnp.zeros((HEAD, 2 * DH), F32)
    for r in range(2 * ids_ref.shape[1]):
        row = jnp.where(lane == r, ids_ref[r % 2, r // 2].astype(F32), row)
    out_ref[:HEAD, :] = row.astype(BF)


def halves_body(cut, after_ref, before_ref, lo_ref, hi_ref, sem):
    copies = [
        pltpu.make_async_copy(after_ref.at[:cut], lo_ref, sem.at[0]),
        pltpu.make_async_copy(before_ref.at[cut:], hi_ref, sem.at[1]),
    ]
    for copy in copies:
        copy.start()
    for copy in copies:
        copy.wait()


def attention_body(geom, pos_ref, ids_ref, q_ref, g_ref, *refs):
    blocks, block_len, n_x, n_y, cap, stored, seg = geom
    kv_refs, (attn_ref, gq_ref, out_ref, all_ids_ref, kv_ref, stage_ref, head_ref, sem) = refs[:-8], refs[-8:]
    inv_root = 1.0 / math.sqrt(DH)
    piece = seg // n_y
    cut = HEAD + stored // 2 * seg
    my_x, my_c = pos_ref[0], pos_ref[1]
    requests = 2 * blocks
    parts = len(kv_refs) // 2

    spots = []
    for r in range(requests):
        i = ids_ref[r % 2, r // 2]
        owner, slot = i // stored, lax.rem(i, stored)
        dx = lax.rem(owner // 2 - my_x + n_x, n_x)
        dc = lax.rem(lax.rem(owner, 2) + my_c, 2)
        part = dx + jnp.where(dx == 3, 1, jnp.where((dx == 2) & (slot >= stored // 2), 1, 0))
        row = HEAD + slot * seg - jnp.where(part == 3, cut, 0)
        row = pl.multiple_of(row, HEAD)
        spots.append(owner)
        for k, ref in enumerate(kv_refs):

            @pl.when(dc * parts + part == k)
            def _(ref=ref, row=row, r=r):
                pltpu.make_async_copy(ref.at[pl.ds(row, seg), :], kv_ref.at[r], sem.at[r]).start()

    heads = [(c, d) for c in range(2) for d in range(n_x)]
    head_copies = []
    for i, (c, d) in enumerate(heads):
        ref = kv_refs[c * parts + (4 if d == 3 else d)]
        head_copies.append(pltpu.make_async_copy(ref.at[:HEAD, :DH], head_ref.at[i], sem.at[requests + i]))
        head_copies[-1].start()

    sent = []
    for r in range(requests):
        pltpu.make_async_copy(kv_refs[0].at[:seg, :], kv_ref.at[r], sem.at[r]).wait()
    for c in range(blocks):
        both = [kv_ref[r] for r in (2 * c, 2 * c + 1)]
        k = jnp.concatenate([b[:, :DH] for b in both], axis=0)
        v = jnp.concatenate([b[:, DH:] for b in both], axis=0)
        rows = slice(c * block_len, (c + 1) * block_len)
        q = q_ref[rows, :]
        g = g_ref[rows, :]
        s = lax.dot_general(q, k, NT, preferred_element_type=F32) * inv_root
        e = jnp.exp(s - jnp.max(s, axis=-1, keepdims=True))
        p = e / jnp.sum(e, axis=-1, keepdims=True)
        ph = p.astype(BF)
        gp = lax.dot_general(g, v, NT, preferred_element_type=F32)
        attn_ref[rows, :] = jnp.dot(ph, v, preferred_element_type=F32).astype(BF)
        gs = (p * (gp - jnp.sum(p * gp, axis=-1, keepdims=True))).astype(BF)
        gq_ref[rows, :] = (jnp.dot(gs, k, preferred_element_type=F32) * inv_root).astype(BF)
        gv = lax.dot_general(ph, g, TN, preferred_element_type=F32).astype(BF)
        gk = (lax.dot_general(gs, q, TN, preferred_element_type=F32) * inv_root).astype(BF)
        for j in range(2):
            r = 2 * c + j
            owner = spots[r]
            pos = sum([(spots[i] == owner).astype(jnp.int32) for i in range(r)], jnp.int32(0))
            for y in range(n_y):
                part = slice(j * seg + y * piece, j * seg + (y + 1) * piece)
                stage_ref[r, y, :, :DH] = gk[part, :]
                stage_ref[r, y, :, DH:] = gv[part, :]
            sent.append(
                pltpu.make_async_copy(stage_ref.at[r], out_ref.at[owner, :, pos], sem.at[requests + len(heads) + r])
            )
            sent[-1].start()
    for i, (c, d) in enumerate(heads):
        head_copies[i].wait()
        owner = lax.rem(my_x + d, n_x) * 2 + lax.rem(my_c + c, 2)
        all_ids_ref[pl.ds(owner, 1), :] = head_ref[i].astype(F32).astype(jnp.int32)[:1, :]
    for copy in sent:
        copy.wait()


def encoded_body(stored, pos_ref, ids_ref, ret_ref, *refs):
    owners, n_y, cap, piece, _ = ret_ref.shape
    w_refs, (out_ref, got_ref, w_ref, acc_ref, prod_ref, sem) = refs[:n_y], refs[n_y:]
    me = pos_ref[0] * 2 + pos_ref[1]
    my_y = pos_ref[2]
    for d in range(owners):
        pltpu.make_async_copy(ret_ref.at[d], got_ref.at[d], sem.at[d]).start()
    weights = [pltpu.make_async_copy(w_refs[y], w_ref.at[y], sem.at[owners + y]) for y in range(n_y)]
    for copy in weights:
        copy.start()
    acc_ref[...] = jnp.zeros_like(acc_ref)

    def from_device(d, carry):
        pltpu.make_async_copy(ret_ref.at[d], got_ref.at[d], sem.at[d]).wait()
        count = jnp.int32(0)
        for r in range(owners * 2):
            at = ids_ref[d, r]
            named = at // stored == me

            @pl.when(named)
            def _(at=at, count=count):
                slot = lax.rem(at, stored)
                for y in range(n_y):
                    acc_ref[y, slot] += got_ref[d, y, count].astype(F32)

            count = count + named.astype(jnp.int32)
        return carry

    lax.fori_loop(0, owners, from_device, 0)
    lanes = prod_ref.shape[0]
    for copy in weights:
        copy.wait()
    both = [acc_ref[lax.rem(my_y + y, n_y)].astype(BF).reshape(stored * piece, 2 * DH) for y in range(n_y)]
    both = jnp.concatenate(both, axis=1)
    for n in range(0, lanes, 2):
        wide = min(2, lanes - n)
        w = jnp.concatenate([w_ref[y, n * DH : (n + wide) * DH, :] for y in range(n_y)], axis=1)
        term = lax.dot_general(both, w, NT, preferred_element_type=F32)
        for i in range(wide):
            prod_ref[n + i] = term[:, i * DH : (i + 1) * DH]
    for t in range(0, piece, 2):
        for n in range(lanes):
            two = [prod_ref[n, pl.ds(t + k, stored, stride=piece), :] for k in range(2)]
            out_ref[pl.ds(t * stored, 2 * stored), n * DH : (n + 1) * DH] = jnp.concatenate(two, axis=0).astype(BF)


def head_sum_body(n_z, n_y, second, pos_ref, *refs):
    pieces, mine, other = refs[:n_z], refs[n_z], refs[n_z + 1]
    *outs, a_ref, w_ref, sem = refs[n_z + 2 :]
    my_c, my_y, my_z = (pos_ref[i] for i in range(1, 4))

    @pl.when(my_c == second)
    def _():
        pltpu.make_async_copy(mine, w_ref, sem.at[n_z]).start()

    @pl.when(my_c != second)
    def _():
        pltpu.make_async_copy(other, w_ref, sem.at[n_z]).start()

    copies = [
        pltpu.make_async_copy(pieces[j], a_ref.at[:, j * DH : (j + 1) * DH], sem.at[j]) for j in range(n_z)
    ]
    for copy in copies:
        copy.start()
    pltpu.make_async_copy(mine, w_ref, sem.at[n_z]).wait()
    for copy in copies:
        copy.wait()
    heads = [lax.rem(my_z + j, n_z) for j in range(n_z)]
    for k in range(0, n_y, 2):
        at = [lax.rem(my_y + k + i, n_y) for i in range(2)]
        if second:
            w = [jnp.concatenate([w_ref[h, at[i]] for h in heads], axis=1) for i in range(2)]
            total = lax.dot_general(a_ref[...], jnp.concatenate(w, axis=0), NT, preferred_element_type=F32)
        else:
            w = [jnp.concatenate([w_ref[h, at[i]] for h in heads], axis=0) for i in range(2)]
            total = jnp.dot(a_ref[...], jnp.concatenate(w, axis=1), preferred_element_type=F32)
        for i in range(2):
            outs[k + i][...] = total[:, i * DH : (i + 1) * DH].astype(outs[k + i].dtype)


def shards(hidden, encoded, neighbours, w_query, w_key, w_value, w_out, cotangent):
    n_x, n_c, n_y, n_z = (lax.axis_size(a) for a in ("x", "c", "y", "z"))
    dp = ("x", "c")
    owners = n_x * n_c
    rows, width = hidden.shape
    blocks, per_block = neighbours.shape
    cap = blocks * per_block // 4
    stored = encoded.shape[0]
    enc_width = w_key.shape[0]
    seg = encoded.shape[1] // enc_width
    block_len = rows // blocks
    piece = seg // n_y
    ids = neighbours.T
    place = jnp.stack([lax.axis_index(a) for a in ("x", "c", "y", "z")]).astype(jnp.int32)

    def shift(axis, n, k):
        return lambda a: lax.ppermute(a, axis, [(i, (i + k) % n) for i in range(n)])

    swap = shift("c", n_c, 1)
    x_up, x_down = shift("x", n_x, -1), shift("x", n_x, 1)
    z_up, z_down = shift("z", n_z, -1), shift("z", n_z, 1)
    tie = lax.optimization_barrier

    enc_rows = encoded.reshape(stored, seg, enc_width).transpose(1, 0, 2).reshape(seg * stored, enc_width)
    kv, pair, mine = call(
        functools.partial(keys_values_body, stored, n_z, n_y),
        (
            jax.ShapeDtypeStruct((HEAD + stored * seg, 2 * DH), BF),
            jax.ShapeDtypeStruct((enc_width, 2 * DH), BF),
            jax.ShapeDtypeStruct((n_z, n_y, DH, DH), BF),
        ),
        "ssvvvaa", 470_000_000, 5 << 20,
        scratch=(pltpu.VMEM((2, seg * stored, DH), F32), pltpu.SemaphoreType.DMA((n_z * n_y,))),
    )(place, ids, enc_rows, w_key, w_value, w_out, w_query)
    after, before, kv_other = x_up(kv), x_down(kv), swap(kv)
    mine = lax.all_to_all(mine, "z", 0, 0, tiled=True)
    y_up, y_down = shift("y", n_y, -1), shift("y", n_y, 1)
    pair_up, pair_down = y_up(pair), y_down(pair)
    queries = jnp.dot(hidden, w_query, preferred_element_type=F32).astype(BF)
    grad_attn = lax.dot_general(cotangent, w_out, NT, preferred_element_type=F32).astype(BF)
    after, before, pair_up, pair_down, queries, grad_attn = tie(
        (after, before, pair_up, pair_down, queries, grad_attn)
    )

    cut = HEAD + stored // 2 * seg
    next_lo, next_hi = call(
        functools.partial(halves_body, cut),
        (jax.ShapeDtypeStruct((cut, 2 * DH), BF), jax.ShapeDtypeStruct((kv.shape[0] - cut, 2 * DH), BF)),
        "aa", 0, 0, scratch=(pltpu.SemaphoreType.DMA((2,)),),
    )(after, before)
    far_lo, far_hi = x_up(next_lo), x_down(next_hi)
    kv_all = [kv, after, far_lo, far_hi, before, kv_other] + [swap(a) for a in (after, far_lo, far_hi, before)]
    pairs = [pair, pair_up, y_up(pair_up), pair_down]

    queries, pairs = tie((queries, pairs))
    other = swap(mine)

    slab = jax.ShapeDtypeStruct((rows, DH), BF)
    attn, gq, outgoing, ids_all = call(
        functools.partial(attention_body, (blocks, block_len, n_x, n_y, cap, stored, seg)),
        (
            slab,
            slab,
            jax.ShapeDtypeStruct((owners, n_y, cap, piece, 2 * DH), BF),
            jax.ShapeDtypeStruct((owners, DH), jnp.int32),
        ),
        "ssvv" + "a" * len(kv_all), 0, 0,
        scratch=(
            pltpu.VMEM((blocks * per_block, seg, 2 * DH), BF),
            pltpu.VMEM((blocks * per_block, n_y, piece, 2 * DH), BF),
            pltpu.VMEM((owners, HEAD, DH), BF),
            pltpu.SemaphoreType.DMA((2 * blocks * per_block + owners,)),
        ),
        out_space="vvav",
    )(place, ids, queries, grad_attn, *kv_all)

    def ring(own):
        pieces = {0: own}
        for k in range(1, n_z // 2 + 1):
            pieces[k] = z_up(pieces[k - 1])
        last = own
        for k in range(1, n_z - n_z // 2):
            last = z_down(last)
            pieces[n_z - k] = last
        return [pieces[k] for k in range(n_z)]

    returned = lax.all_to_all(
        outgoing.reshape(owners * n_y, cap, piece, 2 * DH), dp + ("y",), 0, 0, tiled=True
    ).reshape(owners, n_y, cap, piece, 2 * DH)
    attn_all, gq_all = ring(attn), ring(gq)
    last = n_z // 2
    early = [a for ring_ in (attn_all, gq_all) for k, a in enumerate(ring_) if k != last]
    _, returned = tie((early, returned))
    enc_part = call(
        functools.partial(encoded_body, stored),
        jax.ShapeDtypeStruct((piece * stored, enc_width), BF), "ssa" + "a" * n_y, 500_000_000, 5 << 20,
        scratch=(
            pltpu.VMEM((owners, n_y, cap, piece, 2 * DH), BF),
            pltpu.VMEM((n_y, enc_width, 2 * DH), BF),
            pltpu.VMEM((n_y, stored, piece, 2 * DH), F32),
            pltpu.VMEM((enc_width // DH, stored * piece, DH), F32),
            pltpu.SemaphoreType.DMA((owners + n_y,)),
        ),
    )(place, ids_all, returned, *pairs)
    attn_all, gq_all, enc_part = tie((attn_all, gq_all, enc_part))
    enc_parts = lax.all_to_all(enc_part.reshape(n_z, -1, enc_width), "z", 0, 0, tiled=True)
    enc_rows_sum = jnp.sum(enc_parts.astype(F32), axis=0).astype(BF)
    grad_encoded = enc_rows_sum.reshape(seg // (n_y * n_z), stored, enc_width).transpose(1, 0, 2).reshape(stored, -1)

    def summed(pieces, second):
        parts = call(
            functools.partial(head_sum_body, n_z, n_y, second),
            (jax.ShapeDtypeStruct((rows, DH), F32),) + (slab,) * (n_y - 1),
            "s" + "a" * (n_z + 2), 540_000_000, 3 << 20,
            scratch=(
                pltpu.VMEM((rows, n_z * DH), BF),
                pltpu.VMEM((n_z, n_y, DH, DH), BF),
                pltpu.SemaphoreType.DMA((n_z + 1,)),
            ),
        )(place, *pieces, mine, other)
        total = parts[0]
        for k in range(1, n_y):
            total = total + shift("y", n_y, k)(parts[k]).astype(F32)
        return total.astype(BF)

    return summed(attn_all, 0), summed(gq_all, 1), grad_encoded


def solution(mesh):
    n_y = 4
    dp, mp = mesh.shape["dp"], mesh.shape["mp"]
    split = Mesh(mesh.devices.reshape(dp // 2, 2, n_y, mp // n_y), ("x", "c", "y", "z"))
    d, m = ("x", "c"), ("y", "z")
    return jax.shard_map(
        shards,
        mesh=split,
        in_specs=(P(d, None), P(d, None), P(d, None), P(None, m), P(None, m), P(None, m), P(m, None), P(d, None)),
        out_specs=(P(d, m), P(d, m), P(d, m)),
        check_vma=False,
    )
```

```python
import functools
import math

import jax
import jax.numpy as jnp
from jax import lax
from jax.experimental import pallas as pl
from jax.experimental.pallas import tpu as pltpu
from jax.sharding import Mesh, PartitionSpec as P

DH = 128
BF = jnp.bfloat16
F32 = jnp.float32
NT = (((1,), (1,)), ((), ()))
TN = (((0,), (0,)), ((), ()))
HEAD = 16
VMEM_LIMIT = 63 * 1024 * 1024


def params():
    return pltpu.CompilerParams(vmem_limit_bytes=VMEM_LIMIT)


def call(body, out_shape, in_spaces, flops, moved, scratch=(), out_space="v"):
    spaces = {"s": pltpu.SMEM, "v": pltpu.VMEM, "a": pltpu.HBM}
    single = not isinstance(out_shape, (tuple, list))
    outs = [out_shape] if single else out_shape
    out = tuple(pl.BlockSpec(memory_space=spaces[k]) for k in out_space * (len(outs) if len(out_space) == 1 else 1))
    return pl.pallas_call(
        body,
        out_shape=out_shape,
        in_specs=[pl.BlockSpec(memory_space=spaces[k]) for k in in_spaces],
        out_specs=out[0] if single else out,
        scratch_shapes=list(scratch),
        compiler_params=params(),
        cost_estimate=pl.CostEstimate(flops=flops, bytes_accessed=moved, transcendentals=0),
    )


def keys_values_body(stored, n_z, n_y, pos_ref, ids_ref, x_ref, wk_ref, wv_ref, wo_ref, wq_ref, out_ref, pair_ref, w_ref, kv_ref, sem):
    def moved(block):
        return [
            pltpu.make_async_copy(block((y * n_z + z) * DH), w_ref.at[z, y], sem.at[y * n_z + z])
            for y in range(n_y)
            for z in range(n_z)
        ]

    copies = moved(lambda at: wq_ref.at[at : at + DH, :])

    @pl.when(pos_ref[1] == 0)
    def _():
        for copy in moved(lambda at: wo_ref.at[:, at : at + DH]):
            copy.start()

    @pl.when(pos_ref[1] != 0)
    def _():
        for copy in copies:
            copy.start()

    pair = jnp.concatenate([wk_ref[...], wv_ref[...]], axis=1)
    pair_ref[...] = pair
    seg = x_ref.shape[0] // stored
    both = jnp.dot(x_ref[...], pair, preferred_element_type=F32)
    for n in range(kv_ref.shape[0]):
        kv_ref[n] = both[:, n * DH : (n + 1) * DH]
        for s in range(stored):
            rows = slice(HEAD + s * seg, HEAD + (s + 1) * seg)
            out_ref[rows, n * DH : (n + 1) * DH] = kv_ref[n, pl.ds(s, seg, stride=stored), :].astype(BF)
    for copy in copies:
        copy.wait()
    lane = lax.broadcasted_iota(jnp.int32, (HEAD, 2 * DH), 1)
    row = jnp.zeros((HEAD, 2 * DH), F32)
    for r in range(2 * ids_ref.shape[1]):
        row = jnp.where(lane == r, ids_ref[r % 2, r // 2].astype(F32), row)
    out_ref[:HEAD, :] = row.astype(BF)


def halves_body(cut, after_ref, before_ref, lo_ref, hi_ref, sem):
    copies = [
        pltpu.make_async_copy(after_ref.at[:cut], lo_ref, sem.at[0]),
        pltpu.make_async_copy(before_ref.at[cut:], hi_ref, sem.at[1]),
    ]
    for copy in copies:
        copy.start()
    for copy in copies:
        copy.wait()


def attention_body(geom, pos_ref, ids_ref, q_ref, g_ref, *refs):
    blocks, block_len, n_x, n_y, cap, stored, seg = geom
    kv_refs, (attn_ref, gq_ref, out_ref, all_ids_ref, kv_ref, stage_ref, head_ref, sem) = refs[:-8], refs[-8:]
    inv_root = 1.0 / math.sqrt(DH)
    piece = seg // n_y
    cut = HEAD + stored // 2 * seg
    my_x, my_c = pos_ref[0], pos_ref[1]
    requests = 2 * blocks
    parts = len(kv_refs) // 2

    spots = []
    for r in range(requests):
        i = ids_ref[r % 2, r // 2]
        owner, slot = i // stored, lax.rem(i, stored)
        dx = lax.rem(owner // 2 - my_x + n_x, n_x)
        dc = lax.rem(lax.rem(owner, 2) + my_c, 2)
        part = dx + jnp.where(dx == 3, 1, jnp.where((dx == 2) & (slot >= stored // 2), 1, 0))
        row = HEAD + slot * seg - jnp.where(part == 3, cut, 0)
        row = pl.multiple_of(row, HEAD)
        spots.append(owner)
        for k, ref in enumerate(kv_refs):

            @pl.when(dc * parts + part == k)
            def _(ref=ref, row=row, r=r):
                pltpu.make_async_copy(ref.at[pl.ds(row, seg), :], kv_ref.at[r], sem.at[r]).start()

    heads = [(c, d) for c in range(2) for d in range(n_x)]
    head_copies = []
    for i, (c, d) in enumerate(heads):
        ref = kv_refs[c * parts + (4 if d == 3 else d)]
        head_copies.append(pltpu.make_async_copy(ref.at[:HEAD, :DH], head_ref.at[i], sem.at[requests + i]))
        head_copies[-1].start()

    sent = []
    for r in range(requests):
        pltpu.make_async_copy(kv_refs[0].at[:seg, :], kv_ref.at[r], sem.at[r]).wait()
    for c in range(blocks):
        both = [kv_ref[r] for r in (2 * c, 2 * c + 1)]
        k = jnp.concatenate([b[:, :DH] for b in both], axis=0)
        v = jnp.concatenate([b[:, DH:] for b in both], axis=0)
        rows = slice(c * block_len, (c + 1) * block_len)
        q = q_ref[rows, :]
        g = g_ref[rows, :]
        s = lax.dot_general(q, k, NT, preferred_element_type=F32) * inv_root
        e = jnp.exp(s - jnp.max(s, axis=-1, keepdims=True))
        p = e / jnp.sum(e, axis=-1, keepdims=True)
        ph = p.astype(BF)
        gp = lax.dot_general(g, v, NT, preferred_element_type=F32)
        attn_ref[rows, :] = jnp.dot(ph, v, preferred_element_type=F32).astype(BF)
        gs = (p * (gp - jnp.sum(p * gp, axis=-1, keepdims=True))).astype(BF)
        gq_ref[rows, :] = (jnp.dot(gs, k, preferred_element_type=F32) * inv_root).astype(BF)
        gv = lax.dot_general(ph, g, TN, preferred_element_type=F32).astype(BF)
        gk = (lax.dot_general(gs, q, TN, preferred_element_type=F32) * inv_root).astype(BF)
        for j in range(2):
            r = 2 * c + j
            owner = spots[r]
            pos = sum([(spots[i] == owner).astype(jnp.int32) for i in range(r)], jnp.int32(0))
            for y in range(n_y):
                part = slice(j * seg + y * piece, j * seg + (y + 1) * piece)
                stage_ref[r, y, :, :DH] = gk[part, :]
                stage_ref[r, y, :, DH:] = gv[part, :]
            sent.append(
                pltpu.make_async_copy(stage_ref.at[r], out_ref.at[owner, :, pos], sem.at[requests + len(heads) + r])
            )
            sent[-1].start()
    for i, (c, d) in enumerate(heads):
        head_copies[i].wait()
        owner = lax.rem(my_x + d, n_x) * 2 + lax.rem(my_c + c, 2)
        all_ids_ref[pl.ds(owner, 1), :] = head_ref[i].astype(F32).astype(jnp.int32)[:1, :]
    for copy in sent:
        copy.wait()


def tail_body(stored, n_z, pos_ref, ids_ref, ret_ref, *refs):
    owners, n_y, cap, piece, _ = ret_ref.shape
    pair_refs, refs = refs[:n_y], refs[n_y:]
    piece_refs, (mine, other), refs = refs[: 2 * n_z], refs[2 * n_z : 2 * n_z + 2], refs[2 * n_z + 2 :]
    out_ref, sums, refs = refs[0], refs[1 : 1 + 2 * n_y], refs[1 + 2 * n_y :]
    got_ref, pair_ref, acc_ref, prod_ref, a_ref, w_ref, sem = refs
    my_c, my_y, my_z = (pos_ref[i] for i in range(1, 4))
    me = pos_ref[0] * 2 + my_c

    for d in range(owners):
        pltpu.make_async_copy(ret_ref.at[d], got_ref.at[d], sem.at[d]).start()
    first = owners
    pair_copies = [pltpu.make_async_copy(pair_refs[y], pair_ref.at[y], sem.at[first + y]) for y in range(n_y)]
    first += n_y
    piece_copies = [
        pltpu.make_async_copy(
            piece_refs[k], a_ref.at[k // n_z, :, (k % n_z) * DH : (k % n_z + 1) * DH], sem.at[first + k]
        )
        for k in range(2 * n_z)
    ]
    first += 2 * n_z
    weight_copies = [
        pltpu.make_async_copy(mine, w_ref.at[my_c], sem.at[first]),
        pltpu.make_async_copy(other, w_ref.at[1 - my_c], sem.at[first + 1]),
    ]
    for copy in pair_copies + piece_copies + weight_copies:
        copy.start()

    acc_ref[...] = jnp.zeros_like(acc_ref)

    def from_device(d, carry):
        pltpu.make_async_copy(ret_ref.at[d], got_ref.at[d], sem.at[d]).wait()
        count = jnp.int32(0)
        for r in range(owners * 2):
            at = ids_ref[d, r]
            named = at // stored == me

            @pl.when(named)
            def _(at=at, count=count):
                slot = lax.rem(at, stored)
                for y in range(n_y):
                    acc_ref[y, slot] += got_ref[d, y, count].astype(F32)

            count = count + named.astype(jnp.int32)
        return carry

    lax.fori_loop(0, owners, from_device, 0)
    for copy in pair_copies + piece_copies + weight_copies:
        copy.wait()
    lanes = prod_ref.shape[0]
    both = [acc_ref[lax.rem(my_y + y, n_y)].astype(BF).reshape(stored * piece, 2 * DH) for y in range(n_y)]
    both = jnp.concatenate(both, axis=1)
    for n in range(0, lanes, 2):
        wide = min(2, lanes - n)
        w = jnp.concatenate([pair_ref[y, n * DH : (n + wide) * DH, :] for y in range(n_y)], axis=1)
        term = lax.dot_general(both, w, NT, preferred_element_type=F32)
        for i in range(wide):
            prod_ref[n + i] = term[:, i * DH : (i + 1) * DH]
    for t in range(0, piece, 2):
        for n in range(lanes):
            two = [prod_ref[n, pl.ds(t + k, stored, stride=piece), :] for k in range(2)]
            out_ref[pl.ds(t * stored, 2 * stored), n * DH : (n + 1) * DH] = jnp.concatenate(two, axis=0).astype(BF)

    heads = [lax.rem(my_z + j, n_z) for j in range(n_z)]
    for second in range(2):
        for k in range(0, n_y, 2):
            at = [lax.rem(my_y + k + i, n_y) for i in range(2)]
            if second:
                w = [jnp.concatenate([w_ref[1, h, at[i]] for h in heads], axis=1) for i in range(2)]
                total = lax.dot_general(a_ref[1], jnp.concatenate(w, axis=0), NT, preferred_element_type=F32)
            else:
                w = [jnp.concatenate([w_ref[0, h, at[i]] for h in heads], axis=0) for i in range(2)]
                total = jnp.dot(a_ref[0], jnp.concatenate(w, axis=1), preferred_element_type=F32)
            for i in range(2):
                ref = sums[second * n_y + k + i]
                ref[...] = total[:, i * DH : (i + 1) * DH].astype(ref.dtype)


def shards(hidden, encoded, neighbours, w_query, w_key, w_value, w_out, cotangent):
    n_x, n_c, n_y, n_z = (lax.axis_size(a) for a in ("x", "c", "y", "z"))
    dp = ("x", "c")
    owners = n_x * n_c
    rows, width = hidden.shape
    blocks, per_block = neighbours.shape
    cap = blocks * per_block // 4
    stored = encoded.shape[0]
    enc_width = w_key.shape[0]
    seg = encoded.shape[1] // enc_width
    block_len = rows // blocks
    piece = seg // n_y
    ids = neighbours.T
    place = jnp.stack([lax.axis_index(a) for a in ("x", "c", "y", "z")]).astype(jnp.int32)

    def shift(axis, n, k):
        return lambda a: lax.ppermute(a, axis, [(i, (i + k) % n) for i in range(n)])

    swap = shift("c", n_c, 1)
    x_up, x_down = shift("x", n_x, -1), shift("x", n_x, 1)
    z_up, z_down = shift("z", n_z, -1), shift("z", n_z, 1)
    tie = lax.optimization_barrier

    enc_rows = encoded.reshape(stored, seg, enc_width).transpose(1, 0, 2).reshape(seg * stored, enc_width)
    kv, pair, mine = call(
        functools.partial(keys_values_body, stored, n_z, n_y),
        (
            jax.ShapeDtypeStruct((HEAD + stored * seg, 2 * DH), BF),
            jax.ShapeDtypeStruct((enc_width, 2 * DH), BF),
            jax.ShapeDtypeStruct((n_z, n_y, DH, DH), BF),
        ),
        "ssvvvaa", 470_000_000, 5 << 20,
        scratch=(pltpu.VMEM((2, seg * stored, DH), F32), pltpu.SemaphoreType.DMA((n_z * n_y,))),
    )(place, ids, enc_rows, w_key, w_value, w_out, w_query)
    after, before, kv_other = x_up(kv), x_down(kv), swap(kv)
    mine = lax.all_to_all(mine, "z", 0, 0, tiled=True)
    y_up, y_down = shift("y", n_y, -1), shift("y", n_y, 1)
    queries = jnp.dot(hidden, w_query, preferred_element_type=F32).astype(BF)
    grad_attn = lax.dot_general(cotangent, w_out, NT, preferred_element_type=F32).astype(BF)
    pair_, queries = tie((pair, queries))
    pair_up, pair_down = y_up(pair_), y_down(pair_)
    after, before, queries, grad_attn = tie((after, before, queries, grad_attn))

    cut = HEAD + stored // 2 * seg
    next_lo, next_hi = call(
        functools.partial(halves_body, cut),
        (jax.ShapeDtypeStruct((cut, 2 * DH), BF), jax.ShapeDtypeStruct((kv.shape[0] - cut, 2 * DH), BF)),
        "aa", 0, 0, scratch=(pltpu.SemaphoreType.DMA((2,)),),
    )(after, before)
    next_lo, next_hi, pair_up, pair_down = tie((next_lo, next_hi, pair_up, pair_down))
    far_lo, far_hi = x_up(next_lo), x_down(next_hi)
    kv_all = [kv, after, far_lo, far_hi, before, kv_other] + [swap(a) for a in (after, far_lo, far_hi, before)]
    pairs = [pair, pair_up, y_up(pair_up), pair_down]

    queries, pairs = tie((queries, pairs))
    other = swap(mine)

    slab = jax.ShapeDtypeStruct((rows, DH), BF)
    attn, gq, outgoing, ids_all = call(
        functools.partial(attention_body, (blocks, block_len, n_x, n_y, cap, stored, seg)),
        (
            slab,
            slab,
            jax.ShapeDtypeStruct((owners, n_y, cap, piece, 2 * DH), BF),
            jax.ShapeDtypeStruct((owners, DH), jnp.int32),
        ),
        "ssvv" + "a" * len(kv_all), 0, 0,
        scratch=(
            pltpu.VMEM((blocks * per_block, seg, 2 * DH), BF),
            pltpu.VMEM((blocks * per_block, n_y, piece, 2 * DH), BF),
            pltpu.VMEM((owners, HEAD, DH), BF),
            pltpu.SemaphoreType.DMA((2 * blocks * per_block + owners,)),
        ),
        out_space="vvav",
    )(place, ids, queries, grad_attn, *kv_all)

    def ring(own):
        pieces = {0: own}
        for k in range(1, n_z // 2 + 1):
            pieces[k] = z_up(pieces[k - 1])
        last = own
        for k in range(1, n_z - n_z // 2):
            last = z_down(last)
            pieces[n_z - k] = last
        return [pieces[k] for k in range(n_z)]

    returned = lax.all_to_all(
        outgoing.reshape(owners * n_y, cap, piece, 2 * DH), dp + ("y",), 0, 0, tiled=True
    ).reshape(owners, n_y, cap, piece, 2 * DH)
    attn_all, gq_all = ring(attn), ring(gq)
    sums = (jax.ShapeDtypeStruct((rows, DH), F32),) + (slab,) * (n_y - 1)
    enc_part, *sums = call(
        functools.partial(tail_body, stored, n_z),
        (jax.ShapeDtypeStruct((piece * stored, enc_width), BF),) + sums + sums,
        "ssa" + "a" * (n_y + 2 * n_z + 2), 1_580_000_000, 10 << 20,
        scratch=(
            pltpu.VMEM((owners, n_y, cap, piece, 2 * DH), BF),
            pltpu.VMEM((n_y, enc_width, 2 * DH), BF),
            pltpu.VMEM((n_y, stored, piece, 2 * DH), F32),
            pltpu.VMEM((enc_width // DH, stored * piece, DH), F32),
            pltpu.VMEM((2, rows, n_z * DH), BF),
            pltpu.VMEM((2, n_z, n_y, DH, DH), BF),
            pltpu.SemaphoreType.DMA((owners + n_y + 2 * n_z + 2,)),
        ),
    )(place, ids_all, returned, *pairs, *attn_all, *gq_all, mine, other)
    enc_parts = lax.all_to_all(enc_part.reshape(n_z, -1, enc_width), "z", 0, 0, tiled=True)
    enc_rows_sum = jnp.sum(enc_parts.astype(F32), axis=0).astype(BF)
    grad_encoded = enc_rows_sum.reshape(seg // (n_y * n_z), stored, enc_width).transpose(1, 0, 2).reshape(stored, -1)

    def summed(parts):
        total = parts[0]
        for k in range(1, n_y):
            total = total + shift("y", n_y, k)(parts[k]).astype(F32)
        return total.astype(BF)

    return summed(sums[:n_y]), summed(sums[n_y:]), grad_encoded


def solution(mesh):
    n_y = 4
    dp, mp = mesh.shape["dp"], mesh.shape["mp"]
    split = Mesh(mesh.devices.reshape(dp // 2, 2, n_y, mp // n_y), ("x", "c", "y", "z"))
    d, m = ("x", "c"), ("y", "z")
    return jax.shard_map(
        shards,
        mesh=split,
        in_specs=(P(d, None), P(d, None), P(d, None), P(None, m), P(None, m), P(None, m), P(m, None), P(d, None)),
        out_specs=(P(d, m), P(d, m), P(d, m)),
        check_vma=False,
    )
```

```python
import functools
import math

import jax
import jax.numpy as jnp
from jax import lax
from jax.experimental import pallas as pl
from jax.experimental.pallas import tpu as pltpu
from jax.sharding import Mesh, PartitionSpec as P

DH = 128
BF = jnp.bfloat16
F32 = jnp.float32
NT = (((1,), (1,)), ((), ()))
TN = (((0,), (0,)), ((), ()))
HEAD = 16
VMEM_LIMIT = 63 * 1024 * 1024


def params():
    return pltpu.CompilerParams(vmem_limit_bytes=VMEM_LIMIT)


def call(body, out_shape, in_spaces, flops, moved, scratch=(), out_space="v"):
    spaces = {"s": pltpu.SMEM, "v": pltpu.VMEM, "a": pltpu.HBM}
    single = not isinstance(out_shape, (tuple, list))
    outs = [out_shape] if single else out_shape
    out = tuple(pl.BlockSpec(memory_space=spaces[k]) for k in out_space * (len(outs) if len(out_space) == 1 else 1))
    return pl.pallas_call(
        body,
        out_shape=out_shape,
        in_specs=[pl.BlockSpec(memory_space=spaces[k]) for k in in_spaces],
        out_specs=out[0] if single else out,
        scratch_shapes=list(scratch),
        compiler_params=params(),
        cost_estimate=pl.CostEstimate(flops=flops, bytes_accessed=moved, transcendentals=0),
    )


def keys_values_body(stored, n_z, n_y, pos_ref, ids_ref, x_ref, wk_ref, wv_ref, wo_ref, wq_ref, out_ref, pair_ref, w_ref, kv_ref, sem):
    def moved(block):
        return [
            pltpu.make_async_copy(block((y * n_z + z) * DH), w_ref.at[z, y], sem.at[y * n_z + z])
            for y in range(n_y)
            for z in range(n_z)
        ]

    copies = moved(lambda at: wq_ref.at[at : at + DH, :])

    @pl.when(pos_ref[1] == 0)
    def _():
        for copy in moved(lambda at: wo_ref.at[:, at : at + DH]):
            copy.start()

    @pl.when(pos_ref[1] != 0)
    def _():
        for copy in copies:
            copy.start()

    pair = jnp.concatenate([wk_ref[...], wv_ref[...]], axis=1)
    pair_ref[...] = pair
    seg = x_ref.shape[0] // stored
    both = jnp.dot(x_ref[...], pair, preferred_element_type=F32)
    for n in range(kv_ref.shape[0]):
        kv_ref[n] = both[:, n * DH : (n + 1) * DH]
        for s in range(stored):
            rows = slice(HEAD + s * seg, HEAD + (s + 1) * seg)
            out_ref[rows, n * DH : (n + 1) * DH] = kv_ref[n, pl.ds(s, seg, stride=stored), :].astype(BF)
    for copy in copies:
        copy.wait()
    lane = lax.broadcasted_iota(jnp.int32, (HEAD, 2 * DH), 1)
    row = jnp.zeros((HEAD, 2 * DH), F32)
    for r in range(2 * ids_ref.shape[1]):
        row = jnp.where(lane == r, ids_ref[r % 2, r // 2].astype(F32), row)
    out_ref[:HEAD, :] = row.astype(BF)


def halves_body(cut, after_ref, before_ref, lo_ref, hi_ref, sem):
    copies = [
        pltpu.make_async_copy(after_ref.at[:cut], lo_ref, sem.at[0]),
        pltpu.make_async_copy(before_ref.at[cut:], hi_ref, sem.at[1]),
    ]
    for copy in copies:
        copy.start()
    for copy in copies:
        copy.wait()


def attention_body(geom, pos_ref, ids_ref, q_ref, g_ref, *refs):
    blocks, block_len, n_x, n_y, cap, stored, seg = geom
    kv_refs, (attn_ref, gq_ref, out_ref, all_ids_ref, kv_ref, stage_ref, head_ref, sem) = refs[:-8], refs[-8:]
    inv_root = 1.0 / math.sqrt(DH)
    piece = seg // n_y
    cut = HEAD + stored // 2 * seg
    my_x, my_c = pos_ref[0], pos_ref[1]
    requests = 2 * blocks
    parts = len(kv_refs) // 2

    spots = []
    for r in range(requests):
        i = ids_ref[r % 2, r // 2]
        owner, slot = i // stored, lax.rem(i, stored)
        dx = lax.rem(owner // 2 - my_x + n_x, n_x)
        dc = lax.rem(lax.rem(owner, 2) + my_c, 2)
        part = dx + jnp.where(dx == 3, 1, jnp.where((dx == 2) & (slot >= stored // 2), 1, 0))
        row = HEAD + slot * seg - jnp.where(part == 3, cut, 0)
        row = pl.multiple_of(row, HEAD)
        spots.append(owner)
        for k, ref in enumerate(kv_refs):

            @pl.when(dc * parts + part == k)
            def _(ref=ref, row=row, r=r):
                pltpu.make_async_copy(ref.at[pl.ds(row, seg), :], kv_ref.at[r], sem.at[r]).start()

    heads = [(c, d) for c in range(2) for d in range(n_x)]
    head_copies = []
    for i, (c, d) in enumerate(heads):
        ref = kv_refs[c * parts + (4 if d == 3 else d)]
        head_copies.append(pltpu.make_async_copy(ref.at[:HEAD, :DH], head_ref.at[i], sem.at[requests + i]))
        head_copies[-1].start()

    sent = []
    for r in range(requests):
        pltpu.make_async_copy(kv_refs[0].at[:seg, :], kv_ref.at[r], sem.at[r]).wait()
    for c in range(blocks):
        both = [kv_ref[r] for r in (2 * c, 2 * c + 1)]
        k = jnp.concatenate([b[:, :DH] for b in both], axis=0)
        v = jnp.concatenate([b[:, DH:] for b in both], axis=0)
        rows = slice(c * block_len, (c + 1) * block_len)
        q = q_ref[rows, :]
        g = g_ref[rows, :]
        s = lax.dot_general(q, k, NT, preferred_element_type=F32) * inv_root
        e = jnp.exp(s - jnp.max(s, axis=-1, keepdims=True))
        p = e / jnp.sum(e, axis=-1, keepdims=True)
        ph = p.astype(BF)
        gp = lax.dot_general(g, v, NT, preferred_element_type=F32)
        attn_ref[rows, :] = jnp.dot(ph, v, preferred_element_type=F32).astype(BF)
        gs = (p * (gp - jnp.sum(p * gp, axis=-1, keepdims=True))).astype(BF)
        gq_ref[rows, :] = (jnp.dot(gs, k, preferred_element_type=F32) * inv_root).astype(BF)
        gv = lax.dot_general(ph, g, TN, preferred_element_type=F32).astype(BF)
        gk = (lax.dot_general(gs, q, TN, preferred_element_type=F32) * inv_root).astype(BF)
        for j in range(2):
            r = 2 * c + j
            owner = spots[r]
            pos = sum([(spots[i] == owner).astype(jnp.int32) for i in range(r)], jnp.int32(0))
            for y in range(n_y):
                part = slice(j * seg + y * piece, j * seg + (y + 1) * piece)
                stage_ref[r, y, :, :DH] = gk[part, :]
                stage_ref[r, y, :, DH:] = gv[part, :]
            sent.append(
                pltpu.make_async_copy(stage_ref.at[r], out_ref.at[owner, :, pos], sem.at[requests + len(heads) + r])
            )
            sent[-1].start()
    for i, (c, d) in enumerate(heads):
        head_copies[i].wait()
        owner = lax.rem(my_x + d, n_x) * 2 + lax.rem(my_c + c, 2)
        all_ids_ref[pl.ds(owner, 1), :] = head_ref[i].astype(F32).astype(jnp.int32)[:1, :]
    for copy in sent:
        copy.wait()


def tail_body(stored, n_z, pos_ref, ids_ref, ret_ref, *refs):
    owners, n_y, cap, piece, _ = ret_ref.shape
    pair_refs, refs = refs[:n_y], refs[n_y:]
    piece_refs, (mine, other), refs = refs[: 2 * n_z], refs[2 * n_z : 2 * n_z + 2], refs[2 * n_z + 2 :]
    out_ref, sums, refs = refs[0], refs[1 : 1 + 2 * n_y], refs[1 + 2 * n_y :]
    got_ref, pair_ref, acc_ref, prod_ref, a_ref, w_ref, sem = refs
    my_c, my_y, my_z = (pos_ref[i] for i in range(1, 4))
    me = pos_ref[0] * 2 + my_c

    for d in range(owners):
        pltpu.make_async_copy(ret_ref.at[d], got_ref.at[d], sem.at[d]).start()
    first = owners
    to = (0, 1 + 2 * my_c, 2, 3 - 2 * my_c)
    pair_copies = [pltpu.make_async_copy(pair_refs[y], pair_ref.at[to[y]], sem.at[first + y]) for y in range(n_y)]
    first += n_y
    piece_copies = [
        pltpu.make_async_copy(
            piece_refs[k], a_ref.at[k // n_z, :, (k % n_z) * DH : (k % n_z + 1) * DH], sem.at[first + k]
        )
        for k in range(2 * n_z)
    ]
    first += 2 * n_z
    weight_copies = [
        pltpu.make_async_copy(mine, w_ref.at[my_c], sem.at[first]),
        pltpu.make_async_copy(other, w_ref.at[1 - my_c], sem.at[first + 1]),
    ]
    for copy in pair_copies + piece_copies + weight_copies:
        copy.start()

    acc_ref[...] = jnp.zeros_like(acc_ref)

    def from_device(d, carry):
        pltpu.make_async_copy(ret_ref.at[d], got_ref.at[d], sem.at[d]).wait()
        count = jnp.int32(0)
        for r in range(owners * 2):
            at = ids_ref[d, r]
            named = at // stored == me

            @pl.when(named)
            def _(at=at, count=count):
                slot = lax.rem(at, stored)
                for y in range(n_y):
                    acc_ref[y, slot] += got_ref[d, y, count].astype(F32)

            count = count + named.astype(jnp.int32)
        return carry

    lax.fori_loop(0, owners, from_device, 0)
    for copy in pair_copies + piece_copies + weight_copies:
        copy.wait()
    lanes = prod_ref.shape[0]
    both = [acc_ref[lax.rem(my_y + y, n_y)].astype(BF).reshape(stored * piece, 2 * DH) for y in range(n_y)]
    both = jnp.concatenate(both, axis=1)
    for n in range(0, lanes, 2):
        wide = min(2, lanes - n)
        w = jnp.concatenate([pair_ref[y, n * DH : (n + wide) * DH, :] for y in range(n_y)], axis=1)
        term = lax.dot_general(both, w, NT, preferred_element_type=F32)
        for i in range(wide):
            prod_ref[n + i] = term[:, i * DH : (i + 1) * DH]
    for t in range(0, piece, 2):
        for n in range(lanes):
            two = [prod_ref[n, pl.ds(t + k, stored, stride=piece), :] for k in range(2)]
            out_ref[pl.ds(t * stored, 2 * stored), n * DH : (n + 1) * DH] = jnp.concatenate(two, axis=0).astype(BF)

    heads = [lax.rem(my_z + j, n_z) for j in range(n_z)]
    for second in range(2):
        for k in range(0, n_y, 2):
            at = [lax.rem(my_y + k + i, n_y) for i in range(2)]
            if second:
                w = [jnp.concatenate([w_ref[1, h, at[i]] for h in heads], axis=1) for i in range(2)]
                total = lax.dot_general(a_ref[1], jnp.concatenate(w, axis=0), NT, preferred_element_type=F32)
            else:
                w = [jnp.concatenate([w_ref[0, h, at[i]] for h in heads], axis=0) for i in range(2)]
                total = jnp.dot(a_ref[0], jnp.concatenate(w, axis=1), preferred_element_type=F32)
            for i in range(2):
                ref = sums[second * n_y + k + i]
                ref[...] = total[:, i * DH : (i + 1) * DH].astype(ref.dtype)


def shards(hidden, encoded, neighbours, w_query, w_key, w_value, w_out, cotangent):
    n_x, n_c, n_y, n_z = (lax.axis_size(a) for a in ("x", "c", "y", "z"))
    dp = ("x", "c")
    owners = n_x * n_c
    rows, width = hidden.shape
    blocks, per_block = neighbours.shape
    cap = blocks * per_block // 4
    stored = encoded.shape[0]
    enc_width = w_key.shape[0]
    seg = encoded.shape[1] // enc_width
    block_len = rows // blocks
    piece = seg // n_y
    ids = neighbours.T
    place = jnp.stack([lax.axis_index(a) for a in ("x", "c", "y", "z")]).astype(jnp.int32)

    def shift(axis, n, k):
        return lambda a: lax.ppermute(a, axis, [(i, (i + k) % n) for i in range(n)])

    swap = shift("c", n_c, 1)
    x_up, x_down = shift("x", n_x, -1), shift("x", n_x, 1)
    z_up, z_down = shift("z", n_z, -1), shift("z", n_z, 1)
    tie = lax.optimization_barrier

    enc_rows = encoded.reshape(stored, seg, enc_width).transpose(1, 0, 2).reshape(seg * stored, enc_width)
    kv, pair, mine = call(
        functools.partial(keys_values_body, stored, n_z, n_y),
        (
            jax.ShapeDtypeStruct((HEAD + stored * seg, 2 * DH), BF),
            jax.ShapeDtypeStruct((enc_width, 2 * DH), BF),
            jax.ShapeDtypeStruct((n_z, n_y, DH, DH), BF),
        ),
        "ssvvvaa", 470_000_000, 5 << 20,
        scratch=(pltpu.VMEM((2, seg * stored, DH), F32), pltpu.SemaphoreType.DMA((n_z * n_y,))),
    )(place, ids, enc_rows, w_key, w_value, w_out, w_query)
    after, before, kv_other = x_up(kv), x_down(kv), swap(kv)
    mine = lax.all_to_all(mine, "z", 0, 0, tiled=True)

    ways = [(c * n_y + y, c * n_y + (y + 2 * c - 1) % n_y) for c in range(n_c) for y in range(n_y)]

    def along_y(a):
        return lax.ppermute(a, ("c", "y"), ways)

    queries = jnp.dot(hidden, w_query, preferred_element_type=F32).astype(BF)
    grad_attn = lax.dot_general(cotangent, w_out, NT, preferred_element_type=F32).astype(BF)
    pair_, queries = tie((pair, queries))
    pair_next = along_y(pair_)
    after, before, queries, grad_attn = tie((after, before, queries, grad_attn))

    cut = HEAD + stored // 2 * seg
    next_lo, next_hi = call(
        functools.partial(halves_body, cut),
        (jax.ShapeDtypeStruct((cut, 2 * DH), BF), jax.ShapeDtypeStruct((kv.shape[0] - cut, 2 * DH), BF)),
        "aa", 0, 0, scratch=(pltpu.SemaphoreType.DMA((2,)),),
    )(after, before)
    far_lo, far_hi = x_up(next_lo), x_down(next_hi)
    kv_all = [kv, after, far_lo, far_hi, before, kv_other] + [swap(a) for a in (after, far_lo, far_hi, before)]
    pairs = [pair, pair_next, along_y(pair_next), swap(pair_next)]

    queries, pairs = tie((queries, pairs))
    other = swap(mine)

    slab = jax.ShapeDtypeStruct((rows, DH), BF)
    attn, gq, outgoing, ids_all = call(
        functools.partial(attention_body, (blocks, block_len, n_x, n_y, cap, stored, seg)),
        (
            slab,
            slab,
            jax.ShapeDtypeStruct((owners, n_y, cap, piece, 2 * DH), BF),
            jax.ShapeDtypeStruct((owners, DH), jnp.int32),
        ),
        "ssvv" + "a" * len(kv_all), 0, 0,
        scratch=(
            pltpu.VMEM((blocks * per_block, seg, 2 * DH), BF),
            pltpu.VMEM((blocks * per_block, n_y, piece, 2 * DH), BF),
            pltpu.VMEM((owners, HEAD, DH), BF),
            pltpu.SemaphoreType.DMA((2 * blocks * per_block + owners,)),
        ),
        out_space="vvav",
    )(place, ids, queries, grad_attn, *kv_all)

    def ring(own):
        pieces = {0: own}
        for k in range(1, n_z // 2 + 1):
            pieces[k] = z_up(pieces[k - 1])
        last = own
        for k in range(1, n_z - n_z // 2):
            last = z_down(last)
            pieces[n_z - k] = last
        return [pieces[k] for k in range(n_z)]

    returned = lax.all_to_all(
        outgoing.reshape(owners * n_y, cap, piece, 2 * DH), dp + ("y",), 0, 0, tiled=True
    ).reshape(owners, n_y, cap, piece, 2 * DH)
    attn_all, gq_all = ring(attn), ring(gq)
    sums = (jax.ShapeDtypeStruct((rows, DH), F32),) + (slab,) * (n_y - 1)
    enc_part, *sums = call(
        functools.partial(tail_body, stored, n_z),
        (jax.ShapeDtypeStruct((piece * stored, enc_width), BF),) + sums + sums,
        "ssa" + "a" * (n_y + 2 * n_z + 2), 1_580_000_000, 10 << 20,
        scratch=(
            pltpu.VMEM((owners, n_y, cap, piece, 2 * DH), BF),
            pltpu.VMEM((n_y, enc_width, 2 * DH), BF),
            pltpu.VMEM((n_y, stored, piece, 2 * DH), F32),
            pltpu.VMEM((enc_width // DH, stored * piece, DH), F32),
            pltpu.VMEM((2, rows, n_z * DH), BF),
            pltpu.VMEM((2, n_z, n_y, DH, DH), BF),
            pltpu.SemaphoreType.DMA((owners + n_y + 2 * n_z + 2,)),
        ),
    )(place, ids_all, returned, *pairs, *attn_all, *gq_all, mine, other)
    enc_parts = lax.all_to_all(enc_part.reshape(n_z, -1, enc_width), "z", 0, 0, tiled=True)
    enc_rows_sum = jnp.sum(enc_parts.astype(F32), axis=0).astype(BF)
    grad_encoded = enc_rows_sum.reshape(seg // (n_y * n_z), stored, enc_width).transpose(1, 0, 2).reshape(stored, -1)

    def summed(parts):
        total = parts[0]
        for k in range(1, n_y):
            total = total + shift("y", n_y, k)(parts[k]).astype(F32)
        return total.astype(BF)

    return summed(sums[:n_y]), summed(sums[n_y:]), grad_encoded


def solution(mesh):
    n_y = 4
    dp, mp = mesh.shape["dp"], mesh.shape["mp"]
    split = Mesh(mesh.devices.reshape(dp // 2, 2, n_y, mp // n_y), ("x", "c", "y", "z"))
    d, m = ("x", "c"), ("y", "z")
    return jax.shard_map(
        shards,
        mesh=split,
        in_specs=(P(d, None), P(d, None), P(d, None), P(None, m), P(None, m), P(None, m), P(m, None), P(d, None)),
        out_specs=(P(d, m), P(d, m), P(d, m)),
        check_vma=False,
    )
```

```python
import functools
import math

import jax
import jax.numpy as jnp
from jax import lax
from jax.experimental import pallas as pl
from jax.experimental.pallas import tpu as pltpu
from jax.sharding import Mesh, PartitionSpec as P

DH = 128
BF = jnp.bfloat16
F32 = jnp.float32
NT = (((1,), (1,)), ((), ()))
TN = (((0,), (0,)), ((), ()))
HEAD = 16
GROUP = 8
VMEM_LIMIT = 64 * 1024 * 1024 - 64 * 1024


def params():
    return pltpu.CompilerParams(vmem_limit_bytes=VMEM_LIMIT)


def call(body, out_shape, in_spaces, flops, moved, scratch=(), out_space="v"):
    spaces = {"s": pltpu.SMEM, "v": pltpu.VMEM, "a": pltpu.HBM}
    single = not isinstance(out_shape, (tuple, list))
    outs = [out_shape] if single else out_shape
    out = tuple(pl.BlockSpec(memory_space=spaces[k]) for k in out_space * (len(outs) if len(out_space) == 1 else 1))
    return pl.pallas_call(
        body,
        out_shape=out_shape,
        in_specs=[pl.BlockSpec(memory_space=spaces[k]) for k in in_spaces],
        out_specs=out[0] if single else out,
        scratch_shapes=list(scratch),
        compiler_params=params(),
        cost_estimate=pl.CostEstimate(flops=flops, bytes_accessed=moved, transcendentals=0),
    )


def keys_values_body(stored, n_z, n_y, pos_ref, ids_ref, x_ref, wk_ref, wv_ref, wo_ref, wq_ref, out_ref, pair_ref, w_ref, kv_ref, sem):
    def moved(block):
        return [
            pltpu.make_async_copy(block((y * n_z + z) * DH), w_ref.at[z, y], sem.at[y * n_z + z])
            for y in range(n_y)
            for z in range(n_z)
        ]

    copies = moved(lambda at: wq_ref.at[at : at + DH, :])

    @pl.when(pos_ref[1] == 0)
    def _():
        for copy in moved(lambda at: wo_ref.at[:, at : at + DH]):
            copy.start()

    @pl.when(pos_ref[1] != 0)
    def _():
        for copy in copies:
            copy.start()

    pair = jnp.concatenate([wk_ref[...], wv_ref[...]], axis=1)
    pair_ref[...] = pair
    seg = x_ref.shape[0] // stored
    both = jnp.dot(x_ref[...], pair, preferred_element_type=F32)
    for n in range(kv_ref.shape[0]):
        kv_ref[n] = both[:, n * DH : (n + 1) * DH]
        for s in range(stored):
            rows = slice(HEAD + s * seg, HEAD + (s + 1) * seg)
            out_ref[rows, n * DH : (n + 1) * DH] = kv_ref[n, pl.ds(s, seg, stride=stored), :].astype(BF)
    for copy in copies:
        copy.wait()
    lane = lax.broadcasted_iota(jnp.int32, (HEAD, 2 * DH), 1)
    row = jnp.zeros((HEAD, 2 * DH), F32)
    for r in range(2 * ids_ref.shape[1]):
        row = jnp.where(lane == r, ids_ref[r % 2, r // 2].astype(F32), row)
    out_ref[:HEAD, :] = row.astype(BF)


def halves_body(cut, after_ref, before_ref, lo_ref, hi_ref, sem):
    copies = [
        pltpu.make_async_copy(after_ref.at[:cut], lo_ref, sem.at[0]),
        pltpu.make_async_copy(before_ref.at[cut:], hi_ref, sem.at[1]),
    ]
    for copy in copies:
        copy.start()
    for copy in copies:
        copy.wait()


def attention_body(geom, pos_ref, ids_ref, q_ref, g_ref, *refs):
    blocks, block_len, n_x, n_y, cap, stored, seg = geom
    kv_refs, (attn_ref, gq_ref, out_ref, all_ids_ref, kv_ref, stage_ref, head_ref, sem) = refs[:-8], refs[-8:]
    inv_root = 1.0 / math.sqrt(DH)
    piece = seg // n_y
    cut = HEAD + stored // 2 * seg
    my_x, my_c = pos_ref[0], pos_ref[1]
    requests = 2 * blocks
    parts = len(kv_refs) // 2

    spots = []
    for r in range(requests):
        i = ids_ref[r % 2, r // 2]
        owner, slot = i // stored, lax.rem(i, stored)
        dx = lax.rem(owner // 2 - my_x + n_x, n_x)
        dc = lax.rem(lax.rem(owner, 2) + my_c, 2)
        part = dx + jnp.where(dx == 3, 1, jnp.where((dx == 2) & (slot >= stored // 2), 1, 0))
        row = HEAD + slot * seg - jnp.where(part == 3, cut, 0)
        row = pl.multiple_of(row, HEAD)
        spots.append(owner)
        for k, ref in enumerate(kv_refs):

            @pl.when(dc * parts + part == k)
            def _(ref=ref, row=row, r=r):
                pltpu.make_async_copy(ref.at[pl.ds(row, seg), :], kv_ref.at[r], sem.at[r]).start()

    heads = [(c, d) for c in range(2) for d in range(n_x)]
    head_copies = []
    for i, (c, d) in enumerate(heads):
        ref = kv_refs[c * parts + (4 if d == 3 else d)]
        head_copies.append(pltpu.make_async_copy(ref.at[:HEAD, :DH], head_ref.at[i], sem.at[requests + i]))
        head_copies[-1].start()

    for r in range(requests):
        pltpu.make_async_copy(kv_refs[0].at[:seg, :], kv_ref.at[r], sem.at[r]).wait()

    def context(c):
        both = [kv_ref[r] for r in (2 * c, 2 * c + 1)]
        return [jnp.concatenate([b[:, at : at + DH] for b in both], axis=0) for at in (0, DH)]

    def rows(c):
        return slice(c * block_len, (c + 1) * block_len)

    sent = []
    for first in range(0, blocks, GROUP):
        group = range(first, first + GROUP)
        scores, grad_probs, probs, grad_scores = {}, {}, {}, {}
        for c in group:
            k, v = context(c)
            scores[c] = lax.dot_general(q_ref[rows(c), :], k, NT, preferred_element_type=F32) * inv_root
            grad_probs[c] = lax.dot_general(g_ref[rows(c), :], v, NT, preferred_element_type=F32)
        for c in group:
            e = jnp.exp(scores[c] - jnp.max(scores[c], axis=-1, keepdims=True))
            p = e / jnp.sum(e, axis=-1, keepdims=True)
            probs[c] = p.astype(BF)
            gp = grad_probs[c]
            grad_scores[c] = (p * (gp - jnp.sum(p * gp, axis=-1, keepdims=True))).astype(BF)
        for c in group:
            k, v = context(c)
            attn_ref[rows(c), :] = jnp.dot(probs[c], v, preferred_element_type=F32).astype(BF)
            gq_ref[rows(c), :] = (jnp.dot(grad_scores[c], k, preferred_element_type=F32) * inv_root).astype(BF)
        for c in group:
            gv = lax.dot_general(probs[c], g_ref[rows(c), :], TN, preferred_element_type=F32).astype(BF)
            gk = lax.dot_general(grad_scores[c], q_ref[rows(c), :], TN, preferred_element_type=F32)
            gk = (gk * inv_root).astype(BF)
            for j in range(2):
                r = 2 * c + j
                owner = spots[r]
                pos = sum([(spots[i] == owner).astype(jnp.int32) for i in range(r)], jnp.int32(0))
                for y in range(n_y):
                    part = slice(j * seg + y * piece, j * seg + (y + 1) * piece)
                    stage_ref[r, y, :, :DH] = gk[part, :]
                    stage_ref[r, y, :, DH:] = gv[part, :]
                copy = pltpu.make_async_copy(
                    stage_ref.at[r], out_ref.at[owner, :, pos], sem.at[requests + len(heads) + r]
                )
                copy.start()
                sent.append(copy)
    for i, (c, d) in enumerate(heads):
        head_copies[i].wait()
        owner = lax.rem(my_x + d, n_x) * 2 + lax.rem(my_c + c, 2)
        all_ids_ref[pl.ds(owner, 1), :] = head_ref[i].astype(F32).astype(jnp.int32)[:1, :]
    for copy in sent:
        copy.wait()


def tail_body(stored, n_z, pos_ref, ids_ref, ret_ref, *refs):
    owners, n_y, cap, piece, _ = ret_ref.shape
    pair_refs, refs = refs[:n_y], refs[n_y:]
    piece_refs, (mine, other), refs = refs[: 2 * n_z], refs[2 * n_z : 2 * n_z + 2], refs[2 * n_z + 2 :]
    out_ref, sums, refs = refs[0], refs[1 : 1 + 2 * n_y], refs[1 + 2 * n_y :]
    got_ref, pair_ref, acc_ref, prod_ref, a_ref, w_ref, sem = refs
    my_c, my_y, my_z = (pos_ref[i] for i in range(1, 4))
    me = pos_ref[0] * 2 + my_c

    for d in range(owners):
        pltpu.make_async_copy(ret_ref.at[d], got_ref.at[d], sem.at[d]).start()
    first = owners
    to = (0, 1 + 2 * my_c, 2, 3 - 2 * my_c)
    pair_copies = [pltpu.make_async_copy(pair_refs[y], pair_ref.at[to[y]], sem.at[first + y]) for y in range(n_y)]
    first += n_y
    piece_copies = [
        pltpu.make_async_copy(
            piece_refs[k], a_ref.at[k // n_z, :, (k % n_z) * DH : (k % n_z + 1) * DH], sem.at[first + k]
        )
        for k in range(2 * n_z)
    ]
    first += 2 * n_z
    weight_copies = [
        pltpu.make_async_copy(mine, w_ref.at[my_c], sem.at[first]),
        pltpu.make_async_copy(other, w_ref.at[1 - my_c], sem.at[first + 1]),
    ]
    for copy in pair_copies + piece_copies + weight_copies:
        copy.start()

    acc_ref[...] = jnp.zeros_like(acc_ref)

    def from_device(d, carry):
        pltpu.make_async_copy(ret_ref.at[d], got_ref.at[d], sem.at[d]).wait()
        count = jnp.int32(0)
        for r in range(owners * 2):
            at = ids_ref[d, r]
            named = at // stored == me

            @pl.when(named)
            def _(at=at, count=count):
                slot = lax.rem(at, stored)
                for y in range(n_y):
                    acc_ref[y, slot] += got_ref[d, y, count].astype(F32)

            count = count + named.astype(jnp.int32)
        return carry

    lax.fori_loop(0, owners, from_device, 0)
    for copy in pair_copies + piece_copies + weight_copies:
        copy.wait()
    lanes = prod_ref.shape[0]
    both = [acc_ref[lax.rem(my_y + y, n_y)].astype(BF).reshape(stored * piece, 2 * DH) for y in range(n_y)]
    both = jnp.concatenate(both, axis=1)
    for n in range(0, lanes, 2):
        wide = min(2, lanes - n)
        w = jnp.concatenate([pair_ref[y, n * DH : (n + wide) * DH, :] for y in range(n_y)], axis=1)
        term = lax.dot_general(both, w, NT, preferred_element_type=F32)
        for i in range(wide):
            prod_ref[n + i] = term[:, i * DH : (i + 1) * DH]
    for t in range(0, piece, 2):
        for n in range(lanes):
            two = [prod_ref[n, pl.ds(t + k, stored, stride=piece), :] for k in range(2)]
            out_ref[pl.ds(t * stored, 2 * stored), n * DH : (n + 1) * DH] = jnp.concatenate(two, axis=0).astype(BF)

    heads = [lax.rem(my_z + j, n_z) for j in range(n_z)]
    for second in range(2):
        for k in range(0, n_y, 2):
            at = [lax.rem(my_y + k + i, n_y) for i in range(2)]
            if second:
                w = [jnp.concatenate([w_ref[1, h, at[i]] for h in heads], axis=1) for i in range(2)]
                total = lax.dot_general(a_ref[1], jnp.concatenate(w, axis=0), NT, preferred_element_type=F32)
            else:
                w = [jnp.concatenate([w_ref[0, h, at[i]] for h in heads], axis=0) for i in range(2)]
                total = jnp.dot(a_ref[0], jnp.concatenate(w, axis=1), preferred_element_type=F32)
            for i in range(2):
                ref = sums[second * n_y + k + i]
                ref[...] = total[:, i * DH : (i + 1) * DH].astype(ref.dtype)


def shards(hidden, encoded, neighbours, w_query, w_key, w_value, w_out, cotangent):
    n_x, n_c, n_y, n_z = (lax.axis_size(a) for a in ("x", "c", "y", "z"))
    dp = ("x", "c")
    owners = n_x * n_c
    rows, width = hidden.shape
    blocks, per_block = neighbours.shape
    cap = blocks * per_block // 4
    stored = encoded.shape[0]
    enc_width = w_key.shape[0]
    seg = encoded.shape[1] // enc_width
    block_len = rows // blocks
    piece = seg // n_y
    ids = neighbours.T
    place = jnp.stack([lax.axis_index(a) for a in ("x", "c", "y", "z")]).astype(jnp.int32)

    def shift(axis, n, k):
        return lambda a: lax.ppermute(a, axis, [(i, (i + k) % n) for i in range(n)])

    swap = shift("c", n_c, 1)
    x_up, x_down = shift("x", n_x, -1), shift("x", n_x, 1)
    z_up, z_down = shift("z", n_z, -1), shift("z", n_z, 1)
    tie = lax.optimization_barrier

    enc_rows = encoded.reshape(stored, seg, enc_width).transpose(1, 0, 2).reshape(seg * stored, enc_width)
    kv, pair, mine = call(
        functools.partial(keys_values_body, stored, n_z, n_y),
        (
            jax.ShapeDtypeStruct((HEAD + stored * seg, 2 * DH), BF),
            jax.ShapeDtypeStruct((enc_width, 2 * DH), BF),
            jax.ShapeDtypeStruct((n_z, n_y, DH, DH), BF),
        ),
        "ssvvvaa", 470_000_000, 5 << 20,
        scratch=(pltpu.VMEM((2, seg * stored, DH), F32), pltpu.SemaphoreType.DMA((n_z * n_y,))),
    )(place, ids, enc_rows, w_key, w_value, w_out, w_query)
    after, before, kv_other = x_up(kv), x_down(kv), swap(kv)
    mine = lax.all_to_all(mine, "z", 0, 0, tiled=True)

    ways = [(c * n_y + y, c * n_y + (y + 2 * c - 1) % n_y) for c in range(n_c) for y in range(n_y)]

    def along_y(a):
        return lax.ppermute(a, ("c", "y"), ways)

    queries = jnp.dot(hidden, w_query, preferred_element_type=F32).astype(BF)
    grad_attn = lax.dot_general(cotangent, w_out, NT, preferred_element_type=F32).astype(BF)
    pair_, queries = tie((pair, queries))
    pair_next = along_y(pair_)
    after, before, queries, grad_attn = tie((after, before, queries, grad_attn))

    cut = HEAD + stored // 2 * seg
    next_lo, next_hi = call(
        functools.partial(halves_body, cut),
        (jax.ShapeDtypeStruct((cut, 2 * DH), BF), jax.ShapeDtypeStruct((kv.shape[0] - cut, 2 * DH), BF)),
        "aa", 0, 0, scratch=(pltpu.SemaphoreType.DMA((2,)),),
    )(after, before)
    far_lo, far_hi = x_up(next_lo), x_down(next_hi)
    kv_all = [kv, after, far_lo, far_hi, before, kv_other] + [swap(a) for a in (after, far_lo, far_hi, before)]
    pairs = [pair, pair_next, along_y(pair_next), swap(pair_next)]

    queries, pairs = tie((queries, pairs))
    other = swap(mine)

    slab = jax.ShapeDtypeStruct((rows, DH), BF)
    attn, gq, outgoing, ids_all = call(
        functools.partial(attention_body, (blocks, block_len, n_x, n_y, cap, stored, seg)),
        (
            slab,
            slab,
            jax.ShapeDtypeStruct((owners, n_y, cap, piece, 2 * DH), BF),
            jax.ShapeDtypeStruct((owners, DH), jnp.int32),
        ),
        "ssvv" + "a" * len(kv_all), 0, 0,
        scratch=(
            pltpu.VMEM((blocks * per_block, seg, 2 * DH), BF),
            pltpu.VMEM((blocks * per_block, n_y, piece, 2 * DH), BF),
            pltpu.VMEM((owners, HEAD, DH), BF),
            pltpu.SemaphoreType.DMA((2 * blocks * per_block + owners,)),
        ),
        out_space="vvav",
    )(place, ids, queries, grad_attn, *kv_all)

    def ring(own, long_way, short_way, sign):
        pieces = {0: own}
        last = own
        for k in range(1, n_z // 2 + 1):
            last = long_way(last)
            pieces[(sign * k) % n_z] = last
        last = own
        for k in range(1, n_z - n_z // 2):
            last = short_way(last)
            pieces[(-sign * k) % n_z] = last
        return [pieces[k] for k in range(n_z)]

    returned = lax.all_to_all(
        outgoing.reshape(owners * n_y, cap, piece, 2 * DH), dp + ("y",), 0, 0, tiled=True
    ).reshape(owners, n_y, cap, piece, 2 * DH)
    attn_all, gq_all = ring(attn, z_up, z_down, 1), ring(gq, z_down, z_up, -1)
    sums = (jax.ShapeDtypeStruct((rows, DH), F32),) + (slab,) * (n_y - 1)
    enc_part, *sums = call(
        functools.partial(tail_body, stored, n_z),
        (jax.ShapeDtypeStruct((piece * stored, enc_width), BF),) + sums + sums,
        "ssa" + "a" * (n_y + 2 * n_z + 2), 1_580_000_000, 10 << 20,
        scratch=(
            pltpu.VMEM((owners, n_y, cap, piece, 2 * DH), BF),
            pltpu.VMEM((n_y, enc_width, 2 * DH), BF),
            pltpu.VMEM((n_y, stored, piece, 2 * DH), F32),
            pltpu.VMEM((enc_width // DH, stored * piece, DH), F32),
            pltpu.VMEM((2, rows, n_z * DH), BF),
            pltpu.VMEM((2, n_z, n_y, DH, DH), BF),
            pltpu.SemaphoreType.DMA((owners + n_y + 2 * n_z + 2,)),
        ),
    )(place, ids_all, returned, *pairs, *attn_all, *gq_all, mine, other)
    enc_parts = lax.all_to_all(enc_part.reshape(n_z, -1, enc_width), "z", 0, 0, tiled=True)
    enc_rows_sum = jnp.sum(enc_parts.astype(F32), axis=0).astype(BF)
    grad_encoded = enc_rows_sum.reshape(seg // (n_y * n_z), stored, enc_width).transpose(1, 0, 2).reshape(stored, -1)

    def summed(parts):
        total = parts[0]
        for k in range(1, n_y):
            total = total + shift("y", n_y, k)(parts[k]).astype(F32)
        return total.astype(BF)

    return summed(sums[:n_y]), summed(sums[n_y:]), grad_encoded


def solution(mesh):
    n_y = 4
    dp, mp = mesh.shape["dp"], mesh.shape["mp"]
    split = Mesh(mesh.devices.reshape(dp // 2, 2, n_y, mp // n_y), ("x", "c", "y", "z"))
    d, m = ("x", "c"), ("y", "z")
    return jax.shard_map(
        shards,
        mesh=split,
        in_specs=(P(d, None), P(d, None), P(d, None), P(None, m), P(None, m), P(None, m), P(m, None), P(d, None)),
        out_specs=(P(d, m), P(d, m), P(d, m)),
        check_vma=False,
    )
```

```python
import functools
import math

import jax
import jax.numpy as jnp
from jax import lax
from jax.experimental import pallas as pl
from jax.experimental.pallas import tpu as pltpu
from jax.sharding import Mesh, PartitionSpec as P

DH = 128
BF = jnp.bfloat16
F32 = jnp.float32
NT = (((1,), (1,)), ((), ()))
TN = (((0,), (0,)), ((), ()))
HEAD = 16
GROUP = 8
VMEM_LIMIT = 64 * 1024 * 1024 - 64 * 1024


def params():
    return pltpu.CompilerParams(vmem_limit_bytes=VMEM_LIMIT)


def call(body, out_shape, in_spaces, flops, moved, scratch=(), out_space="v"):
    spaces = {"s": pltpu.SMEM, "v": pltpu.VMEM, "a": pltpu.HBM}
    single = not isinstance(out_shape, (tuple, list))
    outs = [out_shape] if single else out_shape
    out = tuple(pl.BlockSpec(memory_space=spaces[k]) for k in out_space * (len(outs) if len(out_space) == 1 else 1))
    return pl.pallas_call(
        body,
        out_shape=out_shape,
        in_specs=[pl.BlockSpec(memory_space=spaces[k]) for k in in_spaces],
        out_specs=out[0] if single else out,
        scratch_shapes=list(scratch),
        compiler_params=params(),
        cost_estimate=pl.CostEstimate(flops=flops, bytes_accessed=moved, transcendentals=0),
    )


def keys_values_body(stored, n_z, n_y, ids_ref, x_ref, wk_ref, wv_ref, wo_ref, wq_ref, out_ref, pair_ref, w_ref, kv_ref, sem):
    def moved(block):
        return [
            pltpu.make_async_copy(block((y * n_z + z) * DH), w_ref.at[z, y], sem.at[y * n_z + z])
            for y in range(n_y)
            for z in range(n_z)
        ]

    copies = moved(lambda at: wq_ref.at[at : at + DH, :])

    core = lax.axis_index("c")

    @pl.when(core == 0)
    def _():
        for copy in moved(lambda at: wo_ref.at[:, at : at + DH]):
            copy.start()

    @pl.when(core != 0)
    def _():
        for copy in copies:
            copy.start()

    pair = jnp.concatenate([wk_ref[...], wv_ref[...]], axis=1)
    pair_ref[...] = pair
    seg = x_ref.shape[0] // stored
    both = jnp.dot(x_ref[...], pair, preferred_element_type=F32)
    for n in range(kv_ref.shape[0]):
        kv_ref[n] = both[:, n * DH : (n + 1) * DH]
        for s in range(stored):
            rows = slice(HEAD + s * seg, HEAD + (s + 1) * seg)
            out_ref[rows, n * DH : (n + 1) * DH] = kv_ref[n, pl.ds(s, seg, stride=stored), :].astype(BF)
    for copy in copies:
        copy.wait()
    lane = lax.broadcasted_iota(jnp.int32, (HEAD, 2 * DH), 1)
    row = jnp.zeros((HEAD, 2 * DH), F32)
    for r in range(2 * ids_ref.shape[1]):
        row = jnp.where(lane == r, ids_ref[r % 2, r // 2].astype(F32), row)
    out_ref[:HEAD, :] = row.astype(BF)


def halves_body(cut, after_ref, before_ref, lo_ref, hi_ref, sem):
    copies = [
        pltpu.make_async_copy(after_ref.at[:cut], lo_ref, sem.at[0]),
        pltpu.make_async_copy(before_ref.at[cut:], hi_ref, sem.at[1]),
    ]
    for copy in copies:
        copy.start()
    for copy in copies:
        copy.wait()


def attention_body(geom, pos_ref, ids_ref, q_ref, g_ref, *refs):
    blocks, block_len, n_x, n_y, cap, stored, seg = geom
    kv_refs, (attn_ref, gq_ref, out_ref, all_ids_ref, kv_ref, stage_ref, head_ref, sem) = refs[:-8], refs[-8:]
    inv_root = 1.0 / math.sqrt(DH)
    piece = seg // n_y
    cut = HEAD + stored // 2 * seg
    my_x, my_c = pos_ref[0], pos_ref[1]
    requests = 2 * blocks
    parts = len(kv_refs) // 2

    spots = []
    for r in range(requests):
        i = ids_ref[r % 2, r // 2]
        owner, slot = i // stored, lax.rem(i, stored)
        dx = lax.rem(owner // 2 - my_x + n_x, n_x)
        dc = lax.rem(lax.rem(owner, 2) + my_c, 2)
        part = dx + jnp.where(dx == 3, 1, jnp.where((dx == 2) & (slot >= stored // 2), 1, 0))
        row = HEAD + slot * seg - jnp.where(part == 3, cut, 0)
        row = pl.multiple_of(row, HEAD)
        spots.append(owner)
        for k, ref in enumerate(kv_refs):

            @pl.when(dc * parts + part == k)
            def _(ref=ref, row=row, r=r):
                pltpu.make_async_copy(ref.at[pl.ds(row, seg), :], kv_ref.at[r], sem.at[r]).start()

    heads = [(c, d) for c in range(2) for d in range(n_x)]
    head_copies = []
    for i, (c, d) in enumerate(heads):
        ref = kv_refs[c * parts + (4 if d == 3 else d)]
        head_copies.append(pltpu.make_async_copy(ref.at[:HEAD, :DH], head_ref.at[i], sem.at[requests + i]))
        head_copies[-1].start()

    for r in range(requests):
        pltpu.make_async_copy(kv_refs[0].at[:seg, :], kv_ref.at[r], sem.at[r]).wait()

    def context(c):
        both = [kv_ref[r] for r in (2 * c, 2 * c + 1)]
        return [jnp.concatenate([b[:, at : at + DH] for b in both], axis=0) for at in (0, DH)]

    def rows(c):
        return slice(c * block_len, (c + 1) * block_len)

    sent = []
    for first in range(0, blocks, GROUP):
        group = range(first, first + GROUP)
        scores, grad_probs, probs, grad_scores = {}, {}, {}, {}
        for c in group:
            k, v = context(c)
            scores[c] = lax.dot_general(q_ref[rows(c), :], k, NT, preferred_element_type=F32) * inv_root
            grad_probs[c] = lax.dot_general(g_ref[rows(c), :], v, NT, preferred_element_type=F32)
        for c in group:
            e = jnp.exp(scores[c] - jnp.max(scores[c], axis=-1, keepdims=True))
            p = e / jnp.sum(e, axis=-1, keepdims=True)
            probs[c] = p.astype(BF)
            gp = grad_probs[c]
            grad_scores[c] = (p * (gp - jnp.sum(p * gp, axis=-1, keepdims=True))).astype(BF)
        for c in group:
            k, v = context(c)
            attn_ref[rows(c), :] = jnp.dot(probs[c], v, preferred_element_type=F32).astype(BF)
            gq_ref[rows(c), :] = (jnp.dot(grad_scores[c], k, preferred_element_type=F32) * inv_root).astype(BF)
        for c in group:
            gv = lax.dot_general(probs[c], g_ref[rows(c), :], TN, preferred_element_type=F32).astype(BF)
            gk = lax.dot_general(grad_scores[c], q_ref[rows(c), :], TN, preferred_element_type=F32)
            gk = (gk * inv_root).astype(BF)
            for j in range(2):
                r = 2 * c + j
                owner = spots[r]
                pos = sum([(spots[i] == owner).astype(jnp.int32) for i in range(r)], jnp.int32(0))
                for y in range(n_y):
                    part = slice(j * seg + y * piece, j * seg + (y + 1) * piece)
                    stage_ref[r, y, :, :DH] = gk[part, :]
                    stage_ref[r, y, :, DH:] = gv[part, :]
                copy = pltpu.make_async_copy(
                    stage_ref.at[r], out_ref.at[owner, :, pos], sem.at[requests + len(heads) + r]
                )
                copy.start()
                sent.append(copy)
    for i, (c, d) in enumerate(heads):
        head_copies[i].wait()
        owner = lax.rem(my_x + d, n_x) * 2 + lax.rem(my_c + c, 2)
        all_ids_ref[pl.ds(owner, 1), :] = head_ref[i].astype(F32).astype(jnp.int32)[:1, :]
    for copy in sent:
        copy.wait()


def tail_body(stored, n_z, pos_ref, ids_ref, ret_ref, *refs):
    owners, n_y, cap, piece, _ = ret_ref.shape
    pair_refs, refs = refs[:n_y], refs[n_y:]
    piece_refs, (mine, other), refs = refs[: 2 * n_z], refs[2 * n_z : 2 * n_z + 2], refs[2 * n_z + 2 :]
    out_ref, sums, refs = refs[0], refs[1 : 1 + 2 * n_y], refs[1 + 2 * n_y :]
    got_ref, pair_ref, acc_ref, prod_ref, a_ref, w_ref, sem = refs
    my_c, my_y, my_z = (pos_ref[i] for i in range(1, 4))
    me = pos_ref[0] * 2 + my_c

    for d in range(owners):
        pltpu.make_async_copy(ret_ref.at[d], got_ref.at[d], sem.at[d]).start()
    first = owners
    to = (0, 1 + 2 * my_c, 2, 3 - 2 * my_c)
    pair_copies = [pltpu.make_async_copy(pair_refs[y], pair_ref.at[to[y]], sem.at[first + y]) for y in range(n_y)]
    first += n_y
    piece_copies = [
        pltpu.make_async_copy(
            piece_refs[k], a_ref.at[k // n_z, :, (k % n_z) * DH : (k % n_z + 1) * DH], sem.at[first + k]
        )
        for k in range(2 * n_z)
    ]
    first += 2 * n_z
    weight_copies = [
        pltpu.make_async_copy(mine, w_ref.at[my_c], sem.at[first]),
        pltpu.make_async_copy(other, w_ref.at[1 - my_c], sem.at[first + 1]),
    ]
    for copy in pair_copies + piece_copies + weight_copies:
        copy.start()

    acc_ref[...] = jnp.zeros_like(acc_ref)

    def from_device(d, carry):
        pltpu.make_async_copy(ret_ref.at[d], got_ref.at[d], sem.at[d]).wait()
        count = jnp.int32(0)
        for r in range(owners * 2):
            at = ids_ref[d, r]
            named = at // stored == me

            @pl.when(named)
            def _(at=at, count=count):
                slot = lax.rem(at, stored)
                for y in range(n_y):
                    acc_ref[y, slot] += got_ref[d, y, count].astype(F32)

            count = count + named.astype(jnp.int32)
        return carry

    lax.fori_loop(0, owners, from_device, 0)
    for copy in pair_copies + piece_copies + weight_copies:
        copy.wait()
    lanes = prod_ref.shape[0]
    both = [acc_ref[lax.rem(my_y + y, n_y)].astype(BF).reshape(stored * piece, 2 * DH) for y in range(n_y)]
    both = jnp.concatenate(both, axis=1)
    for n in range(0, lanes, 2):
        wide = min(2, lanes - n)
        w = jnp.concatenate([pair_ref[y, n * DH : (n + wide) * DH, :] for y in range(n_y)], axis=1)
        term = lax.dot_general(both, w, NT, preferred_element_type=F32)
        for i in range(wide):
            prod_ref[n + i] = term[:, i * DH : (i + 1) * DH]
    for t in range(0, piece, 2):
        for n in range(lanes):
            two = [prod_ref[n, pl.ds(t + k, stored, stride=piece), :] for k in range(2)]
            out_ref[pl.ds(t * stored, 2 * stored), n * DH : (n + 1) * DH] = jnp.concatenate(two, axis=0).astype(BF)

    heads = [lax.rem(my_z + j, n_z) for j in range(n_z)]
    for second in range(2):
        for k in range(0, n_y, 2):
            at = [lax.rem(my_y + k + i, n_y) for i in range(2)]
            if second:
                w = [jnp.concatenate([w_ref[1, h, at[i]] for h in heads], axis=1) for i in range(2)]
                total = lax.dot_general(a_ref[1], jnp.concatenate(w, axis=0), NT, preferred_element_type=F32)
            else:
                w = [jnp.concatenate([w_ref[0, h, at[i]] for h in heads], axis=0) for i in range(2)]
                total = jnp.dot(a_ref[0], jnp.concatenate(w, axis=1), preferred_element_type=F32)
            for i in range(2):
                ref = sums[second * n_y + k + i]
                ref[...] = total[:, i * DH : (i + 1) * DH].astype(ref.dtype)


def shards(hidden, encoded, neighbours, w_query, w_key, w_value, w_out, cotangent):
    n_x, n_c, n_y, n_z = (lax.axis_size(a) for a in ("x", "c", "y", "z"))
    dp = ("x", "c")
    owners = n_x * n_c
    rows, width = hidden.shape
    blocks, per_block = neighbours.shape
    cap = blocks * per_block // 4
    stored = encoded.shape[0]
    enc_width = w_key.shape[0]
    seg = encoded.shape[1] // enc_width
    block_len = rows // blocks
    piece = seg // n_y
    ids = neighbours.T
    place = jnp.stack([lax.axis_index(a) for a in ("x", "c", "y", "z")]).astype(jnp.int32)

    def shift(axis, n, k):
        return lambda a: lax.ppermute(a, axis, [(i, (i + k) % n) for i in range(n)])

    swap = shift("c", n_c, 1)
    x_up, x_down = shift("x", n_x, -1), shift("x", n_x, 1)
    z_up, z_down = shift("z", n_z, -1), shift("z", n_z, 1)
    tie = lax.optimization_barrier

    enc_rows = encoded.reshape(stored, seg, enc_width).transpose(1, 0, 2).reshape(seg * stored, enc_width)
    kv, pair, mine = call(
        functools.partial(keys_values_body, stored, n_z, n_y),
        (
            jax.ShapeDtypeStruct((HEAD + stored * seg, 2 * DH), BF),
            jax.ShapeDtypeStruct((enc_width, 2 * DH), BF),
            jax.ShapeDtypeStruct((n_z, n_y, DH, DH), BF),
        ),
        "svvvaa", 470_000_000, 5 << 20,
        scratch=(pltpu.VMEM((2, seg * stored, DH), F32), pltpu.SemaphoreType.DMA((n_z * n_y,))),
    )(ids, enc_rows, w_key, w_value, w_out, w_query)
    after, before, kv_other = x_up(kv), x_down(kv), swap(kv)
    mine = lax.all_to_all(mine, "z", 0, 0, tiled=True)

    ways = [(c * n_y + y, c * n_y + (y + 2 * c - 1) % n_y) for c in range(n_c) for y in range(n_y)]

    def along_y(a):
        return lax.ppermute(a, ("c", "y"), ways)

    queries = jnp.dot(hidden, w_query, preferred_element_type=F32).astype(BF)
    grad_attn = lax.dot_general(cotangent, w_out, NT, preferred_element_type=F32).astype(BF)
    pair_, queries = tie((pair, queries))
    pair_next = along_y(pair_)
    after, before, queries, grad_attn = tie((after, before, queries, grad_attn))

    cut = HEAD + stored // 2 * seg
    next_lo, next_hi = call(
        functools.partial(halves_body, cut),
        (jax.ShapeDtypeStruct((cut, 2 * DH), BF), jax.ShapeDtypeStruct((kv.shape[0] - cut, 2 * DH), BF)),
        "aa", 0, 0, scratch=(pltpu.SemaphoreType.DMA((2,)),),
    )(after, before)
    far_lo, far_hi = x_up(next_lo), x_down(next_hi)
    kv_all = [kv, after, far_lo, far_hi, before, kv_other] + [swap(a) for a in (after, far_lo, far_hi, before)]
    pairs = [pair, pair_next, along_y(pair_next), swap(pair_next)]

    queries, pairs = tie((queries, pairs))
    other = swap(mine)

    slab = jax.ShapeDtypeStruct((rows, DH), BF)
    attn, gq, outgoing, ids_all = call(
        functools.partial(attention_body, (blocks, block_len, n_x, n_y, cap, stored, seg)),
        (
            slab,
            slab,
            jax.ShapeDtypeStruct((owners, n_y, cap, piece, 2 * DH), BF),
            jax.ShapeDtypeStruct((owners, DH), jnp.int32),
        ),
        "ssvv" + "a" * len(kv_all), 0, 0,
        scratch=(
            pltpu.VMEM((blocks * per_block, seg, 2 * DH), BF),
            pltpu.VMEM((blocks * per_block, n_y, piece, 2 * DH), BF),
            pltpu.VMEM((owners, HEAD, DH), BF),
            pltpu.SemaphoreType.DMA((2 * blocks * per_block + owners,)),
        ),
        out_space="vvav",
    )(place, ids, queries, grad_attn, *kv_all)

    def ring(own):
        pieces = {0: own}
        for k in range(1, n_z // 2 + 1):
            pieces[k] = z_up(pieces[k - 1])
        last = own
        for k in range(1, n_z - n_z // 2):
            last = z_down(last)
            pieces[n_z - k] = last
        return [pieces[k] for k in range(n_z)]

    returned = lax.all_to_all(
        outgoing.reshape(owners * n_y, cap, piece, 2 * DH), dp + ("y",), 0, 0, tiled=True
    ).reshape(owners, n_y, cap, piece, 2 * DH)
    attn_all, gq_all = ring(attn), ring(gq)
    sums = (jax.ShapeDtypeStruct((rows, DH), F32),) + (slab,) * (n_y - 1)
    enc_part, *sums = call(
        functools.partial(tail_body, stored, n_z),
        (jax.ShapeDtypeStruct((piece * stored, enc_width), BF),) + sums + sums,
        "ssa" + "a" * (n_y + 2 * n_z + 2), 1_580_000_000, 10 << 20,
        scratch=(
            pltpu.VMEM((owners, n_y, cap, piece, 2 * DH), BF),
            pltpu.VMEM((n_y, enc_width, 2 * DH), BF),
            pltpu.VMEM((n_y, stored, piece, 2 * DH), F32),
            pltpu.VMEM((enc_width // DH, stored * piece, DH), F32),
            pltpu.VMEM((2, rows, n_z * DH), BF),
            pltpu.VMEM((2, n_z, n_y, DH, DH), BF),
            pltpu.SemaphoreType.DMA((owners + n_y + 2 * n_z + 2,)),
        ),
    )(place, ids_all, returned, *pairs, *attn_all, *gq_all, mine, other)
    enc_parts = lax.all_to_all(enc_part.reshape(n_z, -1, enc_width), "z", 0, 0, tiled=True)
    enc_rows_sum = jnp.sum(enc_parts.astype(F32), axis=0).astype(BF)

    def summed(parts):
        total = parts[0]
        for k in range(1, n_y):
            total = total + shift("y", n_y, k)(parts[k]).astype(F32)
        return total.astype(BF)

    attended = summed(sums[:n_y])
    own, enc_rows_sum = tie((sums[n_y], enc_rows_sum))
    grad_encoded = enc_rows_sum.reshape(seg // (n_y * n_z), stored, enc_width).transpose(1, 0, 2).reshape(stored, -1)
    return attended, summed([own, *sums[n_y + 1 :]]), grad_encoded


def solution(mesh):
    n_y = 4
    dp, mp = mesh.shape["dp"], mesh.shape["mp"]
    split = Mesh(mesh.devices.reshape(dp // 2, 2, n_y, mp // n_y), ("x", "c", "y", "z"))
    d, m = ("x", "c"), ("y", "z")
    return jax.shard_map(
        shards,
        mesh=split,
        in_specs=(P(d, None), P(d, None), P(d, None), P(None, m), P(None, m), P(None, m), P(m, None), P(d, None)),
        out_specs=(P(d, m), P(d, m), P(d, m)),
        check_vma=False,
    )
```

```python
import functools
import math

import jax
import jax.numpy as jnp
from jax import lax
from jax.experimental import pallas as pl
from jax.experimental.pallas import tpu as pltpu
from jax.sharding import Mesh, PartitionSpec as P

DH = 128
BF = jnp.bfloat16
F32 = jnp.float32
NT = (((1,), (1,)), ((), ()))
TN = (((0,), (0,)), ((), ()))
HEAD = 16
GROUP = 8
VMEM_LIMIT = 64 * 1024 * 1024 - 64 * 1024


def params():
    return pltpu.CompilerParams(vmem_limit_bytes=VMEM_LIMIT)


def call(body, out_shape, in_spaces, flops, moved, scratch=(), out_space="v"):
    spaces = {"s": pltpu.SMEM, "v": pltpu.VMEM, "a": pltpu.HBM}
    single = not isinstance(out_shape, (tuple, list))
    outs = [out_shape] if single else out_shape
    out = tuple(pl.BlockSpec(memory_space=spaces[k]) for k in out_space * (len(outs) if len(out_space) == 1 else 1))
    return pl.pallas_call(
        body,
        out_shape=out_shape,
        in_specs=[pl.BlockSpec(memory_space=spaces[k]) for k in in_spaces],
        out_specs=out[0] if single else out,
        scratch_shapes=list(scratch),
        compiler_params=params(),
        cost_estimate=pl.CostEstimate(flops=flops, bytes_accessed=moved, transcendentals=0),
    )


def keys_values_body(stored, n_z, n_y, ids_ref, x_ref, wk_ref, wv_ref, wo_ref, wq_ref, out_ref, pair_ref, w_ref, kv_ref, sem):
    def moved(block):
        return [
            pltpu.make_async_copy(block((y * n_z + z) * DH), w_ref.at[z, y], sem.at[y * n_z + z])
            for y in range(n_y)
            for z in range(n_z)
        ]

    copies = moved(lambda at: wq_ref.at[at : at + DH, :])

    core = lax.axis_index("c")

    @pl.when(core == 0)
    def _():
        for copy in moved(lambda at: wo_ref.at[:, at : at + DH]):
            copy.start()

    @pl.when(core != 0)
    def _():
        for copy in copies:
            copy.start()

    pair = jnp.concatenate([wk_ref[...], wv_ref[...]], axis=1)
    pair_ref[...] = pair
    seg = x_ref.shape[0] // stored
    both = jnp.dot(x_ref[...], pair, preferred_element_type=F32)
    for n in range(kv_ref.shape[0]):
        kv_ref[n] = both[:, n * DH : (n + 1) * DH]
        for s in range(stored):
            rows = slice(HEAD + s * seg, HEAD + (s + 1) * seg)
            out_ref[rows, n * DH : (n + 1) * DH] = kv_ref[n, pl.ds(s, seg, stride=stored), :].astype(BF)
    for copy in copies:
        copy.wait()
    lane = lax.broadcasted_iota(jnp.int32, (HEAD, 2 * DH), 1)
    row = jnp.zeros((HEAD, 2 * DH), F32)
    for r in range(2 * ids_ref.shape[1]):
        row = jnp.where(lane == r, ids_ref[r % 2, r // 2].astype(F32), row)
    out_ref[:HEAD, :] = row.astype(BF)


def halves_body(cut, after_ref, before_ref, lo_ref, hi_ref, sem):
    copies = [
        pltpu.make_async_copy(after_ref.at[:cut], lo_ref, sem.at[0]),
        pltpu.make_async_copy(before_ref.at[cut:], hi_ref, sem.at[1]),
    ]
    for copy in copies:
        copy.start()
    for copy in copies:
        copy.wait()


def attention_body(geom, ids_ref, q_ref, g_ref, *refs):
    blocks, block_len, n_x, n_y, cap, stored, seg = geom
    kv_refs, (attn_ref, gq_ref, out_ref, all_ids_ref, kv_ref, stage_ref, head_ref, sem) = refs[:-8], refs[-8:]
    inv_root = 1.0 / math.sqrt(DH)
    piece = seg // n_y
    cut = HEAD + stored // 2 * seg
    my_x, my_c = lax.axis_index("x"), lax.axis_index("c")
    requests = 2 * blocks
    parts = len(kv_refs) // 2

    spots = []
    for r in range(requests):
        i = ids_ref[r % 2, r // 2]
        owner, slot = i // stored, lax.rem(i, stored)
        dx = lax.rem(owner // 2 - my_x + n_x, n_x)
        dc = lax.rem(lax.rem(owner, 2) + my_c, 2)
        part = dx + jnp.where(dx == 3, 1, jnp.where((dx == 2) & (slot >= stored // 2), 1, 0))
        row = HEAD + slot * seg - jnp.where(part == 3, cut, 0)
        row = pl.multiple_of(row, HEAD)
        spots.append(owner)
        for k, ref in enumerate(kv_refs):

            @pl.when(dc * parts + part == k)
            def _(ref=ref, row=row, r=r):
                pltpu.make_async_copy(ref.at[pl.ds(row, seg), :], kv_ref.at[r], sem.at[r]).start()

    heads = [(c, d) for c in range(2) for d in range(n_x)]
    head_copies = []
    for i, (c, d) in enumerate(heads):
        ref = kv_refs[c * parts + (4 if d == 3 else d)]
        head_copies.append(pltpu.make_async_copy(ref.at[:HEAD, :DH], head_ref.at[i], sem.at[requests + i]))
        head_copies[-1].start()

    for r in range(requests):
        pltpu.make_async_copy(kv_refs[0].at[:seg, :], kv_ref.at[r], sem.at[r]).wait()

    def context(c):
        both = [kv_ref[r] for r in (2 * c, 2 * c + 1)]
        return [jnp.concatenate([b[:, at : at + DH] for b in both], axis=0) for at in (0, DH)]

    def rows(c):
        return slice(c * block_len, (c + 1) * block_len)

    sent = []
    for first in range(0, blocks, GROUP):
        group = range(first, first + GROUP)
        scores, grad_probs, probs, grad_scores = {}, {}, {}, {}
        for c in group:
            k, v = context(c)
            scores[c] = lax.dot_general(q_ref[rows(c), :], k, NT, preferred_element_type=F32) * inv_root
            grad_probs[c] = lax.dot_general(g_ref[rows(c), :], v, NT, preferred_element_type=F32)
        for c in group:
            e = jnp.exp(scores[c] - jnp.max(scores[c], axis=-1, keepdims=True))
            p = e / jnp.sum(e, axis=-1, keepdims=True)
            probs[c] = p.astype(BF)
            gp = grad_probs[c]
            grad_scores[c] = (p * (gp - jnp.sum(p * gp, axis=-1, keepdims=True))).astype(BF)
        for c in group:
            k, v = context(c)
            attn_ref[rows(c), :] = jnp.dot(probs[c], v, preferred_element_type=F32).astype(BF)
            gq_ref[rows(c), :] = (jnp.dot(grad_scores[c], k, preferred_element_type=F32) * inv_root).astype(BF)
        for c in group:
            gv = lax.dot_general(probs[c], g_ref[rows(c), :], TN, preferred_element_type=F32).astype(BF)
            gk = lax.dot_general(grad_scores[c], q_ref[rows(c), :], TN, preferred_element_type=F32)
            gk = (gk * inv_root).astype(BF)
            for j in range(2):
                r = 2 * c + j
                owner = spots[r]
                pos = sum([(spots[i] == owner).astype(jnp.int32) for i in range(r)], jnp.int32(0))
                for y in range(n_y):
                    part = slice(j * seg + y * piece, j * seg + (y + 1) * piece)
                    stage_ref[r, y, :, :DH] = gk[part, :]
                    stage_ref[r, y, :, DH:] = gv[part, :]
                copy = pltpu.make_async_copy(
                    stage_ref.at[r], out_ref.at[owner, :, pos], sem.at[requests + len(heads) + r]
                )
                copy.start()
                sent.append(copy)
    for i, (c, d) in enumerate(heads):
        head_copies[i].wait()
        owner = lax.rem(my_x + d, n_x) * 2 + lax.rem(my_c + c, 2)
        all_ids_ref[pl.ds(owner, 1), :] = head_ref[i].astype(F32).astype(jnp.int32)[:1, :]
    for copy in sent:
        copy.wait()


def tail_body(stored, n_z, ids_ref, ret_ref, *refs):
    owners, n_y, cap, piece, _ = ret_ref.shape
    pair_refs, refs = refs[:n_y], refs[n_y:]
    piece_refs, (mine, other), refs = refs[: 2 * n_z], refs[2 * n_z : 2 * n_z + 2], refs[2 * n_z + 2 :]
    out_hbm, sums_hbm, refs = refs[0], refs[1 : 1 + 2 * n_y], refs[1 + 2 * n_y :]
    got_ref, pair_ref, acc_ref, prod_ref, a_ref, w_ref, out_ref, own_ref, sent_ref, sem = refs
    my_x, my_c, my_y, my_z = (lax.axis_index(a) for a in ("x", "c", "y", "z"))
    me = my_x * 2 + my_c

    for d in range(owners):
        pltpu.make_async_copy(ret_ref.at[d], got_ref.at[d], sem.at[d]).start()
    first = owners
    to = (0, 1 + 2 * my_c, 2, 3 - 2 * my_c)
    pair_copies = [pltpu.make_async_copy(pair_refs[y], pair_ref.at[to[y]], sem.at[first + y]) for y in range(n_y)]
    first += n_y
    piece_copies = [
        pltpu.make_async_copy(
            piece_refs[k], a_ref.at[k // n_z, :, (k % n_z) * DH : (k % n_z + 1) * DH], sem.at[first + k]
        )
        for k in range(2 * n_z)
    ]
    first += 2 * n_z
    weight_copies = [
        pltpu.make_async_copy(mine, w_ref.at[my_c], sem.at[first]),
        pltpu.make_async_copy(other, w_ref.at[1 - my_c], sem.at[first + 1]),
    ]
    for copy in pair_copies + piece_copies + weight_copies:
        copy.start()

    acc_ref[...] = jnp.zeros_like(acc_ref)

    def from_device(d, carry):
        pltpu.make_async_copy(ret_ref.at[d], got_ref.at[d], sem.at[d]).wait()
        count = jnp.int32(0)
        for r in range(owners * 2):
            at = ids_ref[d, r]
            named = at // stored == me

            @pl.when(named)
            def _(at=at, count=count):
                slot = lax.rem(at, stored)
                for y in range(n_y):
                    acc_ref[y, slot] += got_ref[d, y, count].astype(F32)

            count = count + named.astype(jnp.int32)
        return carry

    lax.fori_loop(0, owners, from_device, 0)
    for copy in pair_copies:
        copy.wait()
    lanes = prod_ref.shape[0]
    both = [acc_ref[lax.rem(my_y + y, n_y)].astype(BF).reshape(stored * piece, 2 * DH) for y in range(n_y)]
    both = jnp.concatenate(both, axis=1)
    for n in range(0, lanes, 2):
        wide = min(2, lanes - n)
        w = jnp.concatenate([pair_ref[y, n * DH : (n + wide) * DH, :] for y in range(n_y)], axis=1)
        term = lax.dot_general(both, w, NT, preferred_element_type=F32)
        for i in range(wide):
            prod_ref[n + i] = term[:, i * DH : (i + 1) * DH]
    for t in range(0, piece, 2):
        for n in range(lanes):
            two = [prod_ref[n, pl.ds(t + k, stored, stride=piece), :] for k in range(2)]
            out_ref[pl.ds(t * stored, 2 * stored), n * DH : (n + 1) * DH] = jnp.concatenate(two, axis=0).astype(BF)

    first += 2
    leaving = [pltpu.make_async_copy(out_ref, out_hbm, sem.at[first])]
    leaving[0].start()

    for copy in piece_copies + weight_copies:
        copy.wait()
    heads = [lax.rem(my_z + j, n_z) for j in range(n_z)]
    for second in range(2):
        for k in range(0, n_y, 2):
            at = [lax.rem(my_y + k + i, n_y) for i in range(2)]
            if second:
                w = [jnp.concatenate([w_ref[1, h, at[i]] for h in heads], axis=1) for i in range(2)]
                total = lax.dot_general(a_ref[1], jnp.concatenate(w, axis=0), NT, preferred_element_type=F32)
            else:
                w = [jnp.concatenate([w_ref[0, h, at[i]] for h in heads], axis=0) for i in range(2)]
                total = jnp.dot(a_ref[0], jnp.concatenate(w, axis=1), preferred_element_type=F32)
            for i in range(2):
                ref = sent_ref.at[second, k + i - 1] if k + i else own_ref.at[second]
                ref[...] = total[:, i * DH : (i + 1) * DH].astype(ref.dtype)
        for k in range(n_y):
            ref = sent_ref.at[second, k - 1] if k else own_ref.at[second]
            n = second * n_y + k
            leaving.append(pltpu.make_async_copy(ref, sums_hbm[n], sem.at[first + 1 + n]))
            leaving[-1].start()
    for copy in leaving:
        copy.wait()


def shards(hidden, encoded, neighbours, w_query, w_key, w_value, w_out, cotangent):
    n_x, n_c, n_y, n_z = (lax.axis_size(a) for a in ("x", "c", "y", "z"))
    dp = ("x", "c")
    owners = n_x * n_c
    rows, width = hidden.shape
    blocks, per_block = neighbours.shape
    cap = blocks * per_block // 4
    stored = encoded.shape[0]
    enc_width = w_key.shape[0]
    seg = encoded.shape[1] // enc_width
    block_len = rows // blocks
    piece = seg // n_y
    ids = neighbours.T

    def shift(axis, n, k):
        return lambda a: lax.ppermute(a, axis, [(i, (i + k) % n) for i in range(n)])

    swap = shift("c", n_c, 1)
    x_up, x_down = shift("x", n_x, -1), shift("x", n_x, 1)
    z_up, z_down = shift("z", n_z, -1), shift("z", n_z, 1)
    tie = lax.optimization_barrier

    enc_rows = encoded.reshape(stored, seg, enc_width).transpose(1, 0, 2).reshape(seg * stored, enc_width)
    kv, pair, mine = call(
        functools.partial(keys_values_body, stored, n_z, n_y),
        (
            jax.ShapeDtypeStruct((HEAD + stored * seg, 2 * DH), BF),
            jax.ShapeDtypeStruct((enc_width, 2 * DH), BF),
            jax.ShapeDtypeStruct((n_z, n_y, DH, DH), BF),
        ),
        "svvvaa", 470_000_000, 5 << 20,
        scratch=(pltpu.VMEM((2, seg * stored, DH), F32), pltpu.SemaphoreType.DMA((n_z * n_y,))),
    )(ids, enc_rows, w_key, w_value, w_out, w_query)
    after, before, kv_other = x_up(kv), x_down(kv), swap(kv)
    mine = lax.all_to_all(mine, "z", 0, 0, tiled=True)

    ways = [(c * n_y + y, c * n_y + (y + 2 * c - 1) % n_y) for c in range(n_c) for y in range(n_y)]

    def along_y(a):
        return lax.ppermute(a, ("c", "y"), ways)

    queries = jnp.dot(hidden, w_query, preferred_element_type=F32).astype(BF)
    grad_attn = lax.dot_general(cotangent, w_out, NT, preferred_element_type=F32).astype(BF)
    pair_, queries = tie((pair, queries))
    pair_next = along_y(pair_)
    after, before, queries, grad_attn = tie((after, before, queries, grad_attn))

    cut = HEAD + stored // 2 * seg
    next_lo, next_hi = call(
        functools.partial(halves_body, cut),
        (jax.ShapeDtypeStruct((cut, 2 * DH), BF), jax.ShapeDtypeStruct((kv.shape[0] - cut, 2 * DH), BF)),
        "aa", 0, 0, scratch=(pltpu.SemaphoreType.DMA((2,)),),
    )(after, before)
    far_lo, far_hi = x_up(next_lo), x_down(next_hi)
    kv_all = [kv, after, far_lo, far_hi, before, kv_other] + [swap(a) for a in (after, far_lo, far_hi, before)]
    pairs = [pair, pair_next, along_y(pair_next), swap(pair_next)]

    queries, pairs = tie((queries, pairs))
    other = swap(mine)

    slab = jax.ShapeDtypeStruct((rows, DH), BF)
    attn, gq, outgoing, ids_all = call(
        functools.partial(attention_body, (blocks, block_len, n_x, n_y, cap, stored, seg)),
        (
            slab,
            slab,
            jax.ShapeDtypeStruct((owners, n_y, cap, piece, 2 * DH), BF),
            jax.ShapeDtypeStruct((owners, DH), jnp.int32),
        ),
        "svv" + "a" * len(kv_all), 0, 0,
        scratch=(
            pltpu.VMEM((blocks * per_block, seg, 2 * DH), BF),
            pltpu.VMEM((blocks * per_block, n_y, piece, 2 * DH), BF),
            pltpu.VMEM((owners, HEAD, DH), BF),
            pltpu.SemaphoreType.DMA((2 * blocks * per_block + owners,)),
        ),
        out_space="vvav",
    )(ids, queries, grad_attn, *kv_all)

    def ring(own):
        pieces = {0: own}
        for k in range(1, n_z // 2 + 1):
            pieces[k] = z_up(pieces[k - 1])
        last = own
        for k in range(1, n_z - n_z // 2):
            last = z_down(last)
            pieces[n_z - k] = last
        return [pieces[k] for k in range(n_z)]

    returned = lax.all_to_all(
        outgoing.reshape(owners * n_y, cap, piece, 2 * DH), dp + ("y",), 0, 0, tiled=True
    ).reshape(owners, n_y, cap, piece, 2 * DH)
    attn_all, gq_all = ring(attn), ring(gq)
    sums = (jax.ShapeDtypeStruct((rows, DH), F32),) + (slab,) * (n_y - 1)
    enc_part, *sums = call(
        functools.partial(tail_body, stored, n_z),
        (jax.ShapeDtypeStruct((piece * stored, enc_width), BF),) + sums + sums,
        "sa" + "a" * (n_y + 2 * n_z + 2), 1_580_000_000, 10 << 20,
        scratch=(
            pltpu.VMEM((owners, n_y, cap, piece, 2 * DH), BF),
            pltpu.VMEM((n_y, enc_width, 2 * DH), BF),
            pltpu.VMEM((n_y, stored, piece, 2 * DH), F32),
            pltpu.VMEM((enc_width // DH, stored * piece, DH), F32),
            pltpu.VMEM((2, rows, n_z * DH), BF),
            pltpu.VMEM((2, n_z, n_y, DH, DH), BF),
            pltpu.VMEM((piece * stored, enc_width), BF),
            pltpu.VMEM((2, rows, DH), F32),
            pltpu.VMEM((2, n_y - 1, rows, DH), BF),
            pltpu.SemaphoreType.DMA((owners + n_y + 2 * n_z + 2 + 1 + 2 * n_y,)),
        ),
        out_space="a",
    )(ids_all, returned, *pairs, *attn_all, *gq_all, mine, other)
    enc_parts = lax.all_to_all(enc_part.reshape(n_z, -1, enc_width), "z", 0, 0, tiled=True)
    enc_rows_sum = jnp.sum(enc_parts.astype(F32), axis=0).astype(BF)

    def summed(parts):
        total = parts[0]
        for k in range(1, n_y):
            total = total + shift("y", n_y, k)(parts[k]).astype(F32)
        return total.astype(BF)

    attended = summed(sums[:n_y])
    own, enc_rows_sum = tie((sums[n_y], enc_rows_sum))
    grad_encoded = enc_rows_sum.reshape(seg // (n_y * n_z), stored, enc_width).transpose(1, 0, 2).reshape(stored, -1)
    return attended, summed([own, *sums[n_y + 1 :]]), grad_encoded


def solution(mesh):
    n_y = 4
    dp, mp = mesh.shape["dp"], mesh.shape["mp"]
    split = Mesh(mesh.devices.reshape(dp // 2, 2, n_y, mp // n_y), ("x", "c", "y", "z"))
    d, m = ("x", "c"), ("y", "z")
    return jax.shard_map(
        shards,
        mesh=split,
        in_specs=(P(d, None), P(d, None), P(d, None), P(None, m), P(None, m), P(None, m), P(m, None), P(d, None)),
        out_specs=(P(d, m), P(d, m), P(d, m)),
        check_vma=False,
    )
```

```python
import functools
import math

import jax
import jax.numpy as jnp
from jax import lax
from jax.experimental import pallas as pl
from jax.experimental.pallas import tpu as pltpu
from jax.sharding import Mesh, PartitionSpec as P

DH = 128
BF = jnp.bfloat16
F32 = jnp.float32
NT = (((1,), (1,)), ((), ()))
TN = (((0,), (0,)), ((), ()))
HEAD = 16
GROUP = 8
VMEM_LIMIT = 64 * 1024 * 1024 - 64 * 1024


def params():
    return pltpu.CompilerParams(vmem_limit_bytes=VMEM_LIMIT)


def call(body, out_shape, in_spaces, flops, moved, scratch=(), out_space="v"):
    spaces = {"s": pltpu.SMEM, "v": pltpu.VMEM, "a": pltpu.HBM}
    single = not isinstance(out_shape, (tuple, list))
    outs = [out_shape] if single else out_shape
    out = tuple(pl.BlockSpec(memory_space=spaces[k]) for k in out_space * (len(outs) if len(out_space) == 1 else 1))
    return pl.pallas_call(
        body,
        out_shape=out_shape,
        in_specs=[pl.BlockSpec(memory_space=spaces[k]) for k in in_spaces],
        out_specs=out[0] if single else out,
        scratch_shapes=list(scratch),
        compiler_params=params(),
        cost_estimate=pl.CostEstimate(flops=flops, bytes_accessed=moved, transcendentals=0),
    )


def keys_values_body(stored, n_z, n_y, ids_ref, x_ref, wk_ref, wv_ref, wo_ref, wq_ref, out_ref, pair_ref, w_ref, kv_ref, sem):
    def moved(block):
        return [
            pltpu.make_async_copy(block((y * n_z + z) * DH), w_ref.at[z, y], sem.at[y * n_z + z])
            for y in range(n_y)
            for z in range(n_z)
        ]

    copies = moved(lambda at: wq_ref.at[at : at + DH, :])

    core = lax.axis_index("c")

    @pl.when(core == 0)
    def _():
        for copy in moved(lambda at: wo_ref.at[:, at : at + DH]):
            copy.start()

    @pl.when(core != 0)
    def _():
        for copy in copies:
            copy.start()

    pair = jnp.concatenate([wk_ref[...], wv_ref[...]], axis=1)
    pair_ref[...] = pair
    seg = x_ref.shape[0] // stored
    both = jnp.dot(x_ref[...], pair, preferred_element_type=F32)
    for n in range(kv_ref.shape[0]):
        kv_ref[n] = both[:, n * DH : (n + 1) * DH]
        for s in range(stored):
            rows = slice(HEAD + s * seg, HEAD + (s + 1) * seg)
            out_ref[rows, n * DH : (n + 1) * DH] = kv_ref[n, pl.ds(s, seg, stride=stored), :].astype(BF)
    for copy in copies:
        copy.wait()
    lane = lax.broadcasted_iota(jnp.int32, (HEAD, 2 * DH), 1)
    row = jnp.zeros((HEAD, 2 * DH), F32)
    for r in range(2 * ids_ref.shape[1]):
        row = jnp.where(lane == r, ids_ref[r % 2, r // 2].astype(F32), row)
    out_ref[:HEAD, :] = row.astype(BF)


def halves_body(cut, after_ref, before_ref, lo_ref, hi_ref, sem):
    copies = [
        pltpu.make_async_copy(after_ref.at[:cut], lo_ref, sem.at[0]),
        pltpu.make_async_copy(before_ref.at[cut:], hi_ref, sem.at[1]),
    ]
    for copy in copies:
        copy.start()
    for copy in copies:
        copy.wait()


def attention_body(geom, ids_ref, q_ref, g_ref, *refs):
    blocks, block_len, n_x, n_y, cap, stored, seg = geom
    kv_refs, (attn_ref, gq_ref, out_ref, all_ids_ref, kv_ref, stage_ref, head_ref, sem) = refs[:-8], refs[-8:]
    inv_root = 1.0 / math.sqrt(DH)
    piece = seg // n_y
    cut = HEAD + stored // 2 * seg
    my_x, my_c = lax.axis_index("x"), lax.axis_index("c")
    requests = 2 * blocks
    parts = len(kv_refs) // 2

    spots = []
    for r in range(requests):
        i = ids_ref[r % 2, r // 2]
        owner, slot = i // stored, lax.rem(i, stored)
        dx = lax.rem(owner // 2 - my_x + n_x, n_x)
        dc = lax.rem(lax.rem(owner, 2) + my_c, 2)
        part = dx + jnp.where(dx == 3, 1, jnp.where((dx == 2) & (slot >= stored // 2), 1, 0))
        row = HEAD + slot * seg - jnp.where(part == 3, cut, 0)
        row = pl.multiple_of(row, HEAD)
        spots.append(owner)
        for k, ref in enumerate(kv_refs):

            @pl.when(dc * parts + part == k)
            def _(ref=ref, row=row, r=r):
                pltpu.make_async_copy(ref.at[pl.ds(row, seg), :], kv_ref.at[r], sem.at[r]).start()

    heads = [(c, d) for c in range(2) for d in range(n_x)]
    head_copies = []
    for i, (c, d) in enumerate(heads):
        ref = kv_refs[c * parts + (4 if d == 3 else d)]
        head_copies.append(pltpu.make_async_copy(ref.at[:HEAD, :DH], head_ref.at[i], sem.at[requests + i]))
        head_copies[-1].start()

    for r in range(requests):
        pltpu.make_async_copy(kv_refs[0].at[:seg, :], kv_ref.at[r], sem.at[r]).wait()

    def context(c):
        both = [kv_ref[r] for r in (2 * c, 2 * c + 1)]
        return [jnp.concatenate([b[:, at : at + DH] for b in both], axis=0) for at in (0, DH)]

    def rows(c):
        return slice(c * block_len, (c + 1) * block_len)

    sent = []
    for first in range(0, blocks, GROUP):
        group = range(first, first + GROUP)
        scores, grad_probs, probs, grad_scores = {}, {}, {}, {}
        for c in group:
            k, v = context(c)
            scores[c] = lax.dot_general(q_ref[rows(c), :], k, NT, preferred_element_type=F32) * inv_root
            grad_probs[c] = lax.dot_general(g_ref[rows(c), :], v, NT, preferred_element_type=F32)
        for c in group:
            e = jnp.exp(scores[c] - jnp.max(scores[c], axis=-1, keepdims=True))
            p = e / jnp.sum(e, axis=-1, keepdims=True)
            probs[c] = p.astype(BF)
            gp = grad_probs[c]
            grad_scores[c] = (p * (gp - jnp.sum(p * gp, axis=-1, keepdims=True))).astype(BF)
        for c in group:
            k, v = context(c)
            attn_ref[rows(c), :] = jnp.dot(probs[c], v, preferred_element_type=F32).astype(BF)
            gq_ref[rows(c), :] = (jnp.dot(grad_scores[c], k, preferred_element_type=F32) * inv_root).astype(BF)
        for c in group:
            gv = lax.dot_general(probs[c], g_ref[rows(c), :], TN, preferred_element_type=F32).astype(BF)
            gk = lax.dot_general(grad_scores[c], q_ref[rows(c), :], TN, preferred_element_type=F32)
            gk = (gk * inv_root).astype(BF)
            for j in range(2):
                r = 2 * c + j
                owner = spots[r]
                pos = sum([(spots[i] == owner).astype(jnp.int32) for i in range(r)], jnp.int32(0))
                for y in range(n_y):
                    part = slice(j * seg + y * piece, j * seg + (y + 1) * piece)
                    stage_ref[r, y, :, :DH] = gk[part, :]
                    stage_ref[r, y, :, DH:] = gv[part, :]
                copy = pltpu.make_async_copy(
                    stage_ref.at[r], out_ref.at[owner, :, pos], sem.at[requests + len(heads) + r]
                )
                copy.start()
                sent.append(copy)
    for i, (c, d) in enumerate(heads):
        head_copies[i].wait()
        owner = lax.rem(my_x + d, n_x) * 2 + lax.rem(my_c + c, 2)
        all_ids_ref[pl.ds(owner, 1), :] = head_ref[i].astype(F32).astype(jnp.int32)[:1, :]
    for copy in sent:
        copy.wait()


def tail_body(stored, n_z, ids_ref, ret_ref, *refs):
    owners, n_y, cap, piece, _ = ret_ref.shape
    pair_refs, refs = refs[:n_y], refs[n_y:]
    piece_refs, (mine, other), refs = refs[: 2 * n_z], refs[2 * n_z : 2 * n_z + 2], refs[2 * n_z + 2 :]
    out_hbm, sums_hbm, refs = refs[0], refs[1 : 1 + 2 * n_y], refs[1 + 2 * n_y :]
    got_ref, pair_ref, acc_ref, prod_ref, a_ref, w_ref, out_ref, own_ref, sent_ref, sem = refs
    my_x, my_c, my_y, my_z = (lax.axis_index(a) for a in ("x", "c", "y", "z"))
    me = my_x * 2 + my_c

    for d in range(owners):
        pltpu.make_async_copy(ret_ref.at[d], got_ref.at[d], sem.at[d]).start()
    first = owners
    to = (0, 1 + 2 * my_c, 2, 3 - 2 * my_c)
    pair_copies = [pltpu.make_async_copy(pair_refs[y], pair_ref.at[to[y]], sem.at[first + y]) for y in range(n_y)]
    first += n_y
    piece_copies = [
        pltpu.make_async_copy(
            piece_refs[k], a_ref.at[k // n_z, :, (k % n_z) * DH : (k % n_z + 1) * DH], sem.at[first + k]
        )
        for k in range(2 * n_z)
    ]
    first += 2 * n_z
    weight_copies = [
        pltpu.make_async_copy(mine, w_ref.at[my_c], sem.at[first]),
        pltpu.make_async_copy(other, w_ref.at[1 - my_c], sem.at[first + 1]),
    ]
    for copy in pair_copies + piece_copies + weight_copies:
        copy.start()

    acc_ref[...] = jnp.zeros_like(acc_ref)

    def from_device(d, carry):
        pltpu.make_async_copy(ret_ref.at[d], got_ref.at[d], sem.at[d]).wait()
        count = jnp.int32(0)
        for r in range(owners * 2):
            at = ids_ref[d, r]
            named = at // stored == me

            @pl.when(named)
            def _(at=at, count=count):
                slot = lax.rem(at, stored)
                for y in range(n_y):
                    acc_ref[y, slot] += got_ref[d, y, count].astype(F32)

            count = count + named.astype(jnp.int32)
        return carry

    lax.fori_loop(0, owners, from_device, 0)
    for copy in pair_copies:
        copy.wait()
    lanes = prod_ref.shape[0]
    both = [acc_ref[lax.rem(my_y + y, n_y)].astype(BF).reshape(stored * piece, 2 * DH) for y in range(n_y)]
    both = jnp.concatenate(both, axis=1)
    for n in range(0, lanes, 2):
        wide = min(2, lanes - n)
        w = jnp.concatenate([pair_ref[y, n * DH : (n + wide) * DH, :] for y in range(n_y)], axis=1)
        term = lax.dot_general(both, w, NT, preferred_element_type=F32)
        for i in range(wide):
            prod_ref[n + i] = term[:, i * DH : (i + 1) * DH]
    for t in range(0, piece, 2):
        for n in range(lanes):
            two = [prod_ref[n, pl.ds(t + k, stored, stride=piece), :] for k in range(2)]
            out_ref[pl.ds(t * stored, 2 * stored), n * DH : (n + 1) * DH] = jnp.concatenate(two, axis=0).astype(BF)

    first += 2
    leaving = [pltpu.make_async_copy(out_ref, out_hbm, sem.at[first])]
    leaving[0].start()

    for copy in piece_copies + weight_copies:
        copy.wait()
    heads = [lax.rem(my_z + j, n_z) for j in range(n_z)]
    for second in range(2):
        for k in range(0, n_y, 2):
            at = [lax.rem(my_y + k + i, n_y) for i in range(2)]
            if second:
                w = [jnp.concatenate([w_ref[1, h, at[i]] for h in heads], axis=1) for i in range(2)]
                total = lax.dot_general(a_ref[1], jnp.concatenate(w, axis=0), NT, preferred_element_type=F32)
            else:
                w = [jnp.concatenate([w_ref[0, h, at[i]] for h in heads], axis=0) for i in range(2)]
                total = jnp.dot(a_ref[0], jnp.concatenate(w, axis=1), preferred_element_type=F32)
            for i in range(2):
                ref = sent_ref.at[second, k + i - 1] if k + i else own_ref.at[second]
                ref[...] = total[:, i * DH : (i + 1) * DH].astype(ref.dtype)
        for k in range(n_y):
            ref = sent_ref.at[second, k - 1] if k else own_ref.at[second]
            n = second * n_y + k
            leaving.append(pltpu.make_async_copy(ref, sums_hbm[n], sem.at[first + 1 + n]))
            leaving[-1].start()
    for copy in leaving:
        copy.wait()


def shards(hidden, encoded, neighbours, w_query, w_key, w_value, w_out, cotangent):
    n_x, n_c, n_y, n_z = (lax.axis_size(a) for a in ("x", "c", "y", "z"))
    dp = ("x", "c")
    owners = n_x * n_c
    rows, width = hidden.shape
    blocks, per_block = neighbours.shape
    cap = blocks * per_block // 4
    stored = encoded.shape[0]
    enc_width = w_key.shape[0]
    seg = encoded.shape[1] // enc_width
    block_len = rows // blocks
    piece = seg // n_y
    ids = neighbours.T

    def shift(axis, n, k):
        return lambda a: lax.ppermute(a, axis, [(i, (i + k) % n) for i in range(n)])

    swap = shift("c", n_c, 1)
    x_up, x_down = shift("x", n_x, -1), shift("x", n_x, 1)
    z_up, z_down = shift("z", n_z, -1), shift("z", n_z, 1)
    tie = lax.optimization_barrier

    enc_rows = encoded.reshape(stored, seg, enc_width).transpose(1, 0, 2).reshape(seg * stored, enc_width)
    kv, pair, mine = call(
        functools.partial(keys_values_body, stored, n_z, n_y),
        (
            jax.ShapeDtypeStruct((HEAD + stored * seg, 2 * DH), BF),
            jax.ShapeDtypeStruct((enc_width, 2 * DH), BF),
            jax.ShapeDtypeStruct((n_z, n_y, DH, DH), BF),
        ),
        "svvvaa", 470_000_000, 5 << 20,
        scratch=(pltpu.VMEM((2, seg * stored, DH), F32), pltpu.SemaphoreType.DMA((n_z * n_y,))),
    )(ids, enc_rows, w_key, w_value, w_out, w_query)
    after, before, kv_other = x_up(kv), x_down(kv), swap(kv)
    mine = lax.all_to_all(mine, "z", 0, 0, tiled=True)

    ways = [(c * n_y + y, c * n_y + (y + 2 * c - 1) % n_y) for c in range(n_c) for y in range(n_y)]

    def along_y(a):
        return lax.ppermute(a, ("c", "y"), ways)

    queries = jnp.dot(hidden, w_query, preferred_element_type=F32).astype(BF)
    grad_attn = lax.dot_general(cotangent, w_out, NT, preferred_element_type=F32).astype(BF)
    pair_, queries = tie((pair, queries))
    pair_next = along_y(pair_)
    after, before, queries, grad_attn = tie((after, before, queries, grad_attn))

    cut = HEAD + stored // 2 * seg
    next_lo, next_hi = call(
        functools.partial(halves_body, cut),
        (jax.ShapeDtypeStruct((cut, 2 * DH), BF), jax.ShapeDtypeStruct((kv.shape[0] - cut, 2 * DH), BF)),
        "aa", 0, 0, scratch=(pltpu.SemaphoreType.DMA((2,)),),
    )(after, before)
    far_lo, far_hi = x_up(next_lo), x_down(next_hi)
    kv_all = [kv, after, far_lo, far_hi, before, kv_other] + [swap(a) for a in (after, far_lo, far_hi, before)]
    pairs = [pair, pair_next, along_y(pair_next), swap(pair_next)]

    queries, pairs = tie((queries, pairs))
    other = swap(mine)

    slab = jax.ShapeDtypeStruct((rows, DH), BF)
    attn, gq, outgoing, ids_all = call(
        functools.partial(attention_body, (blocks, block_len, n_x, n_y, cap, stored, seg)),
        (
            slab,
            slab,
            jax.ShapeDtypeStruct((owners, n_y, cap, piece, 2 * DH), BF),
            jax.ShapeDtypeStruct((owners, DH), jnp.int32),
        ),
        "svv" + "a" * len(kv_all), 0, 0,
        scratch=(
            pltpu.VMEM((blocks * per_block, seg, 2 * DH), BF),
            pltpu.VMEM((blocks * per_block, n_y, piece, 2 * DH), BF),
            pltpu.VMEM((owners, HEAD, DH), BF),
            pltpu.SemaphoreType.DMA((2 * blocks * per_block + owners,)),
        ),
        out_space="vvav",
    )(ids, queries, grad_attn, *kv_all)

    def ring(own):
        pieces = {0: own}
        for k in range(1, n_z // 2 + 1):
            pieces[k] = z_up(pieces[k - 1])
        last = own
        for k in range(1, n_z - n_z // 2):
            last = z_down(last)
            pieces[n_z - k] = last
        return [pieces[k] for k in range(n_z)]

    returned = lax.all_to_all(
        outgoing.reshape(owners * n_y, cap, piece, 2 * DH), dp + ("y",), 0, 0, tiled=True
    ).reshape(owners, n_y, cap, piece, 2 * DH)
    attn_all, gq_all = ring(attn), ring(gq)
    sums = (jax.ShapeDtypeStruct((rows, DH), F32),) + (slab,) * (n_y - 1)
    enc_part, *sums = call(
        functools.partial(tail_body, stored, n_z),
        (jax.ShapeDtypeStruct((piece * stored, enc_width), BF),) + sums + sums,
        "sa" + "a" * (n_y + 2 * n_z + 2), 1_580_000_000, 10 << 20,
        scratch=(
            pltpu.VMEM((owners, n_y, cap, piece, 2 * DH), BF),
            pltpu.VMEM((n_y, enc_width, 2 * DH), BF),
            pltpu.VMEM((n_y, stored, piece, 2 * DH), F32),
            pltpu.VMEM((enc_width // DH, stored * piece, DH), F32),
            pltpu.VMEM((2, rows, n_z * DH), BF),
            pltpu.VMEM((2, n_z, n_y, DH, DH), BF),
            pltpu.VMEM((piece * stored, enc_width), BF),
            pltpu.VMEM((2, rows, DH), F32),
            pltpu.VMEM((2, n_y - 1, rows, DH), BF),
            pltpu.SemaphoreType.DMA((owners + n_y + 2 * n_z + 2 + 1 + 2 * n_y,)),
        ),
        out_space="a",
    )(ids_all, returned, *pairs, *attn_all, *gq_all, mine, other)
    enc_parts = lax.all_to_all(enc_part.reshape(n_z, -1, enc_width), "z", 0, 0, tiled=True)
    enc_rows_sum = jnp.sum(enc_parts.astype(F32), axis=0).astype(BF)

    def summed(parts):
        total = parts[0]
        for k in range(1, n_y):
            total = total + shift("y", n_y, k)(parts[k]).astype(F32)
        return total.astype(BF)

    attended = summed(sums[:n_y])
    grad_encoded = enc_rows_sum.reshape(seg // (n_y * n_z), stored, enc_width).transpose(1, 0, 2).reshape(stored, -1)
    return attended, summed(sums[n_y:]), grad_encoded


def solution(mesh):
    n_y = 4
    dp, mp = mesh.shape["dp"], mesh.shape["mp"]
    split = Mesh(mesh.devices.reshape(dp // 2, 2, n_y, mp // n_y), ("x", "c", "y", "z"))
    d, m = ("x", "c"), ("y", "z")
    return jax.shard_map(
        shards,
        mesh=split,
        in_specs=(P(d, None), P(d, None), P(d, None), P(None, m), P(None, m), P(None, m), P(m, None), P(d, None)),
        out_specs=(P(d, m), P(d, m), P(d, m)),
        check_vma=False,
    )
```
